32 devices in a mesh: dp: 16 (over z, x, core), mp: 2 (over y).
Axes of the slice: x: 2, y: 2, z: 4, core: 2. Of those that a mesh axis runs over, the one named last changes fastest.
Arguments:
- tokens: bfloat16 [16384, 1024], P('dp'), may hold values from -6 to 6
- page_lengths: int32 [32], P('dp'), may hold values from 64 to 512, as said below
- qkv_weight: bfloat16 [3, 1024, 1024], P(None, None, 'mp'), may hold values from -0.1875 to 0.1875
- qv_bias: bfloat16 [2, 1024], P(None, 'mp'), may hold values from -1.5 to 1.5
- out_weight: bfloat16 [1024, 1024], P('mp'), may hold values from -0.75 to 0.75
- out_bias: bfloat16 [1024], replicated, may hold values from -1.5 to 1.5
- ln1_gain: bfloat16 [1024], replicated, may hold values from 0.5 to 1.5
- ln1_bias: bfloat16 [1024], replicated, may hold values from -1.5 to 1.5
- ff1_weight: bfloat16 [1024, 4096], P(None, 'mp'), may hold values from -0.1875 to 0.1875
- ff1_bias: bfloat16 [4096], P('mp'), may hold values from -1.5 to 1.5
- ff2_weight: bfloat16 [4096, 1024], P('mp'), may hold values from -0.09375 to 0.09375
- ff2_bias: bfloat16 [1024], replicated, may hold values from -1.5 to 1.5
- ln2_gain: bfloat16 [1024], replicated, may hold values from 0.5 to 1.5
- ln2_bias: bfloat16 [1024], replicated, may hold values from -1.5 to 1.5
- cotangent: bfloat16 [16384, 1024], P('dp'), may hold values from -6 to 6
Outputs:
- out_rows: bfloat16 [16384, 1024], P(('dp', 'mp'))
- input_grad: bfloat16 [16384, 1024], P(('dp', 'mp'))
- qkv_weight_grad: float32 [3, 1024, 1024], P(None, 'dp', 'mp')
- qv_bias_grad: float32 [2, 1024], replicated
- out_weight_grad: float32 [1024, 1024], P('mp', 'dp')
- out_bias_grad: float32 [1024], replicated
- ln1_gain_grad: float32 [1024], replicated
- ln1_bias_grad: float32 [1024], replicated
- ff1_weight_grad: float32 [1024, 4096], P('dp', 'mp')
- ff1_bias_grad: float32 [4096], replicated
- ff2_weight_grad: float32 [4096, 1024], P('mp', 'dp')
- ff2_bias_grad: float32 [1024], replicated
- ln2_gain_grad: float32 [1024], replicated
- ln2_bias_grad: float32 [1024], replicated
The draws below stay inside these ranges and needn't reach their ends.
Inputs may be any that keep to these rules, and one draw needn't show every extreme that they name: `page_lengths`: valid tokens of a page; some page has all 512 slots valid.
All inputs are finite; a program needn't handle non-finite values.
Results may differ from the reference program's by a relative error of at most 0.02.
Values may be sent and summed in bfloat16 or wider, within the bound.
No kernel may reach another device: no remote copies, remote signals or barrier semaphores. Data moves between devices by JAX's collectives and lax.ppermute only.
A program may use at most 192 MiB of HBM per device.

```python
import math
import jax
import jax.numpy as jnp
from jax import lax

D = 1024
HEADS = 16
HD = 64
FF = 4096
LEN = 512
PAGES = 32
TOKENS = 16384
N_MP = 2


def draw_page_lengths(key, part):
    first_key, second_key = jax.random.split(jax.random.fold_in(key, 11))
    drawn = jax.random.randint(first_key, (PAGES,), LEN // 8, LEN + 1)
    chosen = jax.random.randint(second_key, (), 0, PAGES)
    return jnp.where(jnp.arange(PAGES) == chosen, LEN, drawn).astype(jnp.int32)


def raised(values, stream_key, source, target, blocks, factor):
    def block_of(axis_at):
        return (jnp.arange(values.shape[axis_at]) // (values.shape[axis_at] // blocks)).reshape((-1,) + (1,) * (values.ndim - 1 - axis_at))

    one_side = jax.random.permutation(stream_key, blocks)[block_of(target)]
    second = (block_of(target) + blocks // 2) % blocks
    return jnp.where((block_of(source) == one_side) | (block_of(source) == second), factor * values, values)


def shard_levels(rng, extent, pieces, least, largest):
    loudness = 1.0
    for dim, blocks in pieces:
        draws = jax.random.uniform(jax.random.fold_in(jax.random.fold_in(rng, 6), dim), (blocks,), jnp.float32, least / len(pieces), largest / len(pieces))
        loudness = loudness * jnp.repeat(jnp.exp(draws), extent[dim] // blocks).reshape((-1,) + (1,) * (len(extent) - 1 - dim))
    return loudness


def scatter_about(own_key, shape, scale, reach, cuts=(), held_as=jnp.bfloat16):
    array = scale * jax.random.normal(own_key, shape, jnp.float32)
    if cuts:
        array = array * shard_levels(own_key, shape, cuts, -0.22, 0.18)
    return jnp.clip(array, -reach, reach).astype(held_as)


def gaussian_with(stream_key, extent, deviation, bound, cuts, heavy, held_as=jnp.bfloat16):
    values = deviation * jax.random.normal(stream_key, extent, jnp.float32)
    if cuts:
        values = values * shard_levels(stream_key, extent, cuts, -0.22, 0.18)
    return jnp.clip(raised(values, jax.random.fold_in(stream_key, 3), *heavy), -bound, bound).astype(held_as)


def setup_inputs(seed: int = 0) -> dict:
    key_of = jax.random.split(jax.random.key(seed), 16)
    return {
        "tokens": scatter_about(key_of[0], (TOKENS, D), 1.0, 6.0, ((0, 16),)),
        "page_lengths": draw_page_lengths(jax.random.fold_in(key_of[15], 71), 0),
        "qkv_weight": scatter_about(key_of[2], (3, D, D), D ** -0.5, 0.1875, ((2, 2),)),
        "qv_bias": scatter_about(key_of[3], (2, D), 0.3, 1.5, ((1, 2),)),
        "out_weight": scatter_about(key_of[4], (D, D), (D // 16) ** -0.5, 0.75, ((0, 2),)),
        "out_bias": scatter_about(key_of[5], (D,), 0.3, 1.5),
        "ln1_gain": jnp.clip(1.0 + 0.1 * jax.random.normal(key_of[6], (D,), jnp.float32), 0.5, 1.5).astype(jnp.bfloat16),
        "ln1_bias": scatter_about(key_of[7], (D,), 0.3, 1.5),
        "ff1_weight": scatter_about(key_of[8], (D, FF), D ** -0.5, 0.1875, ((1, 2),)),
        "ff1_bias": scatter_about(key_of[9], (FF,), 0.3, 1.5, ((0, 2),)),
        "ff2_weight": scatter_about(key_of[10], (FF, D), FF ** -0.5, 0.09375, ((0, 2),)),
        "ff2_bias": scatter_about(key_of[11], (D,), 0.3, 1.5),
        "ln2_gain": jnp.clip(1.0 + 0.1 * jax.random.normal(key_of[12], (D,), jnp.float32), 0.5, 1.5).astype(jnp.bfloat16),
        "ln2_bias": scatter_about(key_of[13], (D,), 0.3, 1.5),
        "cotangent": gaussian_with(key_of[14], (TOKENS, D), 1.0, 6.0, ((0, 16),), (0, 1, 16, 2.0)),
    }


@jax.custom_vjp
def low(v):
    return lax.optimization_barrier(v.astype(jnp.bfloat16)).astype(jnp.float32)

@jax.custom_vjp
def low_back(v):
    return v

def low_keep(v):
    return (low(v), None)

def low_pass(kept, grad):
    return (grad,)

def back_keep(v):
    return (v, None)

def back_low(kept, grad):
    return (low(grad),)
low.defvjp(low_keep, low_pass)
low_back.defvjp(back_keep, back_low)
EPSILON = 1e-05
NEGATIVE = -1e+30
HIGH = lax.Precision.HIGHEST

def layer_norm(values, gain, shift):
    center = values - lax.optimization_barrier(jnp.mean(values, axis=-1, keepdims=True))
    spread = lax.optimization_barrier(jnp.mean(center * center, axis=-1, keepdims=True))
    return center * lax.rsqrt(spread + EPSILON) * gain + shift

def forward(inputs, lengths, params):
    qkv_w, qv_b, out_w, out_b, gain_one, shift_one, ff1_w, ff1_b, ff2_w, ff2_b, gain_two, shift_two = params
    row_count = inputs.shape[0]
    page_count = lengths.shape[0]
    cols = D // N_MP
    group_heads = HEADS // N_MP
    ff_cols = FF // N_MP
    spread_in = low_back(jnp.broadcast_to(low(inputs), (N_MP, row_count, D)))
    projected = jnp.einsum('grd,tdgc->tgrc', spread_in, qkv_w.reshape(3, D, N_MP, cols), precision=HIGH)
    query = low_back(low(projected[0] + qv_b[0].reshape(N_MP, 1, cols)))
    keyset = low_back(low(projected[1]))
    valueset = low_back(low(projected[2] + qv_b[1].reshape(N_MP, 1, cols)))
    shape_five = (N_MP, page_count, LEN, group_heads, HD)
    raw = jnp.einsum('gpqhe,gpkhe->gphqk', query.reshape(shape_five), keyset.reshape(shape_five), precision=HIGH)
    scores = low_back(raw * HD ** (-0.5))
    valid = jnp.arange(LEN)[None, :] < lengths[:, None]
    scores = jnp.where(valid[None, :, None, None, :], scores, NEGATIVE)
    probs = jax.nn.softmax(scores, axis=-1)
    context = jnp.einsum('gphqk,gpkhe->gpqhe', low(probs), valueset.reshape(shape_five), precision=HIGH)
    context = low_back(low(context.reshape(N_MP, row_count, cols)))
    attn_parts = low(jnp.einsum('grc,gcd->grd', context, out_w.reshape(N_MP, cols, D), precision=HIGH))
    attn = low_back(lax.optimization_barrier(jnp.sum(attn_parts, axis=0)))
    hidden = layer_norm(inputs + attn + out_b, gain_one, shift_one)
    spread_hid = low_back(jnp.broadcast_to(low(hidden), (N_MP, row_count, D)))
    pre = jnp.einsum('grd,dgf->grf', spread_hid, ff1_w.reshape(D, N_MP, ff_cols), precision=HIGH)
    pre = low_back(pre + ff1_b.reshape(N_MP, 1, ff_cols))
    act = low(jax.nn.gelu(pre, approximate=False))
    ffn_parts = low(jnp.einsum('grf,gfd->grd', act, ff2_w.reshape(N_MP, ff_cols, D), precision=HIGH))
    ffn = low_back(lax.optimization_barrier(jnp.sum(ffn_parts, axis=0)))
    return layer_norm(hidden + ffn + ff2_b, gain_two, shift_two)

def reference(tokens, page_lengths, qkv_weight, qv_bias, out_weight, out_bias, ln1_gain, ln1_bias, ff1_weight, ff1_bias, ff2_weight, ff2_bias, ln2_gain, ln2_bias, cotangent):
    page_step = math.gcd(PAGES, max(1, 4096 // LEN))
    step_count = PAGES // page_step
    step_rows = page_step * LEN
    params = tuple((item.astype(jnp.float32) for item in (qkv_weight, qv_bias, out_weight, out_bias, ln1_gain, ln1_bias, ff1_weight, ff1_bias, ff2_weight, ff2_bias, ln2_gain, ln2_bias)))

    def one_step(totals, block):
        inputs, lengths, cot = block
        outputs, back = jax.vjp(lambda first, second: forward(first, lengths, second), inputs, params)
        grad_in, grad_params = back(cot)
        totals = jax.tree.map(jnp.add, totals, grad_params)
        return (totals, (outputs.astype(jnp.bfloat16), grad_in.astype(jnp.bfloat16)))
    initial = tuple((jnp.zeros_like(item) for item in params))
    blocks = (tokens.astype(jnp.float32).reshape(step_count, step_rows, D), page_lengths.reshape(step_count, page_step), cotangent.astype(jnp.float32).reshape(step_count, step_rows, D))
    totals, (outputs, grads) = lax.scan(one_step, initial, blocks)
    return (outputs.reshape(TOKENS, D), grads.reshape(TOKENS, D), totals[0], totals[1], totals[2], totals[3], totals[4], totals[5], totals[6], totals[7], totals[8], totals[9], totals[10], totals[11])
```

```python
import functools

import jax
import jax.numpy as jnp
from jax import lax
from jax.experimental import pallas as pl
from jax.experimental.pallas import tpu as pltpu
from jax.sharding import PartitionSpec as P

HD = 64


EPSILON = 1e-05
NEGATIVE = -1e30


def normalize(values):
    center = values - jnp.mean(values, axis=-1, keepdims=True)
    spread = jnp.mean(center * center, axis=-1, keepdims=True)
    return center * lax.rsqrt(spread + EPSILON)


def gelu_exact(values):
    return jax.nn.gelu(values, approximate=False)


def over_rows(left, right):
    return lax.dot_general(
        left, right, (((0,), (0,)), ((), ())), preferred_element_type=jnp.float32
    )


def over_cols(left, right):
    return lax.dot_general(
        left, right, (((1,), (1,)), ((), ())), preferred_element_type=jnp.float32
    )


def page_scores(query, keyset, valid):
    raw = jnp.einsum("qhe,khe->hqk", query, keyset, preferred_element_type=jnp.float32) * HD ** (
        -0.5
    )
    return jnp.where(valid[None, None, :], raw, NEGATIVE)


def attend(block):
    query, keyset, valueset, valid = block
    scores = page_scores(query, keyset, valid)
    top = jnp.max(scores, axis=-1, keepdims=True)
    expo = jnp.exp(scores - top)
    total = jnp.sum(expo, axis=-1, keepdims=True)
    probs = expo / total
    context = jnp.einsum(
        "hqk,khe->qhe", probs.astype(jnp.bfloat16), valueset, preferred_element_type=jnp.float32
    )
    context = context.astype(jnp.bfloat16)
    return (context.reshape(context.shape[0], -1), top[..., 0] + jnp.log(total[..., 0]))


def attend_back(block):
    query, keyset, valueset, valid, logsum, dcontext = block
    scale = HD ** (-0.5)
    scores = page_scores(query, keyset, valid)
    probs = jnp.exp(scores - logsum[..., None])
    dprobs = jnp.einsum("qhe,khe->hqk", dcontext, valueset, preferred_element_type=jnp.float32)
    delta = jnp.sum(probs * dprobs, axis=-1, keepdims=True)
    dscores = (probs * (dprobs - delta)).astype(jnp.bfloat16)
    dquery = (
        jnp.einsum("hqk,khe->qhe", dscores, keyset, preferred_element_type=jnp.float32) * scale
    ).astype(jnp.bfloat16)
    dkeys = (
        jnp.einsum("hqk,qhe->khe", dscores, query, preferred_element_type=jnp.float32) * scale
    ).astype(jnp.bfloat16)
    dvalues = jnp.einsum(
        "hqk,qhe->khe", probs.astype(jnp.bfloat16), dcontext, preferred_element_type=jnp.float32
    ).astype(jnp.bfloat16)
    seq_len = query.shape[0]
    return (dquery.reshape(seq_len, -1), dkeys.reshape(seq_len, -1), dvalues.reshape(seq_len, -1))


def local(
    tokens,
    page_lengths,
    qkv_weight,
    qv_bias,
    out_weight,
    out_bias,
    ln1_gain,
    ln1_bias,
    ff1_weight,
    ff1_bias,
    ff2_weight,
    ff2_bias,
    ln2_gain,
    ln2_bias,
    cotangent,
):
    row_count = tokens.shape[0]
    page_count = page_lengths.shape[0]
    seq_len = row_count // page_count
    cols = qkv_weight.shape[2]
    ff_cols = ff1_weight.shape[1]
    group_heads = cols // HD
    share = row_count // lax.axis_size("mp")
    group = lax.axis_index("mp")
    share_start = group * share
    gain_one = ln1_gain.astype(jnp.float32)
    shift_one = ln1_bias.astype(jnp.float32)
    gain_two = ln2_gain.astype(jnp.float32)
    shift_two = ln2_bias.astype(jnp.float32)

    def own_rows(values):
        return lax.dynamic_slice_in_dim(values, share_start, share, 0)

    projected = jnp.einsum("rd,tdc->trc", tokens, qkv_weight, preferred_element_type=jnp.float32)
    bias_rows = jnp.stack([qv_bias[0], jnp.zeros_like(qv_bias[0]), qv_bias[1]]).astype(jnp.float32)
    qkv_rows = (projected + bias_rows[:, None, :]).astype(jnp.bfloat16)
    qkv_pages = qkv_rows.reshape(3, page_count, seq_len, group_heads, HD)
    valid = jnp.arange(seq_len)[None, :] < page_lengths[:, None]
    context, logsum = lax.map(attend, (qkv_pages[0], qkv_pages[1], qkv_pages[2], valid))
    context = context.reshape(row_count, cols)
    attn_part = jnp.dot(context, out_weight, preferred_element_type=jnp.float32).astype(
        jnp.bfloat16
    )
    attn = lax.psum(attn_part, "mp").astype(jnp.float32)
    first_sum = tokens.astype(jnp.float32) + attn + out_bias.astype(jnp.float32)
    normed_one, norm_one_back = jax.vjp(normalize, first_sum)
    hidden = normed_one * gain_one + shift_one
    hidden_low = hidden.astype(jnp.bfloat16)
    normed_one_own = own_rows(normed_one)
    pre = jnp.dot(hidden_low, ff1_weight, preferred_element_type=jnp.float32) + ff1_bias.astype(
        jnp.float32
    )
    activated, gelu_back = jax.vjp(gelu_exact, pre)
    act_low = activated.astype(jnp.bfloat16)
    ffn_part = jnp.dot(act_low, ff2_weight, preferred_element_type=jnp.float32).astype(jnp.bfloat16)
    cot_own = own_rows(cotangent).astype(jnp.float32)
    ffn = lax.psum(ffn_part, "mp").astype(jnp.float32)
    second_sum = hidden + ffn + ff2_bias.astype(jnp.float32)
    normed_two, norm_two_back = jax.vjp(normalize, second_sum)
    normed_two_own = own_rows(normed_two)
    out_rows = (normed_two_own * gain_two + shift_two).astype(jnp.bfloat16)
    dsecond = norm_two_back(cotangent.astype(jnp.float32) * gain_two)[0]
    dffn = dsecond.astype(jnp.bfloat16)
    dsecond_own = own_rows(dsecond)
    dgain_two = jnp.sum(cot_own * normed_two_own, axis=0)
    dshift_two = jnp.sum(cot_own, axis=0)
    dff2_bias = jnp.sum(dsecond_own, axis=0)
    dff2_weight = over_rows(act_low, dffn)
    dact = over_cols(dffn, ff2_weight)
    dpre = gelu_back(dact)[0].astype(jnp.bfloat16)
    dff1_bias = jnp.sum(dpre.astype(jnp.float32), axis=0)
    dff1_weight = over_rows(hidden_low, dpre)
    dhid_part = over_cols(dpre, ff1_weight).astype(jnp.bfloat16)
    dhidden = dsecond + lax.psum(dhid_part, "mp").astype(jnp.float32)
    dfirst = norm_one_back(dhidden * gain_one)[0]
    dattn = dfirst.astype(jnp.bfloat16)
    dhidden_own = own_rows(dhidden)
    dfirst_own = own_rows(dfirst)
    dgain_one = jnp.sum(dhidden_own * normed_one_own, axis=0)
    dshift_one = jnp.sum(dhidden_own, axis=0)
    dout_bias = jnp.sum(dfirst_own, axis=0)
    dout_weight = over_rows(context, dattn)
    dcontext = over_cols(dattn, out_weight).astype(jnp.bfloat16)
    dcontext_pages = dcontext.reshape(page_count, seq_len, group_heads, HD)
    dquery, dkeys, dvalues = lax.map(
        attend_back, (qkv_pages[0], qkv_pages[1], qkv_pages[2], valid, logsum, dcontext_pages)
    )
    dqkv = jnp.stack(
        [
            dquery.reshape(row_count, cols),
            dkeys.reshape(row_count, cols),
            dvalues.reshape(row_count, cols),
        ]
    )
    dqv_bias = jnp.stack(
        [jnp.sum(dqkv[0].astype(jnp.float32), axis=0), jnp.sum(dqkv[2].astype(jnp.float32), axis=0)]
    )
    dqkv_weight = jnp.einsum("rd,trc->tdc", tokens, dqkv, preferred_element_type=jnp.float32)
    dtok_part = jnp.einsum(
        "trc,tdc->rd", dqkv, qkv_weight, preferred_element_type=jnp.float32
    ).astype(jnp.bfloat16)
    input_grad = (
        dfirst_own
        + lax.psum_scatter(dtok_part, "mp", scatter_dimension=0, tiled=True).astype(jnp.float32)
    ).astype(jnp.bfloat16)
    qkv_share, out_share, ff1_share, ff2_share = (
        lax.psum_scatter(
            dqkv_weight.astype(jnp.bfloat16), "dp", scatter_dimension=1, tiled=True
        ).astype(jnp.float32),
        lax.psum_scatter(
            dout_weight.astype(jnp.bfloat16), "dp", scatter_dimension=1, tiled=True
        ).astype(jnp.float32),
        lax.psum_scatter(
            dff1_weight.astype(jnp.bfloat16), "dp", scatter_dimension=0, tiled=True
        ).astype(jnp.float32),
        lax.psum_scatter(
            dff2_weight.astype(jnp.bfloat16), "dp", scatter_dimension=1, tiled=True
        ).astype(jnp.float32),
    )
    qv_placed = lax.dynamic_update_slice_in_dim(
        jnp.zeros((2, cols * lax.axis_size("mp")), jnp.float32), dqv_bias, group * cols, 1
    )
    ff1_placed = lax.dynamic_update_slice_in_dim(
        jnp.zeros((ff_cols * lax.axis_size("mp"),), jnp.float32), dff1_bias, group * ff_cols, 0
    )
    small = lax.psum(
        (qv_placed, dout_bias, dgain_one, dshift_one, ff1_placed, dff2_bias, dgain_two, dshift_two),
        ("dp", "mp"),
    )
    return (
        out_rows,
        input_grad,
        qkv_share,
        small[0],
        out_share,
        small[1],
        small[2],
        small[3],
        ff1_share,
        small[4],
        ff2_share,
        small[5],
        small[6],
        small[7],
    )


BF = jnp.bfloat16
F32 = jnp.float32


def dg(left, right, left_dim, right_dim):
    return lax.dot_general(
        left, right, (((left_dim,), (right_dim,)), ((), ())), preferred_element_type=F32
    )


def attn_fwd_body(len_ref, q_ref, k_ref, v_ref, ctx_ref, lse_ref, *, seq):
    count = len_ref[pl.program_id(0)]
    query = q_ref[...] * BF(HD**-0.5)
    keyset = k_ref[...]
    turned = v_ref[...].T
    first = lax.broadcasted_iota(jnp.int32, query.shape, 1) < HD
    keep = lax.broadcasted_iota(jnp.int32, (seq, seq), 0) < count
    outs = []
    for h in range(2):
        own = jnp.where(first if h == 0 else ~first, query, BF(0))
        scores = jnp.where(keep, dg(keyset, own, 1, 1), NEGATIVE)
        top = jnp.max(scores, axis=0, keepdims=True)
        expo = jnp.exp(scores - top)
        total = jnp.sum(expo, axis=0, keepdims=True)
        part = dg(turned[h * HD : (h + 1) * HD], expo.astype(BF), 1, 0)
        outs.append(part * (1.0 / total))
        lse_ref[0, 0, h : h + 1, :] = top + jnp.log(total)
    ctx_ref[...] = jnp.concatenate(outs, axis=0).T.astype(BF)


def attn_fwd(lengths, query, keyset, valueset):
    rows, cols = query.shape
    pages = lengths.shape[0]
    seq = rows // pages
    pairs = cols // (2 * HD)
    spec = pl.BlockSpec((seq, 2 * HD), lambda p, j, n: (p, j))
    return pl.pallas_call(
        functools.partial(attn_fwd_body, seq=seq),
        out_shape=(
            jax.ShapeDtypeStruct((rows, cols), BF),
            jax.ShapeDtypeStruct((pages, pairs, 2, seq), F32),
        ),
        grid_spec=pltpu.PrefetchScalarGridSpec(
            num_scalar_prefetch=1,
            grid=(pages, pairs),
            in_specs=[spec] * 3,
            out_specs=[spec, pl.BlockSpec((1, 1, 2, seq), lambda p, j, n: (p, j, 0, 0))],
        ),
        cost_estimate=pl.CostEstimate(
            flops=16 * rows * seq * cols,
            bytes_accessed=rows * cols * 8,
            transcendentals=rows * seq * cols // HD,
        ),
        name="attn_fwd",
    )(lengths, query, keyset, valueset)


def attn_bwd_body(
    len_ref, q_ref, k_ref, v_ref, lse_ref, dc_ref, dq_ref, dk_ref, dv_ref, *, seq
):
    count = len_ref[pl.program_id(0)]
    query = q_ref[...] * BF(HD**-0.5)
    keyset = k_ref[...]
    valueset = v_ref[...]
    dctx = dc_ref[...]
    first = lax.broadcasted_iota(jnp.int32, query.shape, 1) < HD
    keep = lax.broadcasted_iota(jnp.int32, (seq, seq), 0) < count
    dquery = dkeys = dvalues = 0.0
    for h in range(2):
        mask = first if h == 0 else ~first
        q_own = jnp.where(mask, query, BF(0))
        k_own = jnp.where(mask, keyset, BF(0))
        dc_own = jnp.where(mask, dctx, BF(0))
        scores = dg(keyset, q_own, 1, 1) - lse_ref[0, 0, h : h + 1, :]
        probs = jnp.exp(jnp.where(keep, scores, NEGATIVE))
        dprobs = dg(valueset, dc_own, 1, 1)
        delta = jnp.sum(probs * dprobs, axis=0, keepdims=True)
        dscores = (probs * (dprobs - delta)).astype(BF)
        dvalues = dvalues + dg(probs.astype(BF), dc_own, 1, 0)
        dkeys = dkeys + dg(dscores, q_own, 1, 0)
        dquery = dquery + dg(dscores, k_own, 0, 0)
    dq_ref[...] = (dquery * HD**-0.5).astype(BF)
    dk_ref[...] = dkeys.astype(BF)
    dv_ref[...] = dvalues.astype(BF)


def attn_bwd(lengths, query, keyset, valueset, logsum, dctx):
    rows, cols = query.shape
    pages = lengths.shape[0]
    seq = rows // pages
    pairs = cols // (2 * HD)
    spec = pl.BlockSpec((seq, 2 * HD), lambda p, j, n: (p, j))
    return pl.pallas_call(
        functools.partial(attn_bwd_body, seq=seq),
        out_shape=(jax.ShapeDtypeStruct((rows, cols), BF),) * 3,
        grid_spec=pltpu.PrefetchScalarGridSpec(
            num_scalar_prefetch=1,
            grid=(pages, pairs),
            in_specs=[spec] * 3
            + [pl.BlockSpec((1, 1, 2, seq), lambda p, j, n: (p, j, 0, 0)), spec],
            out_specs=[spec] * 3,
        ),
        cost_estimate=pl.CostEstimate(
            flops=40 * rows * seq * cols,
            bytes_accessed=rows * cols * 14,
            transcendentals=rows * seq * cols // HD,
        ),
        name="attn_bwd",
    )(lengths, query, keyset, valueset, logsum, dctx)


def ff1_body(h_ref, w_ref, b_ref, act_ref, slope_ref):
    pre = dg(h_ref[...], w_ref[...], 1, 0) + b_ref[...].astype(F32)
    phi = 0.5 + 0.5 * lax.erf(pre * F32(2**-0.5))
    act_ref[...] = (pre * phi).astype(BF)
    density = jnp.exp(-0.5 * pre * pre) * F32(0.3989422804014327)
    slope_ref[...] = (phi + pre * density).astype(BF)


def ff1_gelu(hidden, weight, bias):
    rows, depth = hidden.shape
    units = weight.shape[1]
    tile = min(512, units)
    return pl.pallas_call(
        ff1_body,
        out_shape=(jax.ShapeDtypeStruct((rows, units), BF),) * 2,
        grid=(units // tile,),
        in_specs=[
            pl.BlockSpec((rows, depth), lambda j: (0, 0)),
            pl.BlockSpec((depth, tile), lambda j: (0, j)),
            pl.BlockSpec((1, tile), lambda j: (0, j)),
        ],
        out_specs=[pl.BlockSpec((rows, tile), lambda j: (0, j))] * 2,
        cost_estimate=pl.CostEstimate(
            flops=2 * rows * depth * units,
            bytes_accessed=2 * (rows * depth + depth * units + 2 * rows * units),
            transcendentals=2 * rows * units,
        ),
        name="ff1_gelu",
    )(hidden, weight, bias.reshape(1, units))


def swap(values, bit):
    count = lax.axis_size("dp")
    return lax.ppermute(values, "dp", [(i, i ^ (1 << bit)) for i in range(count)])


def swap_y(values):
    return lax.ppermute(values, "mp", [(0, 1), (1, 0)])


def place_body(me_ref, *refs, offsets):
    pieces = refs[: len(offsets)]
    out = refs[len(offsets)]
    for piece, (rel, start, size) in zip(pieces, offsets):
        at = pl.multiple_of(((me_ref[0] ^ rel) & 7) * size + start, 16)
        out[pl.ds(at, piece.shape[0]), :] = piece[...]


def gather_other(weight, me):
    rows, cols = weight.shape
    size = rows // 8
    half = size // 2
    mine = swap_y(lax.dynamic_slice_in_dim(weight, (me & 7) * size, size, 0))
    by_x = swap(mine, 1)
    by_z = swap(mine, 2)
    low = swap(by_z[:half], 1)
    high = swap(by_x[half:], 2)
    near = [(0, 0, mine), (2, 0, by_x), (4, 0, by_z), (6, 0, low), (6, half, high)]
    pieces = near + [(rel ^ 1, start, swap(piece, 0)) for rel, start, piece in near]
    offsets = tuple((rel, start, size) for rel, start, _ in pieces)
    tile = min(256, cols)
    return pl.pallas_call(
        functools.partial(place_body, offsets=offsets),
        out_shape=jax.ShapeDtypeStruct((rows, cols), weight.dtype),
        grid_spec=pltpu.PrefetchScalarGridSpec(
            num_scalar_prefetch=1,
            grid=(cols // tile,),
            in_specs=[
                pl.BlockSpec((piece.shape[0], tile), lambda j, me: (0, j))
                for _, _, piece in pieces
            ],
            out_specs=pl.BlockSpec((rows, tile), lambda j, me: (0, j)),
        ),
        cost_estimate=pl.CostEstimate(
            flops=0, bytes_accessed=4 * rows * cols, transcendentals=0
        ),
        name="place_weight",
    )(me.reshape(1), *[piece for _, _, piece in pieces])


def gather_sc(weight, me):
    size = weight.shape[0] // 8
    mine = swap_y(lax.dynamic_slice_in_dim(weight, (me & 7) * size, size, 0))
    count = lax.axis_size("dp")
    groups = [[base + i for i in range(8)] for base in range(0, count, 8)]
    return lax.all_gather(mine, "dp", axis_index_groups=groups, tiled=True)


def relative_order(depth, me):
    count = lax.axis_size("dp")
    bits = count.bit_length() - 1
    half = depth // count // 2
    place = jnp.arange(depth, dtype=jnp.int32)
    inner = place % half
    order = place // half
    which = (order >> (bits - 1)) & 1
    rel = (order >> bits) & 1
    for bit in range(1, bits):
        rel = rel | (((order >> (bits - 1 - bit)) & 1) << bit)
    source = (rel ^ me) * (2 * half) + which * half + inner
    columns = lax.broadcasted_iota(jnp.int32, (depth, depth), 1)
    return (columns == source[:, None]).astype(BF)


def add(left, right):
    return left.astype(F32) + right.astype(F32)


def low_add(left, right):
    return add(left, right).astype(BF)


def finish(values, first_bit):
    count = lax.axis_size("dp")
    last = count.bit_length() - 2
    for bit in range(first_bit, last + 1):
        half = values.shape[0] // 2
        got = swap(values[half:], bit)
        values = (add if bit == last else low_add)(values[:half], got)
    return values


def reduce_grad(turned, own, other):
    half = turned.shape[0] // 2
    quarter = half // 2
    kept = []
    for side in (own, other):
        got = swap(dg(turned[half:], side, 1, 0).astype(BF), 0)
        kept.append((dg(turned[:half], side, 1, 0) + got.astype(F32)).astype(BF))
    k_own, k_other = kept
    eighth = quarter // 2
    a_own = low_add(k_own[:eighth], swap(k_own[eighth:quarter], 1))
    a_other = low_add(k_other[:eighth], swap(k_other[eighth:quarter], 1))
    a_sum = low_add(a_own, swap_y(a_other))
    b_sum = low_add(k_own[quarter:], swap_y(k_other[quarter:]))
    return jnp.concatenate([finish(a_sum, 2), finish(b_sum, 1)], axis=0)


def sum_everywhere(values):
    count = lax.axis_size("dp")
    for bit in range(count.bit_length() - 1):
        values = values + swap(values, bit)
    return values + swap_y(values)


def stats(values):
    center = values - jnp.mean(values, axis=-1, keepdims=True)
    spread = jnp.mean(center * center, axis=-1, keepdims=True)
    scale = lax.rsqrt(spread + EPSILON)
    return center * scale, scale


def norm_back(grad, normed, scale):
    return scale * (
        grad
        - jnp.mean(grad, axis=-1, keepdims=True)
        - normed * jnp.mean(grad * normed, axis=-1, keepdims=True)
    )


def paged(
    tokens,
    page_lengths,
    qkv_weight,
    qv_bias,
    out_weight,
    out_bias,
    ln1_gain,
    ln1_bias,
    ff1_weight,
    ff1_bias,
    ff2_weight,
    ff2_bias,
    ln2_gain,
    ln2_bias,
    cotangent,
):
    row_count, depth = tokens.shape
    share = row_count // 2
    cols = qkv_weight.shape[2]
    group = lax.axis_index("mp")
    me = lax.axis_index("dp")
    own_pages = page_lengths.shape[0] // 2

    def own_rows(values, size):
        return lax.dynamic_slice_in_dim(values, group * size, size, 0)

    def in_order(own, other):
        return jnp.where(
            group == 0,
            jnp.concatenate([own, other], axis=-1),
            jnp.concatenate([other, own], axis=-1),
        )

    rows = own_rows(tokens, share)
    cot = own_rows(cotangent, share).astype(F32)
    lengths = own_rows(page_lengths, own_pages)

    qkv_sides = (
        qkv_weight,
        gather_other(qkv_weight.reshape(3 * depth, cols), me).reshape(3, depth, cols),
    )
    qv_sides = (qv_bias, swap_y(qv_bias))
    out_sides = (out_weight, gather_other(out_weight, me))
    ff1_sides = (ff1_weight, gather_other(ff1_weight, me))
    ff1b_sides = (ff1_bias, swap_y(ff1_bias))
    ff2_sides = (ff2_weight, gather_other(ff2_weight, me))
    order = relative_order(depth, me)

    def turned(values):
        return dg(order, values, 1, 1).astype(BF)

    gain_one = ln1_gain.astype(F32)
    gain_two = ln2_gain.astype(F32)

    saved = []
    attn = 0.0
    for weight, bias, out_w in zip(qkv_sides, qv_sides, out_sides):
        query = (dg(rows, weight[0], 1, 0) + bias[0].astype(F32)).astype(BF)
        keyset = dg(rows, weight[1], 1, 0).astype(BF)
        valueset = (dg(rows, weight[2], 1, 0) + bias[1].astype(F32)).astype(BF)
        context, logsum = attn_fwd(lengths, query, keyset, valueset)
        saved.append((query, keyset, valueset, logsum, context))
        attn = attn + dg(context, out_w, 1, 0)
    normed_one, scale_one = stats(rows.astype(F32) + attn + out_bias.astype(F32))
    hidden = normed_one * gain_one + ln1_bias.astype(F32)
    hidden_low = hidden.astype(BF)

    acts = []
    ffn = 0.0
    for w_one, b_one, w_two in zip(ff1_sides, ff1b_sides, ff2_sides):
        act, slope = ff1_gelu(hidden_low, w_one, b_one)
        acts.append((act, slope))
        ffn = ffn + dg(act, w_two, 1, 0)
    normed_two, scale_two = stats(hidden + ffn + ff2_bias.astype(F32))
    out_rows = (normed_two * gain_two + ln2_bias.astype(F32)).astype(BF)

    dsecond = norm_back(cot * gain_two, normed_two, scale_two)
    dffn = dsecond.astype(BF)
    dgain_two = jnp.sum(cot * normed_two, axis=0)
    dshift_two = jnp.sum(cot, axis=0)
    dff2_bias = jnp.sum(dsecond, axis=0)
    ff2_share = reduce_grad(turned(dffn), acts[0][0], acts[1][0])

    dpres = []
    dhid = 0.0
    for (act, slope), w_one, w_two in zip(acts, ff1_sides, ff2_sides):
        dpre = (dg(dffn, w_two, 1, 1) * slope.astype(F32)).astype(BF)
        dpres.append(dpre)
        dhid = dhid + dg(dpre, w_one, 1, 1)
    ff1_share = reduce_grad(turned(hidden_low), dpres[0], dpres[1])
    dff1_bias = in_order(*[jnp.sum(dpre.astype(F32), axis=0) for dpre in dpres])

    dhidden = dsecond + dhid
    dfirst = norm_back(dhidden * gain_one, normed_one, scale_one)
    dattn = dfirst.astype(BF)
    dgain_one = jnp.sum(dhidden * normed_one, axis=0)
    dshift_one = jnp.sum(dhidden, axis=0)
    dout_bias = jnp.sum(dfirst, axis=0)
    out_share = reduce_grad(turned(dattn), saved[0][4], saved[1][4])

    small = jnp.concatenate(
        [dout_bias, dgain_one, dshift_one, dff1_bias, dff2_bias, dgain_two, dshift_two]
    )
    small = sum_everywhere(small.reshape(-1, 128)).reshape(-1)

    grads = []
    dtok = 0.0
    for weight, out_w, (query, keyset, valueset, logsum, _) in zip(qkv_sides, out_sides, saved):
        dctx = dg(dattn, out_w, 1, 1).astype(BF)
        parts = attn_bwd(lengths, query, keyset, valueset, logsum, dctx)
        grads.append(parts)
        for t in range(3):
            dtok = dtok + dg(parts[t], weight[t], 1, 1)
    input_grad = (dfirst + dtok).astype(BF)
    qkv_share = reduce_grad(
        turned(rows), jnp.concatenate(grads[0], axis=1), jnp.concatenate(grads[1], axis=1)
    )
    qkv_share = jnp.stack([qkv_share[:, t * cols : (t + 1) * cols] for t in range(3)])
    dqv = jnp.stack(
        [
            in_order(*[jnp.sum(parts[t].astype(F32), axis=0) for parts in grads])
            for t in (0, 2)
        ]
    )
    dqv = sum_everywhere(dqv.reshape(-1, 128)).reshape(2, -1)
    ends = []
    at = 0
    for size in (depth, depth, depth, dff1_bias.shape[0], depth, depth, depth):
        ends.append(small[at : at + size])
        at += size
    return (
        out_rows,
        input_grad,
        qkv_share,
        dqv,
        out_share.T,
        ends[0],
        ends[1],
        ends[2],
        ff1_share,
        ends[3],
        ff2_share.T,
        ends[4],
        ends[5],
        ends[6],
    )


def suits(mesh):
    return mesh.shape["mp"] == 2 and mesh.shape["dp"] == 16


def solution(mesh):
    in_specs = (
        P("dp", None),
        P("dp"),
        P(None, None, "mp"),
        P(None, "mp"),
        P("mp", None),
        P(),
        P(),
        P(),
        P(None, "mp"),
        P("mp"),
        P("mp", None),
        P(),
        P(),
        P(),
        P("dp", None),
    )
    out_specs = (
        P(("dp", "mp"), None),
        P(("dp", "mp"), None),
        P(None, "dp", "mp"),
        P(),
        P("mp", "dp"),
        P(),
        P(),
        P(),
        P("dp", "mp"),
        P(),
        P("mp", "dp"),
        P(),
        P(),
        P(),
    )
    body = paged if suits(mesh) else local
    return jax.shard_map(body, mesh=mesh, in_specs=in_specs, out_specs=out_specs, check_vma=False)
```

```python
import functools

import jax
import jax.numpy as jnp
from jax import lax
from jax.experimental import pallas as pl
from jax.experimental.pallas import tpu as pltpu
from jax.sharding import PartitionSpec as P

HD = 64


EPSILON = 1e-05
NEGATIVE = -1e30


def normalize(values):
    center = values - jnp.mean(values, axis=-1, keepdims=True)
    spread = jnp.mean(center * center, axis=-1, keepdims=True)
    return center * lax.rsqrt(spread + EPSILON)


def gelu_exact(values):
    return jax.nn.gelu(values, approximate=False)


def over_rows(left, right):
    return lax.dot_general(
        left, right, (((0,), (0,)), ((), ())), preferred_element_type=jnp.float32
    )


def over_cols(left, right):
    return lax.dot_general(
        left, right, (((1,), (1,)), ((), ())), preferred_element_type=jnp.float32
    )


def page_scores(query, keyset, valid):
    raw = jnp.einsum("qhe,khe->hqk", query, keyset, preferred_element_type=jnp.float32) * HD ** (
        -0.5
    )
    return jnp.where(valid[None, None, :], raw, NEGATIVE)


def attend(block):
    query, keyset, valueset, valid = block
    scores = page_scores(query, keyset, valid)
    top = jnp.max(scores, axis=-1, keepdims=True)
    expo = jnp.exp(scores - top)
    total = jnp.sum(expo, axis=-1, keepdims=True)
    probs = expo / total
    context = jnp.einsum(
        "hqk,khe->qhe", probs.astype(jnp.bfloat16), valueset, preferred_element_type=jnp.float32
    )
    context = context.astype(jnp.bfloat16)
    return (context.reshape(context.shape[0], -1), top[..., 0] + jnp.log(total[..., 0]))


def attend_back(block):
    query, keyset, valueset, valid, logsum, dcontext = block
    scale = HD ** (-0.5)
    scores = page_scores(query, keyset, valid)
    probs = jnp.exp(scores - logsum[..., None])
    dprobs = jnp.einsum("qhe,khe->hqk", dcontext, valueset, preferred_element_type=jnp.float32)
    delta = jnp.sum(probs * dprobs, axis=-1, keepdims=True)
    dscores = (probs * (dprobs - delta)).astype(jnp.bfloat16)
    dquery = (
        jnp.einsum("hqk,khe->qhe", dscores, keyset, preferred_element_type=jnp.float32) * scale
    ).astype(jnp.bfloat16)
    dkeys = (
        jnp.einsum("hqk,qhe->khe", dscores, query, preferred_element_type=jnp.float32) * scale
    ).astype(jnp.bfloat16)
    dvalues = jnp.einsum(
        "hqk,qhe->khe", probs.astype(jnp.bfloat16), dcontext, preferred_element_type=jnp.float32
    ).astype(jnp.bfloat16)
    seq_len = query.shape[0]
    return (dquery.reshape(seq_len, -1), dkeys.reshape(seq_len, -1), dvalues.reshape(seq_len, -1))


def local(
    tokens,
    page_lengths,
    qkv_weight,
    qv_bias,
    out_weight,
    out_bias,
    ln1_gain,
    ln1_bias,
    ff1_weight,
    ff1_bias,
    ff2_weight,
    ff2_bias,
    ln2_gain,
    ln2_bias,
    cotangent,
):
    row_count = tokens.shape[0]
    page_count = page_lengths.shape[0]
    seq_len = row_count // page_count
    cols = qkv_weight.shape[2]
    ff_cols = ff1_weight.shape[1]
    group_heads = cols // HD
    share = row_count // lax.axis_size("mp")
    group = lax.axis_index("mp")
    share_start = group * share
    gain_one = ln1_gain.astype(jnp.float32)
    shift_one = ln1_bias.astype(jnp.float32)
    gain_two = ln2_gain.astype(jnp.float32)
    shift_two = ln2_bias.astype(jnp.float32)

    def own_rows(values):
        return lax.dynamic_slice_in_dim(values, share_start, share, 0)

    projected = jnp.einsum("rd,tdc->trc", tokens, qkv_weight, preferred_element_type=jnp.float32)
    bias_rows = jnp.stack([qv_bias[0], jnp.zeros_like(qv_bias[0]), qv_bias[1]]).astype(jnp.float32)
    qkv_rows = (projected + bias_rows[:, None, :]).astype(jnp.bfloat16)
    qkv_pages = qkv_rows.reshape(3, page_count, seq_len, group_heads, HD)
    valid = jnp.arange(seq_len)[None, :] < page_lengths[:, None]
    context, logsum = lax.map(attend, (qkv_pages[0], qkv_pages[1], qkv_pages[2], valid))
    context = context.reshape(row_count, cols)
    attn_part = jnp.dot(context, out_weight, preferred_element_type=jnp.float32).astype(
        jnp.bfloat16
    )
    attn = lax.psum(attn_part, "mp").astype(jnp.float32)
    first_sum = tokens.astype(jnp.float32) + attn + out_bias.astype(jnp.float32)
    normed_one, norm_one_back = jax.vjp(normalize, first_sum)
    hidden = normed_one * gain_one + shift_one
    hidden_low = hidden.astype(jnp.bfloat16)
    normed_one_own = own_rows(normed_one)
    pre = jnp.dot(hidden_low, ff1_weight, preferred_element_type=jnp.float32) + ff1_bias.astype(
        jnp.float32
    )
    activated, gelu_back = jax.vjp(gelu_exact, pre)
    act_low = activated.astype(jnp.bfloat16)
    ffn_part = jnp.dot(act_low, ff2_weight, preferred_element_type=jnp.float32).astype(jnp.bfloat16)
    cot_own = own_rows(cotangent).astype(jnp.float32)
    ffn = lax.psum(ffn_part, "mp").astype(jnp.float32)
    second_sum = hidden + ffn + ff2_bias.astype(jnp.float32)
    normed_two, norm_two_back = jax.vjp(normalize, second_sum)
    normed_two_own = own_rows(normed_two)
    out_rows = (normed_two_own * gain_two + shift_two).astype(jnp.bfloat16)
    dsecond = norm_two_back(cotangent.astype(jnp.float32) * gain_two)[0]
    dffn = dsecond.astype(jnp.bfloat16)
    dsecond_own = own_rows(dsecond)
    dgain_two = jnp.sum(cot_own * normed_two_own, axis=0)
    dshift_two = jnp.sum(cot_own, axis=0)
    dff2_bias = jnp.sum(dsecond_own, axis=0)
    dff2_weight = over_rows(act_low, dffn)
    dact = over_cols(dffn, ff2_weight)
    dpre = gelu_back(dact)[0].astype(jnp.bfloat16)
    dff1_bias = jnp.sum(dpre.astype(jnp.float32), axis=0)
    dff1_weight = over_rows(hidden_low, dpre)
    dhid_part = over_cols(dpre, ff1_weight).astype(jnp.bfloat16)
    dhidden = dsecond + lax.psum(dhid_part, "mp").astype(jnp.float32)
    dfirst = norm_one_back(dhidden * gain_one)[0]
    dattn = dfirst.astype(jnp.bfloat16)
    dhidden_own = own_rows(dhidden)
    dfirst_own = own_rows(dfirst)
    dgain_one = jnp.sum(dhidden_own * normed_one_own, axis=0)
    dshift_one = jnp.sum(dhidden_own, axis=0)
    dout_bias = jnp.sum(dfirst_own, axis=0)
    dout_weight = over_rows(context, dattn)
    dcontext = over_cols(dattn, out_weight).astype(jnp.bfloat16)
    dcontext_pages = dcontext.reshape(page_count, seq_len, group_heads, HD)
    dquery, dkeys, dvalues = lax.map(
        attend_back, (qkv_pages[0], qkv_pages[1], qkv_pages[2], valid, logsum, dcontext_pages)
    )
    dqkv = jnp.stack(
        [
            dquery.reshape(row_count, cols),
            dkeys.reshape(row_count, cols),
            dvalues.reshape(row_count, cols),
        ]
    )
    dqv_bias = jnp.stack(
        [jnp.sum(dqkv[0].astype(jnp.float32), axis=0), jnp.sum(dqkv[2].astype(jnp.float32), axis=0)]
    )
    dqkv_weight = jnp.einsum("rd,trc->tdc", tokens, dqkv, preferred_element_type=jnp.float32)
    dtok_part = jnp.einsum(
        "trc,tdc->rd", dqkv, qkv_weight, preferred_element_type=jnp.float32
    ).astype(jnp.bfloat16)
    input_grad = (
        dfirst_own
        + lax.psum_scatter(dtok_part, "mp", scatter_dimension=0, tiled=True).astype(jnp.float32)
    ).astype(jnp.bfloat16)
    qkv_share, out_share, ff1_share, ff2_share = (
        lax.psum_scatter(
            dqkv_weight.astype(jnp.bfloat16), "dp", scatter_dimension=1, tiled=True
        ).astype(jnp.float32),
        lax.psum_scatter(
            dout_weight.astype(jnp.bfloat16), "dp", scatter_dimension=1, tiled=True
        ).astype(jnp.float32),
        lax.psum_scatter(
            dff1_weight.astype(jnp.bfloat16), "dp", scatter_dimension=0, tiled=True
        ).astype(jnp.float32),
        lax.psum_scatter(
            dff2_weight.astype(jnp.bfloat16), "dp", scatter_dimension=1, tiled=True
        ).astype(jnp.float32),
    )
    qv_placed = lax.dynamic_update_slice_in_dim(
        jnp.zeros((2, cols * lax.axis_size("mp")), jnp.float32), dqv_bias, group * cols, 1
    )
    ff1_placed = lax.dynamic_update_slice_in_dim(
        jnp.zeros((ff_cols * lax.axis_size("mp"),), jnp.float32), dff1_bias, group * ff_cols, 0
    )
    small = lax.psum(
        (qv_placed, dout_bias, dgain_one, dshift_one, ff1_placed, dff2_bias, dgain_two, dshift_two),
        ("dp", "mp"),
    )
    return (
        out_rows,
        input_grad,
        qkv_share,
        small[0],
        out_share,
        small[1],
        small[2],
        small[3],
        ff1_share,
        small[4],
        ff2_share,
        small[5],
        small[6],
        small[7],
    )


BF = jnp.bfloat16
F32 = jnp.float32
ROOT_HALF = 2**-0.5
ROOT_TAU = 0.3989422804014327


def dg(left, right, left_dim, right_dim):
    return lax.dot_general(
        left, right, (((left_dim,), (right_dim,)), ((), ())), preferred_element_type=F32
    )


def whole(*shape):
    return pl.BlockSpec(shape, lambda *at: (0,) * len(shape), pipeline_mode=pl.Buffered(1))


def shaped(shape, dtype):
    return jax.ShapeDtypeStruct(shape, dtype)


def far_shaped(shape, dtype):
    return pltpu.HBM(shape, dtype)


TIMES = {
    "attn_fwd": 5,
    "pick": 2,
    "collect": 1,
    "attn_join": 5,
    "ffn_own": 5,
    "ffn_far": 5,
    "norm_two": 5,
    "grad_send": 3,
    "keep_ffn": 6,
    "ffn_back": 24,
    "second": 1000,
    "third": 1,
    "attn_back_other": 20,
    "fourth": 1,
    "keep_far": 5,
    "attn_back_own": 16,
    "second_attn": 1000,
    "keep_own": 2,
    "join_attn": 2,
}


def call(body, name, grid, ins, outs, args, scalars=(), scratch=(), aliases=None, flops=0, room=20, stay=()):
    args = [
        pltpu.with_memory_space_constraint(a, pltpu.HBM) if i in stay else a
        for i, a in enumerate(args)
    ]
    return pl.pallas_call(
        body,
        out_shape=[s for s, _ in outs],
        grid_spec=pltpu.PrefetchScalarGridSpec(
            num_scalar_prefetch=len(scalars),
            grid=grid,
            in_specs=ins,
            out_specs=[s for _, s in outs],
            scratch_shapes=list(scratch),
        ),
        input_output_aliases=aliases or {},
        cost_estimate=pl.CostEstimate(
            flops=TIMES[name] * 10**9, bytes_accessed=0, transcendentals=0
        ),
        name=name,
        compiler_params=pltpu.CompilerParams(vmem_limit_bytes=room * 2**20),
    )(*scalars, *args)


def permute_columns(source, target, me, rows):
    low = me & 1
    high = me >> 1
    lane = lax.broadcasted_iota(jnp.int32, (rows, 128), 1)
    half = target.shape[1] // 2
    for u in range(4):
        blocks = []
        for z in range(2):
            rel = z * 4 + (u & 1) * 2 + (u >> 1)
            start = pl.multiple_of((rel ^ high) * 128, 128)
            blocks.append(source[:, pl.ds(start, 128)])
        turned = [pltpu.roll(block, 64, 1) for block in blocks]
        near = jnp.where(lane < 64, blocks[0], turned[1])
        far = jnp.where(lane < 64, turned[0], blocks[1])
        first = jnp.where(low == 0, near, far)
        second = jnp.where(low == 0, far, near)
        target[:, u * 128 : (u + 1) * 128] = first.astype(BF)
        target[:, half + u * 128 : half + (u + 1) * 128] = second.astype(BF)


def attn_fwd_body(s_ref, len_ref, x_ref, w_ref, b_ref, *outs, keep_rows, skip):
    outs = outs[skip:]
    count = len_ref[s_ref[0]]
    x = x_ref[...]
    seq = x.shape[0]
    query = (dg(x, w_ref[0], 1, 0) + b_ref[0:1, :].astype(F32)).astype(BF)
    keyset = dg(x, w_ref[1], 1, 0).astype(BF)
    valueset = (dg(x, w_ref[2], 1, 0) + b_ref[1:2, :].astype(F32)).astype(BF)
    ctx_ref, lse_ref = outs[:2]
    if keep_rows:
        for t, value in enumerate((query, keyset, valueset)):
            outs[2][t] = value
    query = query * BF(HD**-0.5)
    first = lax.broadcasted_iota(jnp.int32, (seq, 2 * HD), 1) < HD
    valid = lax.broadcasted_iota(jnp.int32, (seq, seq), 0) < count
    for pair in range(query.shape[1] // (2 * HD)):
        cut = slice(pair * 2 * HD, (pair + 1) * 2 * HD)
        q_pair, k_pair = query[:, cut], keyset[:, cut]
        turned = valueset[:, cut].T
        parts = []
        for h in range(2):
            own = jnp.where(first if h == 0 else ~first, q_pair, BF(0))
            scores = jnp.where(valid, dg(k_pair, own, 1, 1), NEGATIVE)
            top = jnp.max(scores, axis=0, keepdims=True)
            expo = jnp.exp(scores - top)
            total = jnp.sum(expo, axis=0, keepdims=True)
            part = dg(turned[h * HD : (h + 1) * HD], expo.astype(BF), 1, 0)
            parts.append(part * (1.0 / total))
            at = pair * 2 + h
            lse_ref[0, at : at + 1, :] = top + jnp.log(total)
        ctx_ref[:, cut] = jnp.concatenate(parts, axis=0).T.astype(BF)


def attn_fwd(page, lengths, tokens, weight, bias, keep_rows, tiles, before=()):
    depth = tokens.shape[1]
    seq = tokens.shape[0] // lengths.shape[0]
    cols = weight.shape[2]
    tile = 256
    heads = tile // HD
    start, stop = tiles
    outs = [
        (shaped((seq, cols), BF), pl.BlockSpec((seq, tile), lambda j, s, n: (0, start + j))),
        (
            shaped((cols // tile, heads, seq), F32),
            pl.BlockSpec((1, heads, seq), lambda j, s, n: (start + j, 0, 0)),
        ),
    ]
    if keep_rows:
        outs.append(
            (
                far_shaped((3, seq, cols), BF),
                pl.BlockSpec((3, seq, tile), lambda j, s, n: (0, 0, start + j)),
            )
        )
    return call(
        functools.partial(attn_fwd_body, keep_rows=keep_rows, skip=len(before)),
        "attn_fwd",
        (stop - start,),
        [
            pl.BlockSpec((seq, depth), lambda j, s, n: (s[0], 0)),
            pl.BlockSpec((3, depth, tile), lambda j, s, n: (0, 0, start + j)),
            pl.BlockSpec((2, tile), lambda j, s, n: (0, start + j)),
            *[pl.BlockSpec(memory_space=pl.ANY)] * len(before),
        ],
        outs,
        (tokens, weight, bias, *before),
        (page.reshape(1), lengths),
        stay=(1,),
        aliases={5 + i: i for i in range(len(before))},
    )


def join_body(s_ref, x_ref, own_ref, oth_ref, w_ref, near_ref, core_ref, *refs):
    bias_ref, gain_ref, shift_ref = refs[:3]
    far_ref, normed_ref, scale_ref, low_ref, perm_ref, wide = refs[3:]
    me = s_ref[1]

    @pl.when(pl.program_id(0) == 0)
    def _():
        size = near_ref.shape[1]
        for i in range(2):
            for flip, stack in ((0, near_ref), (1, core_ref)):
                at = pl.multiple_of(((me & 3) ^ (2 * i) ^ flip) * size, 16)
                far_ref[pl.ds(at, size), :] = stack[i]

    attn = dg(own_ref[...], w_ref[...], 1, 0) + dg(oth_ref[...], far_ref[...], 1, 0)
    total = x_ref[...].astype(F32) + attn + bias_ref[...].astype(F32)
    center = total - jnp.mean(total, axis=-1, keepdims=True)
    scale = lax.rsqrt(jnp.mean(center * center, axis=-1, keepdims=True) + EPSILON)
    normed = center * scale
    normed_ref[...] = normed
    scale_ref[...] = scale
    hidden = normed * gain_ref[...].astype(F32) + shift_ref[...].astype(F32)
    low_ref[...] = hidden.astype(BF)
    wide[...] = hidden
    permute_columns(wide, perm_ref, me, wide.shape[0])


def join(scalars, tokens, own, other, weight, near, core, bias, gain, shift):
    seq, cols = own.shape
    depth = tokens.shape[1]
    steps = 2
    rows = seq // steps
    row = pl.BlockSpec((rows, depth), lambda i, s: (i, 0))
    half = pl.BlockSpec((rows, cols), lambda i, s: (i, 0))
    return call(
        join_body,
        "attn_join",
        (steps,),
        [
            pl.BlockSpec((rows, depth), lambda i, s: (s[0] * steps + i, 0)),
            half,
            half,
            whole(cols, depth),
            whole(*near.shape),
            whole(*near.shape),
            *[whole(1, depth)] * 3,
        ],
        [
            (far_shaped((cols, depth), BF), whole(cols, depth)),
            (far_shaped((seq, depth), F32), row),
            (shaped((seq, 1), F32), pl.BlockSpec((rows, 1), lambda i, s: (i, 0))),
            (shaped((seq, depth), BF), row),
            (far_shaped((seq, depth), BF), row),
        ],
        (
            tokens,
            own,
            other,
            weight,
            near,
            core,
            bias.reshape(1, -1),
            gain.reshape(1, -1),
            shift.reshape(1, -1),
        ),
        (scalars,),
        [pltpu.VMEM((rows, depth), F32)],
        flops=4 * seq * cols * depth,
    )


def ffn_tile(h_ref, w_one, b_ref, w_two, act_ref, slope_ref):
    pre = dg(h_ref[...], w_one, 1, 0) + b_ref[...].astype(F32)
    phi = 0.5 + 0.5 * lax.erf(pre * F32(ROOT_HALF))
    act = (pre * phi).astype(BF)
    act_ref[0] = act
    slope_ref[0] = (phi + pre * (jnp.exp(-0.5 * pre * pre) * F32(ROOT_TAU))).astype(BF)
    return dg(act, w_two, 1, 0)


TILE = 512


def accumulate(sum_ref, in_ref, part):
    @pl.when(pl.program_id(0) == 0)
    def _():
        sum_ref[...] = part if in_ref is None else in_ref[...] + part

    @pl.when(pl.program_id(0) > 0)
    def _():
        sum_ref[...] += part


def ffn_own_body(h_ref, w1_ref, b_ref, w2_ref, *refs):
    act_ref, slope_ref, sum_ref = refs[-3:]
    part = ffn_tile(h_ref, w1_ref[...], b_ref, w2_ref[...], act_ref, slope_ref)
    accumulate(sum_ref, refs[0] if len(refs) > 3 else None, part)


def ffn_own(hidden, w_one, bias, w_two, g, before):
    seq, depth = hidden.shape
    units = w_one.shape[1] // 2
    steps = units // TILE
    base = g * steps
    side = pl.BlockSpec((1, seq, TILE), lambda j: (g, 0, j))
    full = whole(seq, depth)
    hbm = pl.BlockSpec(memory_space=pl.ANY)
    return call(
        ffn_own_body,
        "ffn_own",
        (steps,),
        [
            full,
            pl.BlockSpec((depth, TILE), lambda j: (0, base + j)),
            pl.BlockSpec((1, TILE), lambda j: (0, base + j)),
            pl.BlockSpec((TILE, depth), lambda j: (base + j, 0)),
        ]
        + ([full, hbm, hbm] if before else []),
        [
            (shaped((4, seq, units), BF), side),
            (far_shaped((4, seq, units), BF), side),
            (shaped((seq, depth), F32), full),
        ],
        (hidden, w_one, bias.reshape(1, -1), w_two) + before,
        aliases={4: 2, 5: 0, 6: 1} if before else None,
        stay=(1, 3),
    )


def pick_body(s_ref, one_ref, two_ref, more_ref, ffn_ref, out_ref):
    size = one_ref.shape[0]
    ffn_ref[:size] = one_ref[...]
    ffn_ref[size:] = two_ref[...]
    out_ref[...] = more_ref[...]


def pick(scalars, ff1_weight, ff2_weight, more, g):
    depth, units = ff1_weight.shape[0], ff1_weight.shape[1] // 2
    size = depth // 8
    if more.ndim == 2:
        shape = (more.shape[0] // 4, more.shape[1])
        spec = pl.BlockSpec(shape, lambda i, s: (s[1] & 3, 0))
    else:
        shape = (more.shape[0], more.shape[1] // 8, more.shape[2])
        spec = pl.BlockSpec(shape, lambda i, s: (0, s[1] & 7, 0))
    return call(
        pick_body,
        "pick",
        (1,),
        [
            pl.BlockSpec((size, units), lambda i, s: (s[1] & 7, g)),
            pl.BlockSpec((units // 8, depth), lambda i, s: (g * 8 + (s[1] & 7), 0)),
            spec,
        ],
        [
            (shaped((2 * size, units), BF), whole(2 * size, units)),
            (shaped(shape, BF), whole(*shape)),
        ],
        (ff1_weight, ff2_weight, more),
        (scalars,),
        stay=(0, 1, 2),
    )


def collect_body(*refs):
    for i, piece in enumerate(refs[:-1]):
        refs[-1][i] = piece[...]


def collect(pieces):
    shape = pieces[0].shape
    return call(
        collect_body,
        "collect",
        (1,),
        [whole(*shape)] * len(pieces),
        [(shaped((len(pieces),) + shape, BF), whole(len(pieces), *shape))],
        tuple(pieces),
    )[0]


def ffn_far_body(
    s_ref, h_ref, b_ref, near_ref, core_ref, near2_ref, core2_ref, in_ref, *refs, rels
):
    act_ref, slope_ref, sum_ref, w1_ref, w2_ref = refs[-5:]
    j = pl.program_id(0)
    me = s_ref[1]

    def put(target, near, core):
        size = near.shape[1]
        for i, rel in enumerate(rels):
            for flip, stack in ((0, near), (1, core)):
                at = pl.multiple_of(((me & 7) ^ rel ^ flip) * size, 16)
                target[pl.ds(at, size), :] = stack[i]

    @pl.when(j == 0)
    def _():
        put(w2_ref, near2_ref, core2_ref)

    put(w1_ref, near_ref, core_ref)
    w_two = w2_ref[pl.ds(pl.multiple_of(j * TILE, TILE), TILE), :]
    part = ffn_tile(h_ref, w1_ref[...], b_ref, w_two, act_ref, slope_ref)
    accumulate(sum_ref, in_ref, part)


def ffn_far(scalars, hidden, bias, near, core, rels, g, before):
    seq, depth = hidden.shape
    units = bias.shape[0] // 2
    steps = units // TILE
    size = depth // 8
    side = pl.BlockSpec((1, seq, TILE), lambda j, s: (2 + g, 0, j))
    full = whole(seq, depth)
    hbm = pl.BlockSpec(memory_space=pl.ANY)
    one = pl.BlockSpec((4, size, TILE), lambda j, s: (0, 0, j))
    two = pl.BlockSpec(
        (4, size, depth), lambda j, s: (0, 1, 0), pipeline_mode=pl.Buffered(1)
    )
    args = (hidden, bias.reshape(1, -1), near, core, near, core, *before)
    return call(
        functools.partial(ffn_far_body, rels=rels),
        "ffn_far",
        (steps,),
        [
            full,
            pl.BlockSpec((1, TILE), lambda j, s: (0, g * steps + j)),
            one,
            one,
            two,
            two,
            full,
            *[hbm] * (len(before) - 1),
        ],
        [
            (shaped((4, seq, units), BF), side),
            (far_shaped((4, seq, units), BF), side),
            (shaped((seq, depth), F32), full),
            (
                far_shaped((depth, 2 * units), BF),
                pl.BlockSpec((depth, TILE), lambda j, s: (0, g * steps + j)),
            ),
            (
                far_shaped((2 * units, depth), BF),
                pl.BlockSpec((units, depth), lambda j, s: (g, 0), pipeline_mode=pl.Buffered(1)),
            ),
        ],
        args,
        (scalars,),
        aliases={7: 2, 8: 0, 9: 1} | ({10: 3, 11: 4} if g else {}),
        flops=4 * seq * depth * units,
    )


def norm_back(grad, normed, scale):
    return scale * (
        grad
        - jnp.mean(grad, axis=-1, keepdims=True)
        - normed * jnp.mean(grad * normed, axis=-1, keepdims=True)
    )


CHUNK = 64


def chunked(rows, sums_ref, chunk):
    zero = jnp.zeros((1, sums_ref.shape[1]), F32)

    def step(i, sums):
        news = chunk(pl.ds(pl.multiple_of(i * CHUNK, CHUNK), CHUNK))
        return tuple(
            old + jnp.sum(new, axis=0, keepdims=True) for old, new in zip(sums, news)
        )

    sums = lax.fori_loop(0, rows // CHUNK, step, (zero, zero, zero), unroll=True)
    first = pl.program_id(0) == 0
    for i in range(3):
        old = sums_ref[i : i + 1, :]
        sums_ref[i : i + 1, :] = jnp.where(first, 0.0, old) + sums[i]


def norm_two_body(
    s_ref, in_ref, normed_ref, cot_ref, *refs
):
    gain_one, shift_one, bias, gain, shift = [ref[...].astype(F32) for ref in refs[:5]]
    out_ref, ds_ref, df_ref, perm_ref, sums_ref = refs[5:]

    def chunk(at):
        total = normed_ref[at, :] * gain_one + shift_one + in_ref[at, :] + bias
        center = total - jnp.mean(total, axis=-1, keepdims=True)
        scale = lax.rsqrt(jnp.mean(center * center, axis=-1, keepdims=True) + EPSILON)
        normed = center * scale
        out_ref[at, :] = (normed * gain + shift).astype(BF)
        cot = cot_ref[at, :].astype(F32)
        ds = norm_back(cot * gain, normed, scale)
        ds_ref[at, :] = ds
        df_ref[at, :] = ds.astype(BF)
        return ds, cot * normed, cot

    rows = in_ref.shape[0]
    chunked(rows, sums_ref, chunk)
    permute_columns(ds_ref, perm_ref, s_ref[1], rows)


def norm_two(scalars, total, normed, cotangent, vectors):
    seq, depth = total.shape
    steps = 4
    row = pl.BlockSpec((seq // steps, depth), lambda i, s: (i, 0))
    return call(
        norm_two_body,
        "norm_two",
        (steps,),
        [
            row,
            row,
            pl.BlockSpec((seq // steps, depth), lambda i, s: (s[0] * steps + i, 0)),
            *[whole(1, depth)] * 5,
        ],
        [
            (shaped((seq, depth), BF), row),
            (shaped((seq, depth), F32), row),
            (shaped((seq, depth), BF), row),
            (shaped((seq, depth), BF), row),
            (shaped((8, depth), F32), pl.BlockSpec((8, depth), lambda i, s: (0, 0))),
        ],
        (total, normed, cotangent, *[v.reshape(1, -1) for v in vectors]),
        (scalars,),
        stay=(1, 2),
        flops=40 * seq * depth,
    )


def send_order(i):
    return (i % 2) * 2 + i // 2


def ffn_back_body(
    s_ref,
    df_ref,
    w2_ref,
    w2_far_ref,
    slope_ref,
    w1_ref,
    w1_far_ref,
    ds_ref,
    normed_ref,
    scale_ref,
    gain_ref,
    turned_ref,
    dpre_ref,
    db_ref,
    first_ref,
    low_ref,
    perm_ref,
    sums_ref,
    send_a_ref,
    send_b_ref,
    wide,
    *,
    tiles,
):
    j = pl.program_id(0)
    per = dpre_ref.shape[2] // TILE

    @pl.when(j == 0)
    def _():
        wide[...] = ds_ref[...]

    def tile(w_two, w_one):
        dact = dg(df_ref[...], w_two[...], 1, 1)
        dpre = (dact * slope_ref[0].astype(F32)).astype(BF)
        dpre_ref[j // per, :, pl.ds(pl.multiple_of((j % per) * TILE, TILE), TILE)] = dpre
        db_ref[...] = jnp.sum(dpre.astype(F32), axis=0, keepdims=True)
        wide[...] += dg(dpre, w_one[...], 1, 1)

    pl.when(j < tiles // 2)(functools.partial(tile, w2_ref, w1_ref))
    pl.when((j >= tiles // 2) & (j < tiles))(functools.partial(tile, w2_far_ref, w1_far_ref))

    @pl.when(j == tiles - 1)
    def _():
        gain = gain_ref[...].astype(F32)
        zero = jnp.zeros((1, gain.shape[1]), F32)

        def step(i, sums):
            at = pl.ds(pl.multiple_of(i * CHUNK, CHUNK), CHUNK)
            grad = wide[at, :]
            normed = normed_ref[at, :]
            first = norm_back(grad * gain, normed, scale_ref[at, :])
            first_ref[at, :] = first
            low_ref[at, :] = first.astype(BF)
            return tuple(
                old + jnp.sum(new, axis=0, keepdims=True)
                for old, new in zip(sums, (first, grad * normed, grad))
            )

        rows = wide.shape[0]
        sums = lax.fori_loop(0, rows // CHUNK, step, (zero, zero, zero), unroll=2)
        for i in range(3):
            sums_ref[i : i + 1, :] = sums[i]
        permute_columns(first_ref, perm_ref, s_ref[1], rows)

    @pl.when(j >= tiles)
    def _():
        part = dg(turned_ref[...], dpre_ref[send_order(j - tiles)], 0, 0).astype(BF)

        @pl.when(j < tiles + 2)
        def _():
            send_a_ref[0] = part

        @pl.when(j >= tiles + 2)
        def _():
            send_b_ref[0] = part


def ffn_back(
    scalars, dffn, w_two, w_two_far, slope, w_one, w_one_far, dsecond, normed, scale, gain, turned
):
    seq, depth = dffn.shape
    units = slope.shape[2]
    steps = units // TILE
    half = 2 * steps
    tiles = 2 * half
    full = whole(seq, depth)

    def near(j):
        return jnp.minimum(j, half - 1)

    def far(j):
        return jnp.clip(j - half, 0, half - 1)

    def last(j):
        return jnp.minimum(j, tiles - 1)

    def send(first):
        return pl.BlockSpec(
            (1, depth // 2, units), lambda j, s: (jnp.clip(j - first, 0, 1), 0, 0)
        )

    return call(
        functools.partial(ffn_back_body, tiles=tiles),
        "ffn_back",
        (tiles + 4,),
        [
            full,
            pl.BlockSpec((TILE, depth), lambda j, s: (near(j), 0)),
            pl.BlockSpec((TILE, depth), lambda j, s: (far(j), 0)),
            pl.BlockSpec((1, seq, TILE), lambda j, s: (last(j) // steps, 0, last(j) % steps)),
            pl.BlockSpec((depth, TILE), lambda j, s: (0, near(j))),
            pl.BlockSpec((depth, TILE), lambda j, s: (0, far(j))),
            full,
            full,
            whole(seq, 1),
            whole(1, depth),
            pl.BlockSpec((seq, depth // 2), lambda j, s: (0, 1), pipeline_mode=pl.Buffered(1)),
        ],
        [
            (shaped((4, seq, units), BF), whole(4, seq, units)),
            (shaped((1, 4 * units), F32), pl.BlockSpec((1, TILE), lambda j, s: (0, last(j)))),
            (far_shaped((seq, depth), F32), full),
            (shaped((seq, depth), BF), full),
            (shaped((seq, depth), BF), full),
            (shaped((8, depth), F32), whole(8, depth)),
            (shaped((2, depth // 2, units), BF), send(tiles)),
            (shaped((2, depth // 2, units), BF), send(tiles + 2)),
        ],
        (
            dffn,
            w_two,
            w_two_far,
            slope,
            w_one,
            w_one_far,
            dsecond,
            normed,
            scale,
            gain.reshape(1, -1),
            turned,
        ),
        (scalars,),
        [pltpu.VMEM((seq, depth), F32)],
        room=36,
        stay=(1, 2, 3, 4, 5, 7, 10),
    )


def attn_back_tile(count, query, keyset, valueset, lse_ref, dctx, outs):
    seq = query.shape[0]
    query = query * BF(HD**-0.5)
    first = lax.broadcasted_iota(jnp.int32, (seq, 2 * HD), 1) < HD
    valid = lax.broadcasted_iota(jnp.int32, (seq, seq), 0) < count
    for pair in range(query.shape[1] // (2 * HD)):
        cut = slice(pair * 2 * HD, (pair + 1) * 2 * HD)
        q_pair, k_pair, v_pair, dc_pair = query[:, cut], keyset[:, cut], valueset[:, cut], dctx[:, cut]
        dquery = dkeys = dvalues = 0.0
        for h in range(2):
            mask = first if h == 0 else ~first
            q_own = jnp.where(mask, q_pair, BF(0))
            k_own = jnp.where(mask, k_pair, BF(0))
            dc_own = jnp.where(mask, dc_pair, BF(0))
            at = pair * 2 + h
            scores = dg(k_pair, q_own, 1, 1) - lse_ref[0, at : at + 1, :]
            probs = jnp.exp(jnp.where(valid, scores, NEGATIVE))
            dprobs = dg(v_pair, dc_own, 1, 1)
            delta = jnp.sum(probs * dprobs, axis=0, keepdims=True)
            dscores = (probs * (dprobs - delta)).astype(BF)
            dvalues = dvalues + dg(probs.astype(BF), dc_own, 1, 0)
            dkeys = dkeys + dg(dscores, q_own, 1, 0)
            dquery = dquery + dg(dscores, k_own, 0, 0)
        outs[0].append((dquery * HD**-0.5).astype(BF))
        outs[1].append(dkeys.astype(BF))
        outs[2].append(dvalues.astype(BF))


def attn_back_put(j, outs, dqkv_ref, db_ref):
    for t in range(3):
        outs[t] = jnp.concatenate(outs[t], axis=1)
        size = outs[t].shape[1]
        dqkv_ref[t, :, pl.ds(pl.multiple_of(j * size, size), size)] = outs[t]
    db_ref[0:1, :] = jnp.sum(outs[0].astype(F32), axis=0, keepdims=True)
    db_ref[1:2, :] = jnp.sum(outs[2].astype(F32), axis=0, keepdims=True)


def attn_back_end(weight, outs):
    return sum(dg(outs[t], weight[t], 1, 1) for t in range(3))


def attn_back_other_body(
    s_ref,
    len_ref,
    x_ref,
    da_ref,
    wo_ref,
    lse_ref,
    b_ref,
    near_ref,
    core_ref,
    own_ref,
    oth_ref,
    da_turned_ref,
    dqkv_ref,
    db_ref,
    sum_ref,
    turned_ref,
    far_send_ref,
    out_send_ref,
    w_ref,
    wide,
    *,
    rels,
    tiles,
):
    j = pl.program_id(0)
    me = s_ref[1]
    half = turned_ref.shape[1] // 2

    @pl.when(j < tiles)
    def _():
        size = near_ref.shape[2]
        for i, rel in enumerate(rels):
            for flip, stack in ((0, near_ref), (1, core_ref)):
                at = pl.multiple_of(((me & 7) ^ rel ^ flip) * size, 16)
                w_ref[:, pl.ds(at, size), :] = stack[i]
        x = x_ref[...]
        query = (dg(x, w_ref[0], 1, 0) + b_ref[0:1, :].astype(F32)).astype(BF)
        keyset = dg(x, w_ref[1], 1, 0).astype(BF)
        valueset = (dg(x, w_ref[2], 1, 0) + b_ref[1:2, :].astype(F32)).astype(BF)
        dctx = dg(da_ref[...], wo_ref[...], 1, 1).astype(BF)
        outs = [[], [], []]
        attn_back_tile(len_ref[s_ref[0]], query, keyset, valueset, lse_ref, dctx, outs)
        attn_back_put(j, outs, dqkv_ref, db_ref)
        accumulate(sum_ref, None, attn_back_end(w_ref, outs))

    @pl.when(j == 0)
    def _():
        wide[...] = x_ref[...].astype(F32)
        permute_columns(wide, turned_ref, me, x_ref.shape[0])

    @pl.when((j >= tiles) & (j < tiles + 3))
    def _():
        right = dqkv_ref[jnp.clip(j - tiles, 0, 2)]
        far_send_ref[0] = dg(turned_ref[:, half:], right, 0, 0).astype(BF)

    for side, ref in enumerate((own_ref, oth_ref)):

        @pl.when(j == tiles + 3 + side)
        def _():
            out_send_ref[0] = dg(da_turned_ref[...], ref[...], 0, 0).astype(BF)


def attn_back_other(
    scalars, lengths, tokens, dattn, out_w, logsum, bias, near, core, rels, own, other, da_turned
):
    seq, depth = dattn.shape
    cols = out_w.shape[0]
    tile = 256
    heads = tile // HD
    tiles = cols // tile
    half = depth // 2

    def at(j):
        return jnp.minimum(j, tiles - 1)

    stack = pl.BlockSpec((4, 3, depth // 8, tile), lambda j, s, n: (0, 0, 0, at(j)))
    return call(
        functools.partial(attn_back_other_body, rels=rels, tiles=tiles),
        "attn_back_other",
        (tiles + 5,),
        [
            pl.BlockSpec((seq, depth), lambda j, s, n: (s[0], 0)),
            whole(seq, depth),
            pl.BlockSpec((tile, depth), lambda j, s, n: (at(j), 0)),
            pl.BlockSpec((1, heads, seq), lambda j, s, n: (at(j), 0, 0)),
            pl.BlockSpec((2, tile), lambda j, s, n: (0, at(j))),
            stack,
            stack,
            whole(seq, cols),
            whole(seq, cols),
            pl.BlockSpec((seq, half), lambda j, s, n: (0, 1), pipeline_mode=pl.Buffered(1)),
        ],
        [
            (shaped((3, seq, cols), BF), whole(3, seq, cols)),
            (shaped((2, cols), F32), pl.BlockSpec((2, tile), lambda j, s, n: (0, at(j)))),
            (far_shaped((seq, depth), F32), whole(seq, depth)),
            (shaped((seq, depth), BF), whole(seq, depth)),
            (
                shaped((3, half, cols), BF),
                pl.BlockSpec((1, half, cols), lambda j, s, n: (jnp.clip(j - tiles, 0, 2), 0, 0)),
            ),
            (
                shaped((2, half, cols), BF),
                pl.BlockSpec(
                    (1, half, cols), lambda j, s, n: (jnp.clip(j - tiles - 3, 0, 1), 0, 0)
                ),
            ),
        ],
        (tokens, dattn, out_w, logsum, bias, near, core, own, other, da_turned),
        (scalars, lengths),
        [pltpu.VMEM((3, depth, tile), BF), pltpu.VMEM((seq, depth), F32)],
        room=30,
        stay=(0, 2),
    )


def attn_back_own_body(
    s_ref,
    len_ref,
    da_ref,
    wo_ref,
    lse_ref,
    qkv_ref,
    w_ref,
    in_ref,
    first_ref,
    turned_ref,
    dqkv_ref,
    db_ref,
    grad_ref,
    send_ref,
    wide,
    *,
    tiles,
):
    j = pl.program_id(0)

    @pl.when(j < tiles)
    def _():
        dctx = dg(da_ref[...], wo_ref[...], 1, 1).astype(BF)
        count = len_ref[s_ref[0]]
        outs = [[], [], []]
        attn_back_tile(count, qkv_ref[0], qkv_ref[1], qkv_ref[2], lse_ref, dctx, outs)
        attn_back_put(j, outs, dqkv_ref, db_ref)
        part = attn_back_end(w_ref, outs)

        @pl.when(j == 0)
        def _():
            wide[...] = in_ref[...] + first_ref[...] + part

        @pl.when(j == tiles - 1)
        def _():
            grad_ref[...] = (wide[...] + part).astype(BF)

    @pl.when(j >= tiles)
    def _():
        right = dqkv_ref[jnp.clip(j - tiles, 0, 2)]
        send_ref[0] = dg(turned_ref[...], right, 0, 0).astype(BF)


def attn_back_own(
    scalars, lengths, dattn, out_w, logsum, qkv, weight, partial, dfirst, turned
):
    seq, depth = dattn.shape
    cols = out_w.shape[0]
    tile = 256
    heads = tile // HD
    tiles = cols // tile
    half = depth // 2
    full = whole(seq, depth)

    def at(j):
        return jnp.minimum(j, tiles - 1)

    return call(
        functools.partial(attn_back_own_body, tiles=tiles),
        "attn_back_own",
        (tiles + 3,),
        [
            full,
            pl.BlockSpec((tile, depth), lambda j, s, n: (at(j), 0)),
            pl.BlockSpec((1, heads, seq), lambda j, s, n: (at(j), 0, 0)),
            pl.BlockSpec((3, seq, tile), lambda j, s, n: (0, 0, at(j))),
            pl.BlockSpec((3, depth, tile), lambda j, s, n: (0, 0, at(j))),
            full,
            full,
            pl.BlockSpec((seq, half), lambda j, s, n: (0, 1), pipeline_mode=pl.Buffered(1)),
        ],
        [
            (shaped((3, seq, cols), BF), whole(3, seq, cols)),
            (shaped((2, cols), F32), pl.BlockSpec((2, tile), lambda j, s, n: (0, at(j)))),
            (shaped((seq, depth), BF), full),
            (
                shaped((3, half, cols), BF),
                pl.BlockSpec((1, half, cols), lambda j, s, n: (jnp.clip(j - tiles, 0, 2), 0, 0)),
            ),
        ],
        (dattn, out_w, logsum, qkv, weight, partial, dfirst, turned),
        (scalars, lengths),
        [pltpu.VMEM((seq, depth), F32)],
        room=30,
        stay=(1, 3, 4, 5, 6),
    )


def grad_send_body(a_ref, b_ref, out_ref):
    out_ref[0] = dg(a_ref[...], b_ref[0], 0, 0).astype(BF)


def grad_specs(turned, right, picks, part):
    seq, units = right.shape[1:]
    half = turned.shape[1] // 2
    start, stride = picks[0], (picks[1] - picks[0] if len(picks) > 1 else 1)
    return [
        pl.BlockSpec((seq, half), lambda i: (0, part), pipeline_mode=pl.Buffered(1)),
        pl.BlockSpec((1, seq, units), lambda i: (start + stride * i, 0, 0)),
    ], pl.BlockSpec((1, half, units), lambda i: (i, 0, 0))


def grad_send(turned, right, picks):
    seq, units = right.shape[1:]
    half = turned.shape[1] // 2
    count = len(picks)
    ins, out = grad_specs(turned, right, picks, 1)
    return call(
        grad_send_body,
        "grad_send",
        (count,),
        ins,
        [(shaped((count, half, units), BF), out)],
        (turned, right),
        flops=2 * count * seq * half * units,
    )[0]


def keep_ffn_body(a_ref, b_ref, ra_ref, rb_ref, keep_ref, send_ref, own_ref, far_ref):
    i = pl.program_id(0)
    part = dg(a_ref[...], b_ref[0], 0, 0)
    cut = keep_ref.shape[1]

    @pl.when(i < 2)
    def _():
        total = (part + ra_ref[0].astype(F32)).astype(BF)
        keep_ref[0] = total[:cut]
        send_ref[0] = total[cut:]

    @pl.when(i >= 2)
    def _():
        total = (part + rb_ref[0].astype(F32)).astype(BF)

        @pl.when(i == 2)
        def _():
            own_ref[...] = total

        @pl.when(i == 3)
        def _():
            far_ref[...] = total


def keep_ffn(turned, right, got_a, got_b):
    _, seq, units = right.shape
    half = turned.shape[1] // 2
    cut = pl.BlockSpec((1, half // 2, units), lambda i: (jnp.minimum(i, 1), 0, 0))
    return call(
        keep_ffn_body,
        "keep_ffn",
        (4,),
        [
            pl.BlockSpec((seq, half), lambda i: (0, 0), pipeline_mode=pl.Buffered(1)),
            pl.BlockSpec((1, seq, units), lambda i: (send_order(i), 0, 0)),
            pl.BlockSpec((1, half, units), lambda i: (jnp.minimum(i, 1), 0, 0)),
            pl.BlockSpec((1, half, units), lambda i: (jnp.maximum(i - 2, 0), 0, 0)),
        ],
        [
            (shaped((2, half // 2, units), BF), cut),
            (shaped((2, half // 2, units), BF), cut),
            (shaped((half, units), BF), whole(half, units)),
            (shaped((half, units), BF), whole(half, units)),
        ],
        (turned, right, got_a, got_b),
        room=24,
    )


def total(*refs):
    return sum(ref.astype(F32) for ref in refs).astype(BF)


def second_body(ka_ref, ga_ref, bo_ref, gb_ref, a_own_ref, a_far_ref, b_own_ref, b_send_ref):
    a_own_ref[...] = total(ka_ref[0], ga_ref[0])
    a_far_ref[...] = total(ka_ref[1], ga_ref[1])
    half = b_own_ref.shape[0]
    b_own_ref[...] = total(bo_ref[:half], gb_ref[:half])
    b_send_ref[...] = total(bo_ref[half:], gb_ref[half:])


def second(keep_a, got_a, b_own, got_b):
    _, rows, units = keep_a.shape
    part = (shaped((rows, units), BF), whole(rows, units))
    return call(
        second_body,
        "second",
        (1,),
        [whole(2, rows, units)] * 2 + [whole(2 * rows, units)] * 2,
        [part] * 4,
        (keep_a, got_a, b_own, got_b),
    )


def third_body(a_ref, ga_ref, b_ref, gb_ref, keep_ref, send_ref):
    half, units = keep_ref.shape[0], a_ref.shape[1]
    for at, (left, right) in enumerate(((a_ref, ga_ref), (b_ref, gb_ref))):
        cut = slice(at * units, (at + 1) * units)
        keep_ref[:, cut] = total(left[:half], right[:half])
        send_ref[:, cut] = total(left[half:], right[half:])


def third(a_own, got_a, b_own, got_b):
    rows, units = a_own.shape
    part = (shaped((rows // 2, 2 * units), BF), whole(rows // 2, 2 * units))
    return call(
        third_body,
        "third",
        (1,),
        [whole(rows, units)] * 4,
        [part] * 2,
        (a_own, got_a, b_own, got_b),
    )


def fourth_body(a_ref, g_ref, keep_ref, send_ref):
    half = keep_ref.shape[-2]
    keep_ref[...] = total(a_ref[..., :half, :], g_ref[..., :half, :])
    send_ref[...] = total(a_ref[..., half:, :], g_ref[..., half:, :])


def fourth(values, got):
    shape = values.shape
    out = shape[:-2] + (shape[-2] // 2, shape[-1])
    return call(
        fourth_body,
        "fourth",
        (1,),
        [whole(*shape)] * 2,
        [(shaped(out, BF), whole(*out))] * 2,
        (values, got),
    )


def keep_far_body(
    da_ref, a_ref, own_ref, oth_ref, b_ref, ro_ref, rf_ref, keep_ref, send_ref, far_ref
):
    i = pl.program_id(0)
    cut = keep_ref.shape[1]

    def split(value):
        keep_ref[0] = value[:cut]
        send_ref[0] = value[cut:]

    for side, ref in enumerate((own_ref, oth_ref)):

        @pl.when(i == side)
        def _():
            split((dg(da_ref[...], ref[...], 0, 0) + ro_ref[0].astype(F32)).astype(BF))

    @pl.when(i >= 2)
    def _():
        value = (dg(a_ref[...], b_ref[0], 0, 0) + rf_ref[0].astype(F32)).astype(BF)

        @pl.when(i == 2)
        def _():
            split(value)

        @pl.when(i > 2)
        def _():
            far_ref[0] = value


def keep_far(da_turned, turned, own, other, dqkv, got_out, got_far):
    _, seq, cols = dqkv.shape
    half = turned.shape[1] // 2
    left = pl.BlockSpec((seq, half), lambda i: (0, 0), pipeline_mode=pl.Buffered(1))
    cut = pl.BlockSpec((1, half // 2, cols), lambda i: (jnp.minimum(i, 2), 0, 0))
    return call(
        keep_far_body,
        "keep_far",
        (5,),
        [
            left,
            left,
            whole(seq, cols),
            whole(seq, cols),
            pl.BlockSpec((1, seq, cols), lambda i: (jnp.maximum(i - 2, 0), 0, 0)),
            pl.BlockSpec((1, half, cols), lambda i: (jnp.minimum(i, 1), 0, 0)),
            pl.BlockSpec((1, half, cols), lambda i: (jnp.maximum(i - 2, 0), 0, 0)),
        ],
        [
            (shaped((3, half // 2, cols), BF), cut),
            (shaped((3, half // 2, cols), BF), cut),
            (
                shaped((2, half, cols), BF),
                pl.BlockSpec((1, half, cols), lambda i: (jnp.maximum(i - 3, 0), 0, 0)),
            ),
        ],
        (da_turned, turned, own, other, dqkv, got_out, got_far),
    )


def second_attn_body(k_ref, g_ref, out_ref, far_ref):
    out_ref[0] = total(k_ref[0], g_ref[0])
    far_ref[0] = total(k_ref[2], g_ref[2])
    far_ref[1] = total(k_ref[1], g_ref[1])


def second_attn(keep, got):
    _, rows, cols = keep.shape
    return call(
        second_attn_body,
        "second_attn",
        (1,),
        [whole(3, rows, cols)] * 2,
        [(shaped((n, rows, cols), BF), whole(n, rows, cols)) for n in (1, 2)],
        (keep, got),
    )


def keep_own_body(a_ref, b_ref, r_ref, gb_ref, keep_ref, send_ref):
    i = pl.program_id(0)
    value = dg(a_ref[...], b_ref[0], 0, 0) + r_ref[0].astype(F32)
    cut = keep_ref.shape[1]
    value = jnp.where(i == 0, value, value + gb_ref[0].astype(F32)).astype(BF)
    keep_ref[0] = value[:cut]
    send_ref[0] = value[cut:]


def keep_own(turned, dqkv, got, got_b):
    _, seq, cols = dqkv.shape
    half = turned.shape[1] // 2
    part = (
        shaped((3, half // 2, cols), BF),
        pl.BlockSpec((1, half // 2, cols), lambda i: (i, 0, 0)),
    )
    return call(
        keep_own_body,
        "keep_own",
        (3,),
        [
            pl.BlockSpec((seq, half), lambda i: (0, 0), pipeline_mode=pl.Buffered(1)),
            pl.BlockSpec((1, seq, cols), lambda i: (i, 0, 0)),
            pl.BlockSpec((1, half, cols), lambda i: (i, 0, 0)),
            pl.BlockSpec((1, half, cols), lambda i: (jnp.maximum(i - 1, 0), 0, 0)),
        ],
        [part] * 2,
        (turned, dqkv, got, got_b),
    )


def join_attn_body(k_ref, x_ref, o_ref, y_ref, keep_ref, send_ref):
    half = keep_ref.shape[1]
    for ref, cut in ((keep_ref, slice(0, half)), (send_ref, slice(half, 2 * half))):
        ref[0] = total(k_ref[0, cut], x_ref[0, cut], y_ref[0, cut])
        ref[1] = total(k_ref[1, cut], x_ref[1, cut])
        ref[2] = total(k_ref[2, cut], x_ref[2, cut])
        ref[3] = total(o_ref[0, cut], y_ref[1, cut])


def join_attn(keep, got_x, out, got_y):
    _, rows, cols = keep.shape
    part = (shaped((4, rows // 2, cols), BF), whole(4, rows // 2, cols))
    return call(
        join_attn_body,
        "join_attn",
        (1,),
        [whole(3, rows, cols), whole(3, rows, cols), whole(1, rows, cols), whole(2, rows, cols)],
        [part] * 2,
        (keep, got_x, out, got_y),
    )


def swap(values, bit):
    count = lax.axis_size("dp")
    return lax.ppermute(values, "dp", [(i, i ^ (1 << bit)) for i in range(count)])


def swap_y(values):
    return lax.ppermute(values, "mp", [(0, 1), (1, 0)])


def add(left, right):
    return left.astype(F32) + right.astype(F32)


def low_add(left, right):
    return add(left, right).astype(BF)


def after(value, tick):
    flat, tree = jax.tree.flatten(value)
    arrays = [i for i, leaf in enumerate(flat) if not isinstance(leaf, int)]
    held = lax.optimization_barrier(([flat[i] for i in arrays], tick))[0]
    for i, leaf in zip(arrays, held):
        flat[i] = leaf
    return jax.tree.unflatten(tree, flat)


def sum_everywhere(values):
    count = lax.axis_size("dp")
    for bit in range(count.bit_length() - 1):
        values = values + swap(values, bit)
    return values + swap_y(values)


def paged(
    tokens,
    page_lengths,
    qkv_weight,
    qv_bias,
    out_weight,
    out_bias,
    ln1_gain,
    ln1_bias,
    ff1_weight,
    ff1_bias,
    ff2_weight,
    ff2_bias,
    ln2_gain,
    ln2_bias,
    cotangent,
):
    row_count, depth = tokens.shape
    seq = row_count // 2
    cols = qkv_weight.shape[2]
    units = ff1_weight.shape[1] // 2
    group = lax.axis_index("mp")
    me = lax.axis_index("dp")

    ready = (jnp.stack([group, me]).astype(jnp.int32), 1 - group, group, group == 0)
    scalars, far_page, own_page, is_first = lax.optimization_barrier(ready)

    def in_order(own, far):
        return jnp.where(
            is_first,
            jnp.concatenate([own, far], axis=-1),
            jnp.concatenate([far, own], axis=-1),
        )

    def outer(mine, bits):
        return [mine] + [swap(mine, bit) for bit in bits]

    def rels(bits):
        one, two = (1 << bit for bit in bits)
        return (0, one, two, one | two)

    ways = ((1, 2), (2, 1), (1, 2))

    block0, out_block = pick(scalars, ff1_weight, ff2_weight, out_weight, 0)
    out_mine, mine0 = swap_y(out_block), swap_y(block0)
    far_ctx, far_lse = attn_fwd(
        far_page, page_lengths, after(tokens, block0), qkv_weight, qv_bias, False, (0, 2)
    )
    oth_ctx, oth_lse = swap_y(far_ctx), swap_y(far_lse)
    own = attn_fwd(
        own_page, page_lengths, after(tokens, far_ctx), qkv_weight, qv_bias, True, (0, 1)
    )
    out_mine, mine0 = after((out_mine, mine0), own[0])
    out_x = swap(out_mine, 1)
    by_z = swap(mine0, 2)
    own_ctx, own_lse, own_qkv = attn_fwd(
        own_page, page_lengths, after(tokens, mine0), qkv_weight, qv_bias, True, (1, 2), own
    )
    out_near = collect([out_mine, after(out_x, own_ctx)])
    by_x = swap(after(mine0, out_near), 1)
    out_core = swap(out_near, 0)
    block1, qkv_block = pick(after(scalars, out_near), ff1_weight, ff2_weight, qkv_weight, 1)
    mine1 = swap_y(block1)
    ff1_far, qv_far = swap_y(after(ff1_bias, block1)), swap_y(after(qv_bias, block1))
    out_far, normed_one, scale_one, hidden, hidden_turned = join(
        scalars,
        tokens,
        own_ctx,
        after(oth_ctx, block1),
        out_weight,
        out_near,
        out_core,
        out_bias,
        ln1_gain,
        ln1_bias,
    )
    by_x, by_z, hidden, oth_lse, ff1_far, qv_far = lax.optimization_barrier(
        (by_x, by_z, hidden, oth_lse, ff1_far, qv_far)
    )
    stage0 = [mine0, by_x, by_z]
    last0 = swap(by_z, 1)
    act, slope, partial = ffn_own(hidden, ff1_weight, ff1_bias, ff2_weight, 0, ())
    mine1 = after(mine1, partial)
    stage1 = outer(mine1, ways[1])
    act, slope, partial = ffn_own(
        hidden, ff1_weight, ff1_bias, ff2_weight, 1, (after(partial, mine1), act, slope)
    )
    qkv_mine = swap_y(after(qkv_block, mine1))
    stage1, last0 = after((stage1, last0), partial)
    last1 = swap(stage1[2], ways[1][0])
    near0 = collect(after(stage0 + [last0], stage1[2]))
    core0 = swap(near0, 0)
    act, slope, partial, w1_far, w2_far = ffn_far(
        scalars,
        hidden,
        ff1_far,
        near0,
        core0,
        rels(ways[0]),
        0,
        (partial, act, slope),
    )
    last1, qkv_mine = after((last1, qkv_mine), partial)
    near1 = collect(stage1 + [last1])
    core1 = swap(near1, 0)
    qkv_stage = outer(after(qkv_mine, near1), ways[2])
    act, slope, partial, w1_far, w2_far = ffn_far(
        scalars,
        hidden,
        ff1_far,
        near1,
        core1,
        rels(ways[1]),
        1,
        (partial, act, slope, w1_far, w2_far),
    )
    out_rows, dsecond, dffn, dffn_turned, sums_two = norm_two(
        scalars,
        partial,
        normed_one,
        cotangent,
        (ln1_gain, ln1_bias, ff2_bias, ln2_gain, ln2_bias),
    )

    qkv_stage = after(qkv_stage, dffn)
    last = swap(qkv_stage[2], ways[2][0])
    send_a = grad_send(after(dffn_turned, qkv_stage[0]), act, (0, 2))
    send_b = grad_send(after(dffn_turned, send_a), act, (1, 3))
    got_a, got_b = swap(send_a, 0), swap(send_b, 0)
    keep_a, send_a, b_own, b_far = keep_ffn(after(dffn_turned, send_b), act, got_a, got_b)
    ff2_x, ff2_y = swap(send_a, 1), swap_y(b_far)
    last = after(last, keep_a)
    dpre, db, dfirst, dattn, dattn_turned, sums_one, send_a, send_b = ffn_back(
        scalars,
        after(dffn, last),
        ff2_weight,
        w2_far,
        slope,
        ff1_weight,
        w1_far,
        dsecond,
        normed_one,
        scale_one,
        ln1_gain,
        hidden_turned,
    )
    got_a, got_b = swap(send_a, 0), swap(send_b, 0)
    qkv_near = collect(after(qkv_stage + [last], dattn))
    qkv_core = swap(qkv_near, 0)
    ff2_own, ff2_far, ff2_keep, ff2_send = second(after(keep_a, qkv_near), ff2_x, b_own, ff2_y)
    ff2_y, ff2_x = swap_y(ff2_far), swap(ff2_send, 1)
    keep_a, send_a, b_own, b_far = keep_ffn(after(hidden_turned, ff2_own), dpre, got_a, got_b)
    ff1_x, ff1_y = swap(send_a, 1), swap_y(b_far)
    dqkv_far, dqv_far, dtok, tok_turned, far_send, out_send = attn_back_other(
        scalars,
        page_lengths,
        tokens,
        after(dattn, keep_a),
        out_far,
        oth_lse,
        qv_far,
        qkv_near,
        qkv_core,
        rels(ways[2]),
        own_ctx,
        oth_ctx,
        dattn_turned,
    )
    out_got, far_got = swap(out_send, 0), swap(far_send, 0)
    ff2_keep, ff2_send = third(after(ff2_own, dtok), ff2_y, ff2_keep, ff2_x)
    ff2_z = swap(ff2_send, 2)
    ff1_own, ff1_far, ff1_keep, ff1_send = second(after(keep_a, ff2_keep), ff1_x, b_own, ff1_y)
    ff1_y, ff1_x = swap_y(ff1_far), swap(ff1_send, 1)
    far_keep, far_send, b_far = keep_far(
        after(dattn_turned, ff1_own), tok_turned, own_ctx, oth_ctx, dqkv_far, out_got, far_got
    )
    far_x, far_y = swap(far_send, 1), swap_y(b_far)
    dqkv_own, dqv_own, input_grad, own_send = attn_back_own(
        scalars,
        page_lengths,
        after(dattn, far_keep),
        out_weight,
        own_lse,
        own_qkv,
        qkv_weight,
        dtok,
        dfirst,
        tok_turned,
    )
    own_got = swap(own_send, 0)
    ff1_keep, ff1_send = third(after(ff1_own, own_send), ff1_y, ff1_keep, ff1_x)
    ff1_z = swap(ff1_send, 2)
    ff2_keep, ff2_send = fourth(after(ff2_keep, ff1_keep), ff2_z)
    ff2_z = swap(ff2_send, 3)
    far_keep, far_x, far_y = after((far_keep, far_x, far_y), ff2_keep)
    out_keep, far_send = second_attn(far_keep, far_x)
    got_y = swap_y(far_send)
    keep, send = keep_own(after(tok_turned, out_keep), dqkv_own, own_got, far_y)
    got_x = swap(send, 1)
    db, dqv_own, dqv_far = after((db, dqv_own, dqv_far), keep)
    small = jnp.concatenate(
        [
            in_order(dqv_own, dqv_far).reshape(-1),
            in_order(db[:, : 2 * units], db[:, 2 * units :]).reshape(-1),
            sums_one[:3].reshape(-1),
            sums_two[:3].reshape(-1),
        ]
    ).reshape(-1, 128)
    ff1_keep, ff1_send = fourth(after(ff1_keep, keep), ff1_z)
    ff1_z = swap(ff1_send, 3)
    small = small + after(swap(small, 0), ff1_keep)
    ff2_share = add(*after((ff2_keep, ff2_z), small))
    small = small + after(swap(small, 1), ff2_share)
    keep, send = join_attn(after(keep, small), got_x, out_keep, got_y)
    got = swap(send, 2)
    small = small + after(swap(small, 2), keep)
    ff1_share = add(*after((ff1_keep, ff1_z), small))
    small = small + after(swap(small, 3), ff1_share)
    keep, send = fourth(after(keep, small), got)
    got = swap(send, 3)
    small = (small + after(swap_y(small), keep)).reshape(-1)
    share = add(keep, got)
    qkv_share, out_share = share[:3], share[3]
    ends = []
    at = 0
    for length in (4 * cols, 4 * units, depth, depth, depth, depth, depth, depth):
        ends.append(small[at : at + length])
        at += length
    return (
        out_rows,
        input_grad,
        qkv_share,
        ends[0].reshape(2, -1),
        out_share.T,
        ends[2],
        ends[3],
        ends[4],
        ff1_share,
        ends[1],
        ff2_share.T,
        ends[5],
        ends[6],
        ends[7],
    )


def suits(mesh):
    return mesh.shape["mp"] == 2 and mesh.shape["dp"] == 16


def solution(mesh):
    in_specs = (
        P("dp", None),
        P("dp"),
        P(None, None, "mp"),
        P(None, "mp"),
        P("mp", None),
        P(),
        P(),
        P(),
        P(None, "mp"),
        P("mp"),
        P("mp", None),
        P(),
        P(),
        P(),
        P("dp", None),
    )
    out_specs = (
        P(("dp", "mp"), None),
        P(("dp", "mp"), None),
        P(None, "dp", "mp"),
        P(),
        P("mp", "dp"),
        P(),
        P(),
        P(),
        P("dp", "mp"),
        P(),
        P("mp", "dp"),
        P(),
        P(),
        P(),
    )
    body = paged if suits(mesh) else local
    return jax.shard_map(body, mesh=mesh, in_specs=in_specs, out_specs=out_specs, check_vma=False)
```

```python
import functools

import jax
import jax.numpy as jnp
from jax import lax
from jax.experimental import pallas as pl
from jax.experimental.pallas import tpu as pltpu
from jax.sharding import PartitionSpec as P

HD = 64


EPSILON = 1e-05
NEGATIVE = -1e30


def normalize(values):
    center = values - jnp.mean(values, axis=-1, keepdims=True)
    spread = jnp.mean(center * center, axis=-1, keepdims=True)
    return center * lax.rsqrt(spread + EPSILON)


def gelu_exact(values):
    return jax.nn.gelu(values, approximate=False)


def over_rows(left, right):
    return lax.dot_general(
        left, right, (((0,), (0,)), ((), ())), preferred_element_type=jnp.float32
    )


def over_cols(left, right):
    return lax.dot_general(
        left, right, (((1,), (1,)), ((), ())), preferred_element_type=jnp.float32
    )


def page_scores(query, keyset, valid):
    raw = jnp.einsum("qhe,khe->hqk", query, keyset, preferred_element_type=jnp.float32) * HD ** (
        -0.5
    )
    return jnp.where(valid[None, None, :], raw, NEGATIVE)


def attend(block):
    query, keyset, valueset, valid = block
    scores = page_scores(query, keyset, valid)
    top = jnp.max(scores, axis=-1, keepdims=True)
    expo = jnp.exp(scores - top)
    total = jnp.sum(expo, axis=-1, keepdims=True)
    probs = expo / total
    context = jnp.einsum(
        "hqk,khe->qhe", probs.astype(jnp.bfloat16), valueset, preferred_element_type=jnp.float32
    )
    context = context.astype(jnp.bfloat16)
    return (context.reshape(context.shape[0], -1), top[..., 0] + jnp.log(total[..., 0]))


def attend_back(block):
    query, keyset, valueset, valid, logsum, dcontext = block
    scale = HD ** (-0.5)
    scores = page_scores(query, keyset, valid)
    probs = jnp.exp(scores - logsum[..., None])
    dprobs = jnp.einsum("qhe,khe->hqk", dcontext, valueset, preferred_element_type=jnp.float32)
    delta = jnp.sum(probs * dprobs, axis=-1, keepdims=True)
    dscores = (probs * (dprobs - delta)).astype(jnp.bfloat16)
    dquery = (
        jnp.einsum("hqk,khe->qhe", dscores, keyset, preferred_element_type=jnp.float32) * scale
    ).astype(jnp.bfloat16)
    dkeys = (
        jnp.einsum("hqk,qhe->khe", dscores, query, preferred_element_type=jnp.float32) * scale
    ).astype(jnp.bfloat16)
    dvalues = jnp.einsum(
        "hqk,qhe->khe", probs.astype(jnp.bfloat16), dcontext, preferred_element_type=jnp.float32
    ).astype(jnp.bfloat16)
    seq_len = query.shape[0]
    return (dquery.reshape(seq_len, -1), dkeys.reshape(seq_len, -1), dvalues.reshape(seq_len, -1))


def local(
    tokens,
    page_lengths,
    qkv_weight,
    qv_bias,
    out_weight,
    out_bias,
    ln1_gain,
    ln1_bias,
    ff1_weight,
    ff1_bias,
    ff2_weight,
    ff2_bias,
    ln2_gain,
    ln2_bias,
    cotangent,
):
    row_count = tokens.shape[0]
    page_count = page_lengths.shape[0]
    seq_len = row_count // page_count
    cols = qkv_weight.shape[2]
    ff_cols = ff1_weight.shape[1]
    group_heads = cols // HD
    share = row_count // lax.axis_size("mp")
    group = lax.axis_index("mp")
    share_start = group * share
    gain_one = ln1_gain.astype(jnp.float32)
    shift_one = ln1_bias.astype(jnp.float32)
    gain_two = ln2_gain.astype(jnp.float32)
    shift_two = ln2_bias.astype(jnp.float32)

    def own_rows(values):
        return lax.dynamic_slice_in_dim(values, share_start, share, 0)

    projected = jnp.einsum("rd,tdc->trc", tokens, qkv_weight, preferred_element_type=jnp.float32)
    bias_rows = jnp.stack([qv_bias[0], jnp.zeros_like(qv_bias[0]), qv_bias[1]]).astype(jnp.float32)
    qkv_rows = (projected + bias_rows[:, None, :]).astype(jnp.bfloat16)
    qkv_pages = qkv_rows.reshape(3, page_count, seq_len, group_heads, HD)
    valid = jnp.arange(seq_len)[None, :] < page_lengths[:, None]
    context, logsum = lax.map(attend, (qkv_pages[0], qkv_pages[1], qkv_pages[2], valid))
    context = context.reshape(row_count, cols)
    attn_part = jnp.dot(context, out_weight, preferred_element_type=jnp.float32).astype(
        jnp.bfloat16
    )
    attn = lax.psum(attn_part, "mp").astype(jnp.float32)
    first_sum = tokens.astype(jnp.float32) + attn + out_bias.astype(jnp.float32)
    normed_one, norm_one_back = jax.vjp(normalize, first_sum)
    hidden = normed_one * gain_one + shift_one
    hidden_low = hidden.astype(jnp.bfloat16)
    normed_one_own = own_rows(normed_one)
    pre = jnp.dot(hidden_low, ff1_weight, preferred_element_type=jnp.float32) + ff1_bias.astype(
        jnp.float32
    )
    activated, gelu_back = jax.vjp(gelu_exact, pre)
    act_low = activated.astype(jnp.bfloat16)
    ffn_part = jnp.dot(act_low, ff2_weight, preferred_element_type=jnp.float32).astype(jnp.bfloat16)
    cot_own = own_rows(cotangent).astype(jnp.float32)
    ffn = lax.psum(ffn_part, "mp").astype(jnp.float32)
    second_sum = hidden + ffn + ff2_bias.astype(jnp.float32)
    normed_two, norm_two_back = jax.vjp(normalize, second_sum)
    normed_two_own = own_rows(normed_two)
    out_rows = (normed_two_own * gain_two + shift_two).astype(jnp.bfloat16)
    dsecond = norm_two_back(cotangent.astype(jnp.float32) * gain_two)[0]
    dffn = dsecond.astype(jnp.bfloat16)
    dsecond_own = own_rows(dsecond)
    dgain_two = jnp.sum(cot_own * normed_two_own, axis=0)
    dshift_two = jnp.sum(cot_own, axis=0)
    dff2_bias = jnp.sum(dsecond_own, axis=0)
    dff2_weight = over_rows(act_low, dffn)
    dact = over_cols(dffn, ff2_weight)
    dpre = gelu_back(dact)[0].astype(jnp.bfloat16)
    dff1_bias = jnp.sum(dpre.astype(jnp.float32), axis=0)
    dff1_weight = over_rows(hidden_low, dpre)
    dhid_part = over_cols(dpre, ff1_weight).astype(jnp.bfloat16)
    dhidden = dsecond + lax.psum(dhid_part, "mp").astype(jnp.float32)
    dfirst = norm_one_back(dhidden * gain_one)[0]
    dattn = dfirst.astype(jnp.bfloat16)
    dhidden_own = own_rows(dhidden)
    dfirst_own = own_rows(dfirst)
    dgain_one = jnp.sum(dhidden_own * normed_one_own, axis=0)
    dshift_one = jnp.sum(dhidden_own, axis=0)
    dout_bias = jnp.sum(dfirst_own, axis=0)
    dout_weight = over_rows(context, dattn)
    dcontext = over_cols(dattn, out_weight).astype(jnp.bfloat16)
    dcontext_pages = dcontext.reshape(page_count, seq_len, group_heads, HD)
    dquery, dkeys, dvalues = lax.map(
        attend_back, (qkv_pages[0], qkv_pages[1], qkv_pages[2], valid, logsum, dcontext_pages)
    )
    dqkv = jnp.stack(
        [
            dquery.reshape(row_count, cols),
            dkeys.reshape(row_count, cols),
            dvalues.reshape(row_count, cols),
        ]
    )
    dqv_bias = jnp.stack(
        [jnp.sum(dqkv[0].astype(jnp.float32), axis=0), jnp.sum(dqkv[2].astype(jnp.float32), axis=0)]
    )
    dqkv_weight = jnp.einsum("rd,trc->tdc", tokens, dqkv, preferred_element_type=jnp.float32)
    dtok_part = jnp.einsum(
        "trc,tdc->rd", dqkv, qkv_weight, preferred_element_type=jnp.float32
    ).astype(jnp.bfloat16)
    input_grad = (
        dfirst_own
        + lax.psum_scatter(dtok_part, "mp", scatter_dimension=0, tiled=True).astype(jnp.float32)
    ).astype(jnp.bfloat16)
    qkv_share, out_share, ff1_share, ff2_share = (
        lax.psum_scatter(
            dqkv_weight.astype(jnp.bfloat16), "dp", scatter_dimension=1, tiled=True
        ).astype(jnp.float32),
        lax.psum_scatter(
            dout_weight.astype(jnp.bfloat16), "dp", scatter_dimension=1, tiled=True
        ).astype(jnp.float32),
        lax.psum_scatter(
            dff1_weight.astype(jnp.bfloat16), "dp", scatter_dimension=0, tiled=True
        ).astype(jnp.float32),
        lax.psum_scatter(
            dff2_weight.astype(jnp.bfloat16), "dp", scatter_dimension=1, tiled=True
        ).astype(jnp.float32),
    )
    qv_placed = lax.dynamic_update_slice_in_dim(
        jnp.zeros((2, cols * lax.axis_size("mp")), jnp.float32), dqv_bias, group * cols, 1
    )
    ff1_placed = lax.dynamic_update_slice_in_dim(
        jnp.zeros((ff_cols * lax.axis_size("mp"),), jnp.float32), dff1_bias, group * ff_cols, 0
    )
    small = lax.psum(
        (qv_placed, dout_bias, dgain_one, dshift_one, ff1_placed, dff2_bias, dgain_two, dshift_two),
        ("dp", "mp"),
    )
    return (
        out_rows,
        input_grad,
        qkv_share,
        small[0],
        out_share,
        small[1],
        small[2],
        small[3],
        ff1_share,
        small[4],
        ff2_share,
        small[5],
        small[6],
        small[7],
    )


BF = jnp.bfloat16
F32 = jnp.float32
ROOT_HALF = 2**-0.5
ROOT_TAU = 0.3989422804014327


def dg(left, right, left_dim, right_dim):
    return lax.dot_general(
        left, right, (((left_dim,), (right_dim,)), ((), ())), preferred_element_type=F32
    )


def whole(*shape):
    return pl.BlockSpec(shape, lambda *at: (0,) * len(shape), pipeline_mode=pl.Buffered(1))


def shaped(shape, dtype):
    return jax.ShapeDtypeStruct(shape, dtype)


def far_shaped(shape, dtype):
    return pltpu.HBM(shape, dtype)


TIMES = {
    "attn_fwd": 5,
    "pick": 2,
    "collect": 1,
    "attn_join": 5,
    "ffn_own": 3,
    "ffn_far": 5,
    "norm_two": 5,
    "grad_send": 3,
    "keep_ffn": 6,
    "ffn_back": 24,
    "second": 1000,
    "third": 1,
    "attn_back_other": 20,
    "fourth": 1,
    "keep_far": 5,
    "attn_back_own": 9,
    "second_attn": 1000,
    "keep_own": 2,
    "join_attn": 2,
    "last_attn": 1,
    "share_attn": 1,
}


def call(body, name, grid, ins, outs, args, scalars=(), scratch=(), aliases=None, flops=0, room=20, stay=()):
    args = [
        pltpu.with_memory_space_constraint(a, pltpu.HBM) if i in stay else a
        for i, a in enumerate(args)
    ]
    return pl.pallas_call(
        body,
        out_shape=[s for s, _ in outs],
        grid_spec=pltpu.PrefetchScalarGridSpec(
            num_scalar_prefetch=len(scalars),
            grid=grid,
            in_specs=ins,
            out_specs=[s for _, s in outs],
            scratch_shapes=list(scratch),
        ),
        input_output_aliases=aliases or {},
        cost_estimate=pl.CostEstimate(
            flops=TIMES[name] * 10**9, bytes_accessed=0, transcendentals=0
        ),
        name=name,
        compiler_params=pltpu.CompilerParams(vmem_limit_bytes=room * 2**20),
    )(*scalars, *args)


def permute_columns(source, target, me, rows):
    low = me & 1
    high = me >> 1
    size = min(rows, 128)
    lane = lax.broadcasted_iota(jnp.int32, (size, 128), 1)
    half = target.shape[1] // 2

    @pl.loop(0, rows // size)
    def _(i):
        at = pl.ds(pl.multiple_of(i * size, size), size)
        for u in range(4):
            blocks = []
            for z in range(2):
                rel = z * 4 + (u & 1) * 2 + (u >> 1)
                start = pl.multiple_of((rel ^ high) * 128, 128)
                blocks.append(source[at, pl.ds(start, 128)])
            turned = [pltpu.roll(block, 64, 1) for block in blocks]
            near = jnp.where(lane < 64, blocks[0], turned[1])
            far = jnp.where(lane < 64, turned[0], blocks[1])
            first = jnp.where(low == 0, near, far)
            second = jnp.where(low == 0, far, near)
            target[at, u * 128 : (u + 1) * 128] = first.astype(BF)
            target[at, half + u * 128 : half + (u + 1) * 128] = second.astype(BF)


def attn_fwd_body(s_ref, len_ref, x_ref, w_ref, b_ref, *outs, keep_rows, skip):
    q_ref, k_ref, v_ref = outs[-3:]
    ctx_ref, lse_ref = outs[skip : skip + 2]
    count = len_ref[s_ref[0]]
    x = x_ref[...]
    seq = x.shape[0]
    query = (dg(x, w_ref[0], 1, 0) + b_ref[0:1, :].astype(F32)).astype(BF)
    k_ref[...] = dg(x, w_ref[1], 1, 0).astype(BF)
    v_ref[...] = (dg(x, w_ref[2], 1, 0) + b_ref[1:2, :].astype(F32)).astype(BF)
    if keep_rows:
        outs[skip + 2][0] = query
        outs[skip + 2][1] = k_ref[...]
        outs[skip + 2][2] = v_ref[...]
    q_ref[...] = query * BF(HD**-0.5)
    first = lax.broadcasted_iota(jnp.int32, (seq, 2 * HD), 1) < HD
    valid = lax.broadcasted_iota(jnp.int32, (seq, seq), 0) < count

    for pair in range(query.shape[1] // (2 * HD)):
        cut = slice(pair * 2 * HD, (pair + 1) * 2 * HD)
        q_pair, k_pair = q_ref[:, cut], k_ref[:, cut]
        turned = v_ref[:, cut].T
        parts = []
        for h in range(2):
            own = jnp.where(first if h == 0 else ~first, q_pair, BF(0))
            scores = jnp.where(valid, dg(k_pair, own, 1, 1), NEGATIVE)
            top = jnp.max(scores, axis=0, keepdims=True)
            expo = jnp.exp(scores - top)
            total = jnp.sum(expo, axis=0, keepdims=True)
            part = dg(turned[h * HD : (h + 1) * HD], expo.astype(BF), 1, 0)
            parts.append(part * (1.0 / total))
            lse_ref[0, pair * 2 + h : pair * 2 + h + 1, :] = top + jnp.log(total)
        ctx_ref[:, cut] = jnp.concatenate(parts, axis=0).T.astype(BF)


def attn_fwd(page, lengths, tokens, weight, bias, keep_rows, tiles, before=()):
    depth = tokens.shape[1]
    seq = tokens.shape[0] // lengths.shape[0]
    cols = weight.shape[2]
    tile = 256
    heads = tile // HD
    start, stop = tiles
    outs = [
        (shaped((seq, cols), BF), pl.BlockSpec((seq, tile), lambda j, s, n: (0, start + j))),
        (
            shaped((cols // tile, heads, seq), F32),
            pl.BlockSpec((1, heads, seq), lambda j, s, n: (start + j, 0, 0)),
        ),
    ]
    if keep_rows:
        outs.append(
            (
                far_shaped((3, seq, cols), BF),
                pl.BlockSpec((3, seq, tile), lambda j, s, n: (0, 0, start + j)),
            )
        )
    return call(
        functools.partial(attn_fwd_body, keep_rows=keep_rows, skip=len(before)),
        "attn_fwd",
        (stop - start,),
        [
            pl.BlockSpec((seq, depth), lambda j, s, n: (s[0], 0)),
            pl.BlockSpec((3, depth, tile), lambda j, s, n: (0, 0, start + j)),
            pl.BlockSpec((2, tile), lambda j, s, n: (0, start + j)),
            *[pl.BlockSpec(memory_space=pl.ANY)] * len(before),
        ],
        outs,
        (tokens, weight, bias, *before),
        (page.reshape(1), lengths),
        [pltpu.VMEM((seq, tile), BF)] * 3,
        stay=(1,),
        aliases={5 + i: i for i in range(len(before))},
    )


def join_body(s_ref, x_ref, own_ref, oth_ref, w_ref, near_ref, core_ref, *refs):
    bias_ref, gain_ref, shift_ref = refs[:3]
    far_ref, normed_ref, scale_ref, low_ref, perm_ref, wide = refs[3:]
    me = s_ref[1]

    @pl.when(pl.program_id(0) == 0)
    def _():
        size = near_ref.shape[0]
        for flip, piece in ((0, near_ref), (1, core_ref)):
            at = pl.multiple_of(((me & 1) ^ flip) * size, 16)
            far_ref[pl.ds(at, size), :] = piece[...]

    attn = dg(own_ref[...], w_ref[...], 1, 0) + dg(oth_ref[...], far_ref[...], 1, 0)
    total = x_ref[...].astype(F32) + attn + bias_ref[...].astype(F32)
    center = total - jnp.mean(total, axis=-1, keepdims=True)
    scale = lax.rsqrt(jnp.mean(center * center, axis=-1, keepdims=True) + EPSILON)
    normed = center * scale
    normed_ref[...] = normed
    scale_ref[...] = scale
    hidden = normed * gain_ref[...].astype(F32) + shift_ref[...].astype(F32)
    low_ref[...] = hidden.astype(BF)
    wide[...] = hidden
    permute_columns(wide, perm_ref, me, wide.shape[0])


def join(scalars, tokens, own, other, weight, near, core, bias, gain, shift):
    seq, cols = own.shape
    depth = tokens.shape[1]
    steps = 2
    rows = seq // steps
    row = pl.BlockSpec((rows, depth), lambda i, s: (i, 0))
    half = pl.BlockSpec((rows, cols), lambda i, s: (i, 0))
    return call(
        join_body,
        "attn_join",
        (steps,),
        [
            pl.BlockSpec((rows, depth), lambda i, s: (s[0] * steps + i, 0)),
            half,
            half,
            whole(cols, depth),
            whole(*near.shape),
            whole(*near.shape),
            *[whole(1, depth)] * 3,
        ],
        [
            (far_shaped((cols, depth), BF), whole(cols, depth)),
            (far_shaped((seq, depth), F32), row),
            (shaped((seq, 1), F32), pl.BlockSpec((rows, 1), lambda i, s: (i, 0))),
            (shaped((seq, depth), BF), row),
            (far_shaped((seq, depth), BF), row),
        ],
        (
            tokens,
            own,
            other,
            weight,
            near,
            core,
            bias,
            gain,
            shift,
        ),
        (scalars,),
        [pltpu.VMEM((rows, depth), F32)],
        flops=4 * seq * cols * depth,
    )


def ffn_tile(h_ref, w_one, bias, w_two, act_ref, slope_ref):
    pre = dg(h_ref[...], w_one, 1, 0) + bias
    phi = 0.5 + 0.5 * lax.erf(pre * F32(ROOT_HALF))
    act = (pre * phi).astype(BF)
    act_ref[0] = act
    slope_ref[0] = (phi + pre * (jnp.exp(-0.5 * pre * pre) * F32(ROOT_TAU))).astype(BF)
    return dg(act, w_two, 1, 0)


TILE = 512


def start_sum(sum_ref, in_ref):
    @pl.when(pl.program_id(0) == 0)
    def _():
        sum_ref[...] = jnp.zeros_like(sum_ref) if in_ref is None else in_ref[...]


def ffn_own_body(h_ref, w1_ref, b_ref, w2_ref, *refs):
    act_ref, slope_ref, sum_ref = refs[-3:]
    start_sum(sum_ref, refs[0] if len(refs) > 3 else None)
    bias = b_ref[...].astype(F32)
    sum_ref[...] += ffn_tile(h_ref, w1_ref[...], bias, w2_ref[...], act_ref, slope_ref)


def ffn_own(hidden, w_one, bias, w_two, g, before):
    seq, depth = hidden.shape
    units = w_one.shape[1] // 2
    steps = units // TILE
    base = g * steps
    side = pl.BlockSpec((1, seq, TILE), lambda j: (g, 0, j))
    full = whole(seq, depth)
    hbm = pl.BlockSpec(memory_space=pl.ANY)
    return call(
        ffn_own_body,
        "ffn_own",
        (steps,),
        [
            full,
            pl.BlockSpec((depth, TILE), lambda j: (0, base + j)),
            pl.BlockSpec((1, TILE), lambda j: (0, base + j)),
            pl.BlockSpec((TILE, depth), lambda j: (base + j, 0)),
        ]
        + ([full, hbm, hbm] if before else []),
        [
            (shaped((4, seq, units), BF), side),
            (far_shaped((4, seq, units), BF), side),
            (shaped((seq, depth), F32), full),
        ],
        (hidden, w_one, bias, w_two) + before,
        aliases={4: 2, 5: 0, 6: 1} if before else None,
        stay=(1, 3),
    )


def pick_body(s_ref, one_ref, two_ref, more_ref, *refs):
    ffn_ref, out_ref = refs[-2:]
    size = one_ref.shape[0]
    ffn_ref[:size] = one_ref[...]
    ffn_ref[size : 2 * size] = two_ref[...]
    out_ref[...] = more_ref[...]
    if len(refs) > 2:
        low_ref, qv_ref = refs[:2]
        depth = ffn_ref.shape[1]
        lines = [low_ref[:, i * depth : (i + 1) * depth] for i in range(2)]
        lines.append(jnp.concatenate([qv_ref[i : i + 1] for i in range(2)], axis=1))
        lines.append(jnp.zeros((16 - len(lines), depth), BF))
        ffn_ref[2 * size :] = jnp.concatenate(lines, axis=0)


def pick(scalars, ff1_weight, ff2_weight, more, g, biases=()):
    depth, units = ff1_weight.shape[0], ff1_weight.shape[1] // 2
    size = depth // 8
    if more.ndim == 2:
        shape = (more.shape[0] // 2, more.shape[1])
        spec = pl.BlockSpec(shape, lambda i, s: (s[1] & 1, 0))
    else:
        shape = (more.shape[0], more.shape[1] // 8, more.shape[2])
        spec = pl.BlockSpec(shape, lambda i, s: (0, s[1] & 7, 0))
    rows = 2 * size + (16 if biases else 0)
    return call(
        pick_body,
        "pick",
        (1,),
        [
            pl.BlockSpec((size, units), lambda i, s: (s[1] & 7, g)),
            pl.BlockSpec((units // 8, depth), lambda i, s: (g * 8 + (s[1] & 7), 0)),
            spec,
            *[whole(*bias.shape) for bias in biases],
        ],
        [
            (shaped((rows, units), BF), whole(rows, units)),
            (shaped(shape, BF), whole(*shape)),
        ],
        (ff1_weight, ff2_weight, more, *biases),
        (scalars,),
        stay=(0, 1, 2),
    )


def collect_body(*refs):
    for i, piece in enumerate(refs[:-1]):
        refs[-1][i] = piece[...]


def collect(pieces):
    shape = pieces[0].shape
    return call(
        collect_body,
        "collect",
        (1,),
        [whole(*shape)] * len(pieces),
        [(shaped((len(pieces),) + shape, BF), whole(len(pieces), *shape))],
        tuple(pieces),
    )[0]


def ffn_far_body(
    s_ref, h_ref, b_ref, near_ref, core_ref, near2_ref, core2_ref, in_ref, *refs, rels, row
):
    act_ref, slope_ref, sum_ref, w1_ref, w2_ref = refs[-5:]
    j = pl.program_id(0)
    me = s_ref[1]

    def put(target, near, core):
        size = near.shape[1]
        for i, rel in enumerate(rels):
            for flip, stack in ((0, near), (1, core)):
                at = pl.multiple_of(((me & 7) ^ rel ^ flip) * size, 16)
                target[pl.ds(at, size), :] = stack[i]

    @pl.when(j == 0)
    def _():
        put(w2_ref, near2_ref, core2_ref)

    put(w1_ref, near_ref, core_ref)
    w_two = w2_ref[pl.ds(pl.multiple_of(j * TILE, TILE), TILE), :]
    start_sum(sum_ref, in_ref)
    bias = b_ref[row : row + 1, :].astype(F32)
    sum_ref[...] += ffn_tile(h_ref, w1_ref[...], bias, w_two, act_ref, slope_ref)


def ffn_far(scalars, hidden, bias, near, core, rels, g, before):
    seq, depth = hidden.shape
    units = before[1].shape[2]
    steps = units // TILE
    size = depth // 8
    side = pl.BlockSpec((1, seq, TILE), lambda j, s: (2 + g, 0, j))
    full = whole(seq, depth)
    hbm = pl.BlockSpec(memory_space=pl.ANY)
    one = pl.BlockSpec((4, size, TILE), lambda j, s: (0, 0, j))
    two = pl.BlockSpec(
        (4, size, depth), lambda j, s: (0, 1, 0), pipeline_mode=pl.Buffered(1)
    )
    args = (hidden, bias, near, core, near, core, *before)
    return call(
        functools.partial(ffn_far_body, rels=rels, row=g),
        "ffn_far",
        (steps,),
        [
            full,
            pl.BlockSpec((16, TILE), lambda j, s: (bias.shape[0] // 16 - 1, j)),
            one,
            one,
            two,
            two,
            full,
            *[hbm] * (len(before) - 1),
        ],
        [
            (shaped((4, seq, units), BF), side),
            (far_shaped((4, seq, units), BF), side),
            (shaped((seq, depth), F32), full),
            (
                far_shaped((depth, 2 * units), BF),
                pl.BlockSpec((depth, TILE), lambda j, s: (0, g * steps + j)),
            ),
            (
                far_shaped((2 * units, depth), BF),
                pl.BlockSpec((units, depth), lambda j, s: (g, 0), pipeline_mode=pl.Buffered(1)),
            ),
        ],
        args,
        (scalars,),
        aliases={7: 2, 8: 0, 9: 1} | ({10: 3, 11: 4} if g else {}),
        flops=4 * seq * depth * units,
    )


def norm_back(grad, normed, scale):
    return scale * (
        grad
        - jnp.mean(grad, axis=-1, keepdims=True)
        - normed * jnp.mean(grad * normed, axis=-1, keepdims=True)
    )


CHUNK = 64


def chunked(rows, sums_ref, chunk):
    zero = jnp.zeros((1, sums_ref.shape[1]), F32)

    def step(i, sums):
        news = chunk(pl.ds(pl.multiple_of(i * CHUNK, CHUNK), CHUNK))
        return tuple(
            old + jnp.sum(new, axis=0, keepdims=True) for old, new in zip(sums, news)
        )

    sums = lax.fori_loop(0, rows // CHUNK, step, (zero, zero, zero), unroll=True)
    first = pl.program_id(0) == 0
    for i in range(3):
        old = sums_ref[i : i + 1, :]
        sums_ref[i : i + 1, :] = jnp.where(first, 0.0, old) + sums[i]


def norm_two_body(
    s_ref, in_ref, normed_ref, cot_ref, *refs
):
    gain_one, shift_one, bias, gain, shift = [ref[...].astype(F32) for ref in refs[:5]]
    out_ref, ds_ref, df_ref, perm_ref, sums_ref = refs[5:]

    def chunk(at):
        total = normed_ref[at, :] * gain_one + shift_one + in_ref[at, :] + bias
        center = total - jnp.mean(total, axis=-1, keepdims=True)
        scale = lax.rsqrt(jnp.mean(center * center, axis=-1, keepdims=True) + EPSILON)
        normed = center * scale
        out_ref[at, :] = (normed * gain + shift).astype(BF)
        cot = cot_ref[at, :].astype(F32)
        ds = norm_back(cot * gain, normed, scale)
        ds_ref[at, :] = ds
        df_ref[at, :] = ds.astype(BF)
        return ds, cot * normed, cot

    rows = in_ref.shape[0]
    chunked(rows, sums_ref, chunk)
    permute_columns(ds_ref, perm_ref, s_ref[1], rows)


def norm_two(scalars, total, normed, cotangent, vectors):
    seq, depth = total.shape
    steps = 4
    row = pl.BlockSpec((seq // steps, depth), lambda i, s: (i, 0))
    return call(
        norm_two_body,
        "norm_two",
        (steps,),
        [
            row,
            row,
            pl.BlockSpec((seq // steps, depth), lambda i, s: (s[0] * steps + i, 0)),
            *[whole(1, depth)] * 5,
        ],
        [
            (far_shaped((seq, depth), BF), row),
            (shaped((seq, depth), F32), row),
            (shaped((seq, depth), BF), row),
            (shaped((seq, depth), BF), row),
            (shaped((8, depth), F32), pl.BlockSpec((8, depth), lambda i, s: (0, 0))),
        ],
        (total, normed, cotangent, *vectors),
        (scalars,),
        stay=(1, 2),
        flops=40 * seq * depth,
    )


def send_order(i):
    return (i % 2) * 2 + i // 2


def ffn_back_body(
    s_ref,
    df_ref,
    w2_ref,
    w2_far_ref,
    slope_ref,
    w1_ref,
    w1_far_ref,
    ds_ref,
    normed_ref,
    scale_ref,
    gain_ref,
    turned_ref,
    *refs,
    tiles,
):
    pieces = refs[:4]
    dpre_ref, db_ref, first_ref, low_ref, perm_ref, sums_ref = refs[4:10]
    send_a_ref, send_b_ref, near_ref, wide = refs[10:]
    j = pl.program_id(0)
    per = dpre_ref.shape[2] // TILE

    @pl.when(j == 1)
    def _():
        for i, piece in enumerate(pieces):
            near_ref[i] = piece[...]

    @pl.when(j == 0)
    def _():
        wide[...] = ds_ref[...]

    def tile(w_two, w_one):
        dact = dg(df_ref[...], w_two[...], 1, 1)
        dpre = (dact * slope_ref[0].astype(F32)).astype(BF)
        dpre_ref[j // per, :, pl.ds(pl.multiple_of((j % per) * TILE, TILE), TILE)] = dpre
        db_ref[...] = jnp.sum(dpre.astype(F32), axis=0, keepdims=True)
        wide[...] += dg(dpre, w_one[...], 1, 1)

    pl.when(j < tiles // 2)(functools.partial(tile, w2_ref, w1_ref))
    pl.when((j >= tiles // 2) & (j < tiles))(functools.partial(tile, w2_far_ref, w1_far_ref))

    @pl.when(j == tiles - 1)
    def _():
        gain = gain_ref[...].astype(F32)
        zero = jnp.zeros((1, gain.shape[1]), F32)

        def step(i, sums):
            at = pl.ds(pl.multiple_of(i * CHUNK, CHUNK), CHUNK)
            grad = wide[at, :]
            normed = normed_ref[at, :]
            first = norm_back(grad * gain, normed, scale_ref[at, :])
            first_ref[at, :] = first
            low_ref[at, :] = first.astype(BF)
            return tuple(
                old + jnp.sum(new, axis=0, keepdims=True)
                for old, new in zip(sums, (first, grad * normed, grad))
            )

        rows = wide.shape[0]
        sums = lax.fori_loop(0, rows // CHUNK, step, (zero, zero, zero), unroll=2)
        for i in range(3):
            sums_ref[i : i + 1, :] = sums[i]
        permute_columns(first_ref, perm_ref, s_ref[1], rows)

    @pl.when(j >= tiles)
    def _():
        part = dg(turned_ref[...], dpre_ref[send_order(j - tiles)], 0, 0).astype(BF)

        @pl.when(j < tiles + 2)
        def _():
            send_a_ref[0] = part

        @pl.when(j >= tiles + 2)
        def _():
            send_b_ref[0] = part


def ffn_back(
    scalars,
    dffn,
    w_two,
    w_two_far,
    slope,
    w_one,
    w_one_far,
    dsecond,
    normed,
    scale,
    gain,
    turned,
    pieces,
):
    seq, depth = dffn.shape
    units = slope.shape[2]
    steps = units // TILE
    half = 2 * steps
    tiles = 2 * half
    full = whole(seq, depth)

    def near(j):
        return jnp.minimum(j, half - 1)

    def far(j):
        return jnp.clip(j - half, 0, half - 1)

    def last(j):
        return jnp.minimum(j, tiles - 1)

    def send(first):
        return pl.BlockSpec(
            (1, depth // 2, units), lambda j, s: (jnp.clip(j - first, 0, 1), 0, 0)
        )

    return call(
        functools.partial(ffn_back_body, tiles=tiles),
        "ffn_back",
        (tiles + 4,),
        [
            full,
            pl.BlockSpec((TILE, depth), lambda j, s: (near(j), 0)),
            pl.BlockSpec((TILE, depth), lambda j, s: (far(j), 0)),
            pl.BlockSpec((1, seq, TILE), lambda j, s: (last(j) // steps, 0, last(j) % steps)),
            pl.BlockSpec((depth, TILE), lambda j, s: (0, near(j))),
            pl.BlockSpec((depth, TILE), lambda j, s: (0, far(j))),
            full,
            full,
            whole(seq, 1),
            whole(1, depth),
            pl.BlockSpec((seq, depth // 2), lambda j, s: (0, 1), pipeline_mode=pl.Buffered(1)),
            *[whole(*pieces[0].shape)] * 4,
        ],
        [
            (shaped((4, seq, units), BF), whole(4, seq, units)),
            (shaped((1, 4 * units), F32), pl.BlockSpec((1, TILE), lambda j, s: (0, last(j)))),
            (far_shaped((seq, depth), F32), full),
            (shaped((seq, depth), BF), full),
            (shaped((seq, depth), BF), full),
            (shaped((8, depth), F32), whole(8, depth)),
            (shaped((2, depth // 2, units), BF), send(tiles)),
            (shaped((2, depth // 2, units), BF), send(tiles + 2)),
            (shaped((4,) + pieces[0].shape, BF), whole(4, *pieces[0].shape)),
        ],
        (
            dffn,
            w_two,
            w_two_far,
            slope,
            w_one,
            w_one_far,
            dsecond,
            normed,
            scale,
            gain,
            turned,
            *pieces,
        ),
        (scalars,),
        [pltpu.VMEM((seq, depth), F32)],
        room=36,
        stay=(1, 2, 3, 4, 5, 7, 10),
    )


def attn_back_tile(j, count, refs, lse_ref, dc_ref, out_ref, dqkv_ref, db_ref):
    q_ref, k_ref, v_ref = refs
    seq, size = q_ref.shape
    first = lax.broadcasted_iota(jnp.int32, (seq, 2 * HD), 1) < HD
    valid = lax.broadcasted_iota(jnp.int32, (seq, seq), 0) < count

    @pl.loop(0, size // (2 * HD))
    def _(pair):
        cut = pl.ds(pl.multiple_of(pair * 2 * HD, 2 * HD), 2 * HD)
        q_pair, k_pair, v_pair, dc_pair = q_ref[:, cut], k_ref[:, cut], v_ref[:, cut], dc_ref[:, cut]
        dquery = dkeys = dvalues = 0.0
        for h in range(2):
            mask = first if h == 0 else ~first
            q_own = jnp.where(mask, q_pair, BF(0))
            k_own = jnp.where(mask, k_pair, BF(0))
            dc_own = jnp.where(mask, dc_pair, BF(0))
            scores = dg(k_pair, q_own, 1, 1) - lse_ref[0, pl.ds(pair * 2 + h, 1), :]
            probs = jnp.exp(jnp.where(valid, scores, NEGATIVE))
            dprobs = dg(v_pair, dc_own, 1, 1)
            delta = jnp.sum(probs * dprobs, axis=0, keepdims=True)
            dscores = (probs * (dprobs - delta)).astype(BF)
            dvalues = dvalues + dg(probs.astype(BF), dc_own, 1, 0)
            dkeys = dkeys + dg(dscores, q_own, 1, 0)
            dquery = dquery + dg(dscores, k_own, 0, 0)
        out_ref[0, :, cut] = (dquery * HD**-0.5).astype(BF)
        out_ref[1, :, cut] = dkeys.astype(BF)
        out_ref[2, :, cut] = dvalues.astype(BF)

    for t in range(3):
        dqkv_ref[t, :, pl.ds(pl.multiple_of(j * size, size), size)] = out_ref[t]
    db_ref[0:1, :] = jnp.sum(out_ref[0].astype(F32), axis=0, keepdims=True)
    db_ref[1:2, :] = jnp.sum(out_ref[2].astype(F32), axis=0, keepdims=True)


def attn_back_other_body(
    s_ref,
    len_ref,
    x_ref,
    da_ref,
    wo_ref,
    lse_ref,
    qb_ref,
    vb_ref,
    near_ref,
    core_ref,
    own_ref,
    oth_ref,
    da_turned_ref,
    dqkv_ref,
    db_ref,
    sum_ref,
    turned_ref,
    far_send_ref,
    out_send_ref,
    w_ref,
    wide,
    q_ref,
    k_ref,
    v_ref,
    dc_ref,
    out_ref,
    *,
    rels,
    tiles,
):
    j = pl.program_id(0)
    me = s_ref[1]
    half = turned_ref.shape[1] // 2

    @pl.when(j < tiles)
    def _():
        size = near_ref.shape[2]
        for i, rel in enumerate(rels):
            for flip, stack in ((0, near_ref), (1, core_ref)):
                at = pl.multiple_of(((me & 7) ^ rel ^ flip) * size, 16)
                w_ref[:, pl.ds(at, size), :] = stack[i]
        x = x_ref[...]
        query = (dg(x, w_ref[0], 1, 0) + qb_ref[2:3, :].astype(F32)).astype(BF)
        q_ref[...] = query * BF(HD**-0.5)
        k_ref[...] = dg(x, w_ref[1], 1, 0).astype(BF)
        v_ref[...] = (dg(x, w_ref[2], 1, 0) + vb_ref[2:3, :].astype(F32)).astype(BF)
        dc_ref[...] = dg(da_ref[...], wo_ref[...], 1, 1).astype(BF)
        count = len_ref[s_ref[0]]
        refs = (q_ref, k_ref, v_ref)
        attn_back_tile(j, count, refs, lse_ref, dc_ref, out_ref, dqkv_ref, db_ref)
        start_sum(sum_ref, None)
        for t in range(3):
            sum_ref[...] += dg(out_ref[t], w_ref[t], 1, 1)

    @pl.when(j == 0)
    def _():
        wide[...] = x_ref[...].astype(F32)
        permute_columns(wide, turned_ref, me, x_ref.shape[0])

    @pl.when((j >= tiles) & (j < tiles + 3))
    def _():
        right = dqkv_ref[jnp.clip(j - tiles, 0, 2)]
        far_send_ref[0] = dg(turned_ref[:, half:], right, 0, 0).astype(BF)

    for side, ref in enumerate((own_ref, oth_ref)):

        @pl.when(j == tiles + 3 + side)
        def _():
            out_send_ref[0] = dg(da_turned_ref[...], ref[...], 0, 0).astype(BF)


def attn_back_other(
    scalars, lengths, tokens, dattn, out_w, logsum, bias, near, core, rels, own, other, da_turned
):
    seq, depth = dattn.shape
    cols = out_w.shape[0]
    tile = 256
    heads = tile // HD
    tiles = cols // tile
    half = depth // 2
    ahead = bias.shape[0] // 16 - 1

    def at(j):
        return jnp.minimum(j, tiles - 1)

    stack = pl.BlockSpec((4, 3, depth // 8, tile), lambda j, s, n: (0, 0, 0, at(j)))
    return call(
        functools.partial(attn_back_other_body, rels=rels, tiles=tiles),
        "attn_back_other",
        (tiles + 5,),
        [
            pl.BlockSpec((seq, depth), lambda j, s, n: (s[0], 0)),
            whole(seq, depth),
            pl.BlockSpec((tile, depth), lambda j, s, n: (at(j), 0)),
            pl.BlockSpec((1, heads, seq), lambda j, s, n: (at(j), 0, 0)),
            pl.BlockSpec((16, tile), lambda j, s, n: (ahead, at(j))),
            pl.BlockSpec((16, tile), lambda j, s, n: (ahead, tiles + at(j))),
            stack,
            stack,
            whole(seq, cols),
            whole(seq, cols),
            pl.BlockSpec((seq, half), lambda j, s, n: (0, 1), pipeline_mode=pl.Buffered(1)),
        ],
        [
            (shaped((3, seq, cols), BF), whole(3, seq, cols)),
            (shaped((2, cols), F32), pl.BlockSpec((2, tile), lambda j, s, n: (0, at(j)))),
            (far_shaped((seq, depth), F32), whole(seq, depth)),
            (shaped((seq, depth), BF), whole(seq, depth)),
            (
                shaped((3, half, cols), BF),
                pl.BlockSpec((1, half, cols), lambda j, s, n: (jnp.clip(j - tiles, 0, 2), 0, 0)),
            ),
            (
                shaped((2, half, cols), BF),
                pl.BlockSpec(
                    (1, half, cols), lambda j, s, n: (jnp.clip(j - tiles - 3, 0, 1), 0, 0)
                ),
            ),
        ],
        (tokens, dattn, out_w, logsum, bias, bias, near, core, own, other, da_turned),
        (scalars, lengths),
        [pltpu.VMEM((3, depth, tile), BF), pltpu.VMEM((seq, depth), F32)]
        + [pltpu.VMEM((seq, tile), BF)] * 4
        + [pltpu.VMEM((3, seq, tile), BF)],
        room=30,
        stay=(0, 2),
    )


def attn_back_own_body(
    s_ref, len_ref, da_ref, wo_ref, lse_ref, qkv_ref, w_ref, *refs, last
):
    (wide, db_ref, q_ref, dc_ref, out_ref) = refs[-5:]
    j = pl.program_id(0)
    if last:
        in_ref, turned_ref, early_ref, early_db_ref, ffn_db_ref, far_db_ref = refs[:6]
        one_ref, two_ref, dqkv_ref, small_ref, grad_ref, send_ref = refs[6:12]
    else:
        in_ref, first_ref, dqkv_ref, sum_ref, db_out_ref = refs[:5]

    @pl.when(j == 0)
    def _():
        dc_ref[...] = dg(da_ref[...], wo_ref[...], 1, 1).astype(BF)
        q_ref[...] = qkv_ref[0] * BF(HD**-0.5)
        tile = (q_ref, qkv_ref.at[1], qkv_ref.at[2])
        attn_back_tile(0, len_ref[s_ref[0]], tile, lse_ref, dc_ref, out_ref, dqkv_ref, db_ref)
        wide[...] = in_ref[...] if last else in_ref[...] + first_ref[...]
        for t in range(3):
            wide[...] += dg(out_ref[t], w_ref[t], 1, 1)
        if not last:
            sum_ref[...] = wide[...]
            db_out_ref[...] = db_ref[...]
            return
        grad_ref[...] = wide[...].astype(BF)
        side = s_ref[0]
        cols = far_db_ref.shape[1]
        depth = small_ref.shape[1]
        own = jnp.concatenate([early_db_ref[...], db_ref[...]], axis=1)
        small_ref[0:2, pl.ds(pl.multiple_of(side * cols, 128), cols)] = own
        small_ref[0:2, pl.ds(pl.multiple_of((1 - side) * cols, 128), cols)] = far_db_ref[...]
        lines = [ffn_db_ref[:, i * depth : (i + 1) * depth] for i in range(4)]
        small_ref[2:6] = jnp.where(
            side == 0,
            jnp.concatenate(lines, axis=0),
            jnp.concatenate(lines[2:] + lines[:2], axis=0),
        )
        small_ref[6:9] = one_ref[0:3]
        small_ref[9:12] = two_ref[0:3]
        small_ref[12:16] = jnp.zeros((4, depth), F32)

    if last:

        @pl.when(j > 0)
        def _():
            at = jnp.maximum(j - 1, 0)
            halves = [
                dg(turned_ref[...], ref[at], 0, 0).astype(BF) for ref in (early_ref, dqkv_ref)
            ]
            send_ref[0] = jnp.concatenate(halves, axis=1)


def attn_back_own(scalars, lengths, dattn, out_w, logsum, qkv, weight, *more, last):
    seq, depth = dattn.shape
    cols = out_w.shape[0]
    tile = cols // 2
    heads = tile // HD
    half = depth // 2
    at = int(last)
    full = whole(seq, depth)
    outs = [(shaped((3, seq, tile), BF), whole(3, seq, tile))]
    if last:
        turned = pl.BlockSpec(
            (seq, half), lambda j, s, n: (0, 1), pipeline_mode=pl.Buffered(1)
        )
        ins = [full, turned] + [whole(*arg.shape) for arg in more[2:]]
        outs += [
            (shaped((16, depth), F32), whole(16, depth)),
            (far_shaped((seq, depth), BF), full),
            (
                shaped((3, half, cols), BF),
                pl.BlockSpec((1, half, cols), lambda j, s, n: (jnp.maximum(j - 1, 0), 0, 0)),
            ),
        ]
    else:
        ins = [full, full]
        outs += [(shaped((seq, depth), F32), full), (shaped((2, tile), F32), whole(2, tile))]
    return call(
        functools.partial(attn_back_own_body, last=last),
        "attn_back_own",
        (4 if last else 1,),
        [
            full,
            pl.BlockSpec((tile, depth), lambda j, s, n: (at, 0), pipeline_mode=pl.Buffered(1)),
            pl.BlockSpec(
                (1, heads, seq), lambda j, s, n: (at, 0, 0), pipeline_mode=pl.Buffered(1)
            ),
            pl.BlockSpec(
                (3, seq, tile), lambda j, s, n: (0, 0, at), pipeline_mode=pl.Buffered(1)
            ),
            pl.BlockSpec(
                (3, depth, tile), lambda j, s, n: (0, 0, at), pipeline_mode=pl.Buffered(1)
            ),
        ]
        + ins,
        outs,
        (dattn, out_w, logsum, qkv, weight) + more,
        (scalars, lengths),
        [
            pltpu.VMEM((seq, depth), F32),
            pltpu.VMEM((2, tile), F32),
            pltpu.VMEM((seq, tile), BF),
            pltpu.VMEM((seq, tile), BF),
            pltpu.VMEM((3, seq, tile), BF),
        ],
        room=24,
    )


def grad_send_body(a_ref, b_ref, out_ref):
    out_ref[0] = dg(a_ref[...], b_ref[0], 0, 0).astype(BF)


def grad_specs(turned, right, picks, part):
    seq, units = right.shape[1:]
    half = turned.shape[1] // 2
    start, stride = picks[0], (picks[1] - picks[0] if len(picks) > 1 else 1)
    return [
        pl.BlockSpec((seq, half), lambda i: (0, part), pipeline_mode=pl.Buffered(1)),
        pl.BlockSpec((1, seq, units), lambda i: (start + stride * i, 0, 0)),
    ], pl.BlockSpec((1, half, units), lambda i: (i, 0, 0))


def grad_send(turned, right, picks):
    seq, units = right.shape[1:]
    half = turned.shape[1] // 2
    count = len(picks)
    ins, out = grad_specs(turned, right, picks, 1)
    return call(
        grad_send_body,
        "grad_send",
        (count,),
        ins,
        [(shaped((count, half, units), BF), out)],
        (turned, right),
        flops=2 * count * seq * half * units,
    )[0]


def keep_ffn_body(a_ref, b_ref, ra_ref, rb_ref, keep_ref, send_ref, own_ref, far_ref):
    i = pl.program_id(0)
    part = dg(a_ref[...], b_ref[0], 0, 0)
    cut = keep_ref.shape[1]

    @pl.when(i < 2)
    def _():
        total = (part + ra_ref[0].astype(F32)).astype(BF)
        keep_ref[0] = total[:cut]
        send_ref[0] = total[cut:]

    @pl.when(i >= 2)
    def _():
        total = (part + rb_ref[0].astype(F32)).astype(BF)

        @pl.when(i == 2)
        def _():
            own_ref[...] = total

        @pl.when(i == 3)
        def _():
            far_ref[...] = total


def keep_ffn(turned, right, got_a, got_b):
    _, seq, units = right.shape
    half = turned.shape[1] // 2
    cut = pl.BlockSpec((1, half // 2, units), lambda i: (jnp.minimum(i, 1), 0, 0))
    return call(
        keep_ffn_body,
        "keep_ffn",
        (4,),
        [
            pl.BlockSpec((seq, half), lambda i: (0, 0), pipeline_mode=pl.Buffered(1)),
            pl.BlockSpec((1, seq, units), lambda i: (send_order(i), 0, 0)),
            pl.BlockSpec((1, half, units), lambda i: (jnp.minimum(i, 1), 0, 0)),
            pl.BlockSpec((1, half, units), lambda i: (jnp.maximum(i - 2, 0), 0, 0)),
        ],
        [
            (far_shaped((2, half // 2, units), BF), cut),
            (shaped((2, half // 2, units), BF), cut),
            (far_shaped((half, units), BF), whole(half, units)),
            (shaped((half, units), BF), whole(half, units)),
        ],
        (turned, right, got_a, got_b),
        room=24,
    )


def total(*refs):
    return sum(ref.astype(F32) for ref in refs).astype(BF)


def second_body(ka_ref, ga_ref, bo_ref, gb_ref, a_own_ref, a_far_ref, b_own_ref, b_send_ref):
    a_own_ref[...] = total(ka_ref[0], ga_ref[0])
    a_far_ref[...] = total(ka_ref[1], ga_ref[1])
    half = b_own_ref.shape[0]
    b_own_ref[...] = total(bo_ref[:half], gb_ref[:half])
    b_send_ref[...] = total(bo_ref[half:], gb_ref[half:])


def second(keep_a, got_a, b_own, got_b):
    _, rows, units = keep_a.shape
    part = (shaped((rows, units), BF), whole(rows, units))
    return call(
        second_body,
        "second",
        (1,),
        [whole(2, rows, units)] * 2 + [whole(2 * rows, units)] * 2,
        [part] * 4,
        (keep_a, got_a, b_own, got_b),
        stay=(0, 2),
    )


def third_body(a_ref, ga_ref, b_ref, gb_ref, keep_ref, send_ref):
    half, units = keep_ref.shape[0], a_ref.shape[1]
    for at, (left, right) in enumerate(((a_ref, ga_ref), (b_ref, gb_ref))):
        cut = slice(at * units, (at + 1) * units)
        keep_ref[:, cut] = total(left[:half], right[:half])
        send_ref[:, cut] = total(left[half:], right[half:])


def third(a_own, got_a, b_own, got_b):
    rows, units = a_own.shape
    part = (shaped((rows // 2, 2 * units), BF), whole(rows // 2, 2 * units))
    return call(
        third_body,
        "third",
        (1,),
        [whole(rows, units)] * 4,
        [part] * 2,
        (a_own, got_a, b_own, got_b),
    )


def fourth_body(a_ref, g_ref, keep_ref, send_ref):
    half = keep_ref.shape[-2]
    keep_ref[...] = total(a_ref[..., :half, :], g_ref[..., :half, :])
    send_ref[...] = total(a_ref[..., half:, :], g_ref[..., half:, :])


def fourth(values, got):
    shape = values.shape
    out = shape[:-2] + (shape[-2] // 2, shape[-1])
    return call(
        fourth_body,
        "fourth",
        (1,),
        [whole(*shape)] * 2,
        [(shaped(out, BF), whole(*out))] * 2,
        (values, got),
    )


def keep_far_body(
    da_ref, a_ref, own_ref, oth_ref, b_ref, ro_ref, rf_ref, keep_ref, send_ref, far_ref
):
    i = pl.program_id(0)
    cut = keep_ref.shape[1]

    def split(value):
        keep_ref[0] = value[:cut]
        send_ref[0] = value[cut:]

    for side, ref in enumerate((own_ref, oth_ref)):

        @pl.when(i == side)
        def _():
            split((dg(da_ref[...], ref[...], 0, 0) + ro_ref[0].astype(F32)).astype(BF))

    @pl.when(i >= 2)
    def _():
        value = (dg(a_ref[...], b_ref[0], 0, 0) + rf_ref[0].astype(F32)).astype(BF)

        @pl.when(i == 2)
        def _():
            split(value)

        @pl.when(i > 2)
        def _():
            far_ref[0] = value


def keep_far(da_turned, turned, own, other, dqkv, got_out, got_far):
    _, seq, cols = dqkv.shape
    half = turned.shape[1] // 2
    left = pl.BlockSpec((seq, half), lambda i: (0, 0), pipeline_mode=pl.Buffered(1))
    cut = pl.BlockSpec((1, half // 2, cols), lambda i: (jnp.minimum(i, 2), 0, 0))
    return call(
        keep_far_body,
        "keep_far",
        (5,),
        [
            left,
            left,
            whole(seq, cols),
            whole(seq, cols),
            pl.BlockSpec((1, seq, cols), lambda i: (jnp.maximum(i - 2, 0), 0, 0)),
            pl.BlockSpec((1, half, cols), lambda i: (jnp.minimum(i, 1), 0, 0)),
            pl.BlockSpec((1, half, cols), lambda i: (jnp.maximum(i - 2, 0), 0, 0)),
        ],
        [
            (shaped((3, half // 2, cols), BF), cut),
            (shaped((3, half // 2, cols), BF), cut),
            (
                shaped((2, half, cols), BF),
                pl.BlockSpec((1, half, cols), lambda i: (jnp.maximum(i - 3, 0), 0, 0)),
            ),
        ],
        (da_turned, turned, own, other, dqkv, got_out, got_far),
    )


def second_attn_body(k_ref, g_ref, out_ref, far_ref):
    out_ref[0] = total(k_ref[0], g_ref[0])
    far_ref[0] = total(k_ref[2], g_ref[2])
    far_ref[1] = total(k_ref[1], g_ref[1])


def second_attn(keep, got):
    _, rows, cols = keep.shape
    return call(
        second_attn_body,
        "second_attn",
        (1,),
        [whole(3, rows, cols)] * 2,
        [(shaped((n, rows, cols), BF), whole(n, rows, cols)) for n in (1, 2)],
        (keep, got),
    )


def keep_own_body(
    a_ref, b0_ref, b1_ref, r_ref, gb_ref, keep_ref, send_ref, z_keep_ref, z_send_ref
):
    i = pl.program_id(0)
    parts = [dg(a_ref[...], ref[0], 0, 0) for ref in (b0_ref, b1_ref)]
    value = jnp.concatenate(parts, axis=1) + r_ref[0].astype(F32)
    value = jnp.where(i == 0, value, value + gb_ref[0].astype(F32)).astype(BF)
    cut = keep_ref.shape[1]

    @pl.when(i < 2)
    def _():
        keep_ref[0] = value[:cut]
        send_ref[0] = value[cut:]

    @pl.when(i == 2)
    def _():
        half = cut // 2
        for x in range(2):
            z_keep_ref[x * half : (x + 1) * half] = value[x * cut : x * cut + half]
            z_send_ref[x * half : (x + 1) * half] = value[x * cut + half : (x + 1) * cut]


def keep_own(turned, early, late, got, got_b):
    _, seq, tile = early.shape
    cols = 2 * tile
    half = turned.shape[1] // 2
    part = (
        shaped((2, half // 2, cols), BF),
        pl.BlockSpec((1, half // 2, cols), lambda i: (jnp.minimum(i, 1), 0, 0)),
    )
    flat = (shaped((half // 2, cols), BF), whole(half // 2, cols))
    return call(
        keep_own_body,
        "keep_own",
        (3,),
        [
            pl.BlockSpec((seq, half), lambda i: (0, 0), pipeline_mode=pl.Buffered(1)),
            pl.BlockSpec((1, seq, tile), lambda i: (i, 0, 0)),
            pl.BlockSpec((1, seq, tile), lambda i: (i, 0, 0)),
            pl.BlockSpec((1, half, cols), lambda i: (i, 0, 0)),
            pl.BlockSpec((1, half, cols), lambda i: (jnp.maximum(i - 1, 0), 0, 0)),
        ],
        [part, part, flat, flat],
        (turned, early, late, got, got_b),
    )


def join_attn_body(
    k_ref, x_ref, o_ref, y_ref, v_ref, z_ref, keep_ref, send_ref, v_keep_ref, v_send_ref
):
    half = keep_ref.shape[1]
    for ref, cut in ((keep_ref, slice(0, half)), (send_ref, slice(half, 2 * half))):
        ref[0] = total(k_ref[0, cut], x_ref[0, cut], y_ref[0, cut])
        ref[1] = total(k_ref[1, cut], x_ref[1, cut])
        ref[2] = total(o_ref[0, cut], y_ref[1, cut])
    v_keep_ref[...] = total(v_ref[:half], z_ref[:half])
    v_send_ref[...] = total(v_ref[half:], z_ref[half:])


def join_attn(keep, got_x, out, got_y, value, got_z):
    _, rows, cols = keep.shape
    part = (shaped((3, rows // 2, cols), BF), whole(3, rows // 2, cols))
    flat = (shaped((rows // 2, cols), BF), whole(rows // 2, cols))
    return call(
        join_attn_body,
        "join_attn",
        (1,),
        [
            whole(2, rows, cols),
            whole(2, rows, cols),
            whole(1, rows, cols),
            whole(2, rows, cols),
            whole(rows, cols),
            whole(rows, cols),
        ],
        [part, part, flat, flat],
        (keep, got_x, out, got_y, value, got_z),
    )


def last_attn_body(k_ref, z_ref, v_ref, x_ref, keep_ref, send_ref):
    half = keep_ref.shape[1]
    for ref, cut in ((keep_ref, slice(0, half)), (send_ref, slice(half, 2 * half))):
        for i in range(3):
            ref[i] = total(k_ref[i, cut], z_ref[i, cut])
        ref[3] = total(v_ref[cut], x_ref[cut])


def last_attn(keep, got_z, value, got_x):
    _, rows, cols = keep.shape
    part = (shaped((4, rows // 2, cols), BF), whole(4, rows // 2, cols))
    return call(
        last_attn_body,
        "last_attn",
        (1,),
        [whole(3, rows, cols), whole(3, rows, cols), whole(rows, cols), whole(rows, cols)],
        [part, part],
        (keep, got_z, value, got_x),
    )


def share_attn_body(k_ref, g_ref, qkv_ref, out_ref):
    for at, i in ((0, 0), (1, 1), (2, 3)):
        qkv_ref[at] = k_ref[i].astype(F32) + g_ref[i].astype(F32)
    out_ref[...] = k_ref[2].astype(F32) + g_ref[2].astype(F32)


def share_attn(keep, got):
    _, rows, cols = keep.shape
    return call(
        share_attn_body,
        "share_attn",
        (1,),
        [whole(4, rows, cols)] * 2,
        [
            (far_shaped((3, rows, cols), F32), whole(3, rows, cols)),
            (far_shaped((rows, cols), F32), whole(rows, cols)),
        ],
        (keep, got),
    )


def swap(values, bit):
    count = lax.axis_size("dp")
    return lax.ppermute(values, "dp", [(i, i ^ (1 << bit)) for i in range(count)])


def swap_y(values):
    return lax.ppermute(values, "mp", [(0, 1), (1, 0)])


def add(left, right):
    return left.astype(F32) + right.astype(F32)


def low_add(left, right):
    return add(left, right).astype(BF)


def after(value, tick):
    flat, tree = jax.tree.flatten(value)
    arrays = [i for i, leaf in enumerate(flat) if not isinstance(leaf, int)]
    held = lax.optimization_barrier(([flat[i] for i in arrays], tick))[0]
    for i, leaf in zip(arrays, held):
        flat[i] = leaf
    return jax.tree.unflatten(tree, flat)


def paged(
    tokens,
    page_lengths,
    qkv_weight,
    qv_bias,
    out_weight,
    out_bias,
    ln1_gain,
    ln1_bias,
    ff1_weight,
    ff1_bias,
    ff2_weight,
    ff2_bias,
    ln2_gain,
    ln2_bias,
    cotangent,
):
    row_count, depth = tokens.shape
    seq = row_count // 2
    cols = qkv_weight.shape[2]
    units = ff1_weight.shape[1] // 2
    group = lax.axis_index("mp")
    me = lax.axis_index("dp")

    ready = (
        jnp.stack([group, me]).astype(jnp.int32),
        1 - group,
        group,
    )
    scalars, far_page, own_page = lax.optimization_barrier(ready)

    def outer(mine, bits):
        return [mine] + [swap(mine, bit) for bit in bits]

    def rels(bits):
        one, two = (1 << bit for bit in bits)
        return (0, one, two, one | two)

    ways = ((1, 2), (2, 1), (1, 2))

    block0, out_block = pick(scalars, ff1_weight, ff2_weight, out_weight, 0)
    out_mine, mine0 = swap_y(out_block), swap_y(block0)
    far_ctx, far_lse = attn_fwd(
        far_page, page_lengths, after(tokens, block0), qkv_weight, qv_bias, False, (0, 2)
    )
    oth_ctx, oth_lse = swap_y(far_ctx), swap_y(far_lse)
    own = attn_fwd(
        own_page, page_lengths, after(tokens, far_ctx), qkv_weight, qv_bias, True, (0, 1)
    )
    mine0 = after(mine0, own[0])
    by_x, by_z = swap(mine0, 1), swap(mine0, 2)
    own_ctx, own_lse, own_qkv = attn_fwd(
        own_page, page_lengths, after(tokens, mine0), qkv_weight, qv_bias, True, (1, 2), own
    )
    out_near = after(out_mine, own_ctx)
    out_core = swap(out_near, 0)
    bias_row = after(ff1_bias, own[0]).reshape(1, -1)
    block1, qkv_block = pick(
        after(scalars, out_near), ff1_weight, ff2_weight, qkv_weight, 1, (bias_row, qv_bias)
    )
    mine1 = swap_y(block1)
    rows = [v.reshape(1, -1) for v in after((out_bias, ln1_gain, ln1_bias), out_near)]
    out_bias, ln1_gain, ln1_bias = rows
    own_ctx, by_x, by_z = lax.optimization_barrier((own_ctx, by_x, by_z))
    out_far, normed_one, scale_one, hidden, hidden_turned = join(
        scalars,
        tokens,
        own_ctx,
        after(oth_ctx, (block1, oth_lse)),
        out_weight,
        out_near,
        out_core,
        out_bias,
        ln1_gain,
        ln1_bias,
    )
    stage0 = [mine0, by_x, by_z]
    last0 = swap(by_z, 1)
    act, slope, partial = ffn_own(hidden, ff1_weight, bias_row, ff2_weight, 0, ())
    mine1, last0 = after((mine1, last0), partial)
    far_biases = mine1
    stage1 = outer(mine1, ways[1])
    act, slope, partial = ffn_own(
        hidden, ff1_weight, bias_row, ff2_weight, 1, (after(partial, mine1), act, slope)
    )
    qkv_mine = swap_y(after(qkv_block, mine1))
    stage1 = after(stage1, partial)
    rows = [v.reshape(1, -1) for v in after((ff2_bias, ln2_gain, ln2_bias), partial)]
    ff2_bias, ln2_gain, ln2_bias = rows
    last1 = swap(stage1[2], ways[1][0])
    near0 = collect(after(stage0 + [last0], stage1[2]))
    core0 = swap(near0, 0)
    act, slope, partial, w1_far, w2_far = ffn_far(
        scalars,
        hidden,
        far_biases,
        near0,
        core0,
        rels(ways[0]),
        0,
        (after(partial, rows), act, slope),
    )
    last1, qkv_mine = after((last1, qkv_mine), partial)
    near1 = collect(stage1 + [last1])
    core1 = swap(near1, 0)
    qkv_stage = outer(after(qkv_mine, near1), ways[2])
    act, slope, partial, w1_far, w2_far = ffn_far(
        scalars,
        hidden,
        far_biases,
        near1,
        core1,
        rels(ways[1]),
        1,
        (partial, act, slope, w1_far, w2_far),
    )
    out_rows, dsecond, dffn, dffn_turned, sums_two = norm_two(
        scalars,
        partial,
        normed_one,
        cotangent,
        (ln1_gain, ln1_bias, ff2_bias, ln2_gain, ln2_bias),
    )

    qkv_stage = after(qkv_stage, dffn)
    last = swap(qkv_stage[2], ways[2][0])
    send_a = grad_send(after(dffn_turned, qkv_stage[0]), act, (0, 2))
    send_b = grad_send(after(dffn_turned, send_a), act, (1, 3))
    got_a, got_b = swap(send_a, 0), swap(send_b, 0)
    keep_a, send_a, b_own, b_far = keep_ffn(after(dffn_turned, send_b), act, got_a, got_b)
    ff2_x, ff2_y = swap(send_a, 1), swap_y(b_far)
    last = after(last, keep_a)
    dpre, db, dfirst, dattn, dattn_turned, sums_one, send_a, send_b, qkv_near = ffn_back(
        scalars,
        after(dffn, last),
        ff2_weight,
        w2_far,
        slope,
        ff1_weight,
        w1_far,
        dsecond,
        normed_one,
        scale_one,
        ln1_gain,
        hidden_turned,
        qkv_stage + [last],
    )
    got_a, got_b = swap(send_a, 0), swap(send_b, 0)
    qkv_core = swap(qkv_near, 0)
    ff2_own, ff2_far, ff2_keep, ff2_send = second(after(keep_a, dattn), ff2_x, b_own, ff2_y)
    ff2_y, ff2_x = swap_y(ff2_far), swap(ff2_send, 1)
    keep_a, send_a, b_own, b_far = keep_ffn(after(hidden_turned, ff2_own), dpre, got_a, got_b)
    ff1_x, ff1_y = swap(send_a, 1), swap_y(b_far)
    dqkv_far, dqv_far, dtok, tok_turned, far_send, out_send = attn_back_other(
        scalars,
        page_lengths,
        tokens,
        after(dattn, keep_a),
        out_far,
        oth_lse,
        far_biases,
        qkv_near,
        qkv_core,
        rels(ways[2]),
        own_ctx,
        oth_ctx,
        dattn_turned,
    )
    out_got, far_got = swap(out_send, 0), swap(far_send, 0)
    ff2_keep, ff2_send = third(after(ff2_own, dtok), ff2_y, ff2_keep, ff2_x)
    ff2_z = swap(ff2_send, 2)
    ff1_own, ff1_far, ff1_keep, ff1_send = second(after(keep_a, ff2_keep), ff1_x, b_own, ff1_y)
    ff1_y, ff1_x = swap_y(ff1_far), swap(ff1_send, 1)
    far_keep, far_send, b_far = keep_far(
        after(dattn_turned, ff1_own), tok_turned, own_ctx, oth_ctx, dqkv_far, out_got, far_got
    )
    far_x, far_y = swap(far_send, 1), swap_y(b_far)
    early, dtok, early_db = attn_back_own(
        scalars,
        page_lengths,
        after(dattn, far_keep),
        out_weight,
        own_lse,
        own_qkv,
        qkv_weight,
        dtok,
        dfirst,
        last=False,
    )
    ff1_keep, ff1_send = third(after(ff1_own, dtok), ff1_y, ff1_keep, ff1_x)
    ff1_z = swap(ff1_send, 2)
    ff2_keep, ff2_send = fourth(after(ff2_keep, ff1_keep), ff2_z)
    ff2_z = swap(ff2_send, 3)
    late, small, input_grad, own_send = attn_back_own(
        scalars,
        page_lengths,
        after(dattn, ff2_keep),
        out_weight,
        own_lse,
        own_qkv,
        qkv_weight,
        dtok,
        tok_turned,
        early,
        early_db,
        db,
        dqv_far,
        sums_one,
        sums_two,
        last=True,
    )
    own_got = swap(own_send, 0)
    ff1_keep, ff1_send = fourth(after(ff1_keep, own_send), ff1_z)
    ff1_z = swap(ff1_send, 3)
    far_keep, far_x, far_y = after((far_keep, far_x, far_y), ff1_keep)
    far_keep, ff2_z = lax.optimization_barrier((far_keep, ff2_z))
    out_keep, far_send = second_attn(far_keep, far_x)
    got_y = swap_y(far_send)
    keep, send, z_keep, z_send = keep_own(
        after(tok_turned, out_keep), early, late, own_got, far_y
    )
    got_x, got_z = swap(send, 1), swap(z_send, 2)
    small = after(small, keep)
    small = small + swap(small, 0)
    small = small + swap_y(small)
    small = small + swap(small, 1)
    keep, ff1_z = lax.optimization_barrier((keep, ff1_z))
    keep, send, v_keep, v_send = join_attn(
        after(keep, small), got_x, out_keep, got_y, z_keep, got_z
    )
    got_z, got_x = swap(send, 2), swap(v_send, 1)
    ff2_share = add(*after((ff2_keep, ff2_z), keep))
    other = swap(after(small, keep), 2)
    keep, send = last_attn(after(keep, ff2_share), got_z, v_keep, got_x)
    got = swap(send, 3)
    small = small + after(other, keep)
    other = swap(small, 3)
    ff1_share = add(*after((ff1_keep, ff1_z), keep))
    small = (small + after(other, ff1_share)).reshape(-1)
    ends = []
    at = 0
    for length in (4 * cols, 4 * units, depth, depth, depth, depth, depth, depth):
        ends.append(small[at : at + length])
        at += length
    ends[0] = ends[0].reshape(2, -1)
    keep, ends, ff1_share = lax.optimization_barrier((keep, ends, ff1_share))
    qkv_share, out_share = share_attn(keep, got)
    return (
        out_rows,
        input_grad,
        qkv_share,
        ends[0],
        out_share.T,
        ends[2],
        ends[3],
        ends[4],
        ff1_share,
        ends[1],
        ff2_share.T,
        ends[5],
        ends[6],
        ends[7],
    )


def suits(mesh):
    return mesh.shape["mp"] == 2 and mesh.shape["dp"] == 16


def solution(mesh):
    in_specs = (
        P("dp", None),
        P("dp"),
        P(None, None, "mp"),
        P(None, "mp"),
        P("mp", None),
        P(),
        P(),
        P(),
        P(None, "mp"),
        P("mp"),
        P("mp", None),
        P(),
        P(),
        P(),
        P("dp", None),
    )
    out_specs = (
        P(("dp", "mp"), None),
        P(("dp", "mp"), None),
        P(None, "dp", "mp"),
        P(),
        P("mp", "dp"),
        P(),
        P(),
        P(),
        P("dp", "mp"),
        P(),
        P("mp", "dp"),
        P(),
        P(),
        P(),
    )
    body = paged if suits(mesh) else local
    return jax.shard_map(body, mesh=mesh, in_specs=in_specs, out_specs=out_specs, check_vma=False)
```

```python
import functools

import jax
import jax.numpy as jnp
from jax import lax
from jax.experimental import pallas as pl
from jax.experimental.pallas import tpu as pltpu
from jax.sharding import PartitionSpec as P

HD = 64


EPSILON = 1e-05
NEGATIVE = -1e30


def normalize(values):
    center = values - jnp.mean(values, axis=-1, keepdims=True)
    spread = jnp.mean(center * center, axis=-1, keepdims=True)
    return center * lax.rsqrt(spread + EPSILON)


def gelu_exact(values):
    return jax.nn.gelu(values, approximate=False)


def over_rows(left, right):
    return lax.dot_general(
        left, right, (((0,), (0,)), ((), ())), preferred_element_type=jnp.float32
    )


def over_cols(left, right):
    return lax.dot_general(
        left, right, (((1,), (1,)), ((), ())), preferred_element_type=jnp.float32
    )


def page_scores(query, keyset, valid):
    raw = jnp.einsum("qhe,khe->hqk", query, keyset, preferred_element_type=jnp.float32) * HD ** (
        -0.5
    )
    return jnp.where(valid[None, None, :], raw, NEGATIVE)


def attend(block):
    query, keyset, valueset, valid = block
    scores = page_scores(query, keyset, valid)
    top = jnp.max(scores, axis=-1, keepdims=True)
    expo = jnp.exp(scores - top)
    total = jnp.sum(expo, axis=-1, keepdims=True)
    probs = expo / total
    context = jnp.einsum(
        "hqk,khe->qhe", probs.astype(jnp.bfloat16), valueset, preferred_element_type=jnp.float32
    )
    context = context.astype(jnp.bfloat16)
    return (context.reshape(context.shape[0], -1), top[..., 0] + jnp.log(total[..., 0]))


def attend_back(block):
    query, keyset, valueset, valid, logsum, dcontext = block
    scale = HD ** (-0.5)
    scores = page_scores(query, keyset, valid)
    probs = jnp.exp(scores - logsum[..., None])
    dprobs = jnp.einsum("qhe,khe->hqk", dcontext, valueset, preferred_element_type=jnp.float32)
    delta = jnp.sum(probs * dprobs, axis=-1, keepdims=True)
    dscores = (probs * (dprobs - delta)).astype(jnp.bfloat16)
    dquery = (
        jnp.einsum("hqk,khe->qhe", dscores, keyset, preferred_element_type=jnp.float32) * scale
    ).astype(jnp.bfloat16)
    dkeys = (
        jnp.einsum("hqk,qhe->khe", dscores, query, preferred_element_type=jnp.float32) * scale
    ).astype(jnp.bfloat16)
    dvalues = jnp.einsum(
        "hqk,qhe->khe", probs.astype(jnp.bfloat16), dcontext, preferred_element_type=jnp.float32
    ).astype(jnp.bfloat16)
    seq_len = query.shape[0]
    return (dquery.reshape(seq_len, -1), dkeys.reshape(seq_len, -1), dvalues.reshape(seq_len, -1))


def local(
    tokens,
    page_lengths,
    qkv_weight,
    qv_bias,
    out_weight,
    out_bias,
    ln1_gain,
    ln1_bias,
    ff1_weight,
    ff1_bias,
    ff2_weight,
    ff2_bias,
    ln2_gain,
    ln2_bias,
    cotangent,
):
    row_count = tokens.shape[0]
    page_count = page_lengths.shape[0]
    seq_len = row_count // page_count
    cols = qkv_weight.shape[2]
    ff_cols = ff1_weight.shape[1]
    group_heads = cols // HD
    share = row_count // lax.axis_size("mp")
    group = lax.axis_index("mp")
    share_start = group * share
    gain_one = ln1_gain.astype(jnp.float32)
    shift_one = ln1_bias.astype(jnp.float32)
    gain_two = ln2_gain.astype(jnp.float32)
    shift_two = ln2_bias.astype(jnp.float32)

    def own_rows(values):
        return lax.dynamic_slice_in_dim(values, share_start, share, 0)

    projected = jnp.einsum("rd,tdc->trc", tokens, qkv_weight, preferred_element_type=jnp.float32)
    bias_rows = jnp.stack([qv_bias[0], jnp.zeros_like(qv_bias[0]), qv_bias[1]]).astype(jnp.float32)
    qkv_rows = (projected + bias_rows[:, None, :]).astype(jnp.bfloat16)
    qkv_pages = qkv_rows.reshape(3, page_count, seq_len, group_heads, HD)
    valid = jnp.arange(seq_len)[None, :] < page_lengths[:, None]
    context, logsum = lax.map(attend, (qkv_pages[0], qkv_pages[1], qkv_pages[2], valid))
    context = context.reshape(row_count, cols)
    attn_part = jnp.dot(context, out_weight, preferred_element_type=jnp.float32).astype(
        jnp.bfloat16
    )
    attn = lax.psum(attn_part, "mp").astype(jnp.float32)
    first_sum = tokens.astype(jnp.float32) + attn + out_bias.astype(jnp.float32)
    normed_one, norm_one_back = jax.vjp(normalize, first_sum)
    hidden = normed_one * gain_one + shift_one
    hidden_low = hidden.astype(jnp.bfloat16)
    normed_one_own = own_rows(normed_one)
    pre = jnp.dot(hidden_low, ff1_weight, preferred_element_type=jnp.float32) + ff1_bias.astype(
        jnp.float32
    )
    activated, gelu_back = jax.vjp(gelu_exact, pre)
    act_low = activated.astype(jnp.bfloat16)
    ffn_part = jnp.dot(act_low, ff2_weight, preferred_element_type=jnp.float32).astype(jnp.bfloat16)
    cot_own = own_rows(cotangent).astype(jnp.float32)
    ffn = lax.psum(ffn_part, "mp").astype(jnp.float32)
    second_sum = hidden + ffn + ff2_bias.astype(jnp.float32)
    normed_two, norm_two_back = jax.vjp(normalize, second_sum)
    normed_two_own = own_rows(normed_two)
    out_rows = (normed_two_own * gain_two + shift_two).astype(jnp.bfloat16)
    dsecond = norm_two_back(cotangent.astype(jnp.float32) * gain_two)[0]
    dffn = dsecond.astype(jnp.bfloat16)
    dsecond_own = own_rows(dsecond)
    dgain_two = jnp.sum(cot_own * normed_two_own, axis=0)
    dshift_two = jnp.sum(cot_own, axis=0)
    dff2_bias = jnp.sum(dsecond_own, axis=0)
    dff2_weight = over_rows(act_low, dffn)
    dact = over_cols(dffn, ff2_weight)
    dpre = gelu_back(dact)[0].astype(jnp.bfloat16)
    dff1_bias = jnp.sum(dpre.astype(jnp.float32), axis=0)
    dff1_weight = over_rows(hidden_low, dpre)
    dhid_part = over_cols(dpre, ff1_weight).astype(jnp.bfloat16)
    dhidden = dsecond + lax.psum(dhid_part, "mp").astype(jnp.float32)
    dfirst = norm_one_back(dhidden * gain_one)[0]
    dattn = dfirst.astype(jnp.bfloat16)
    dhidden_own = own_rows(dhidden)
    dfirst_own = own_rows(dfirst)
    dgain_one = jnp.sum(dhidden_own * normed_one_own, axis=0)
    dshift_one = jnp.sum(dhidden_own, axis=0)
    dout_bias = jnp.sum(dfirst_own, axis=0)
    dout_weight = over_rows(context, dattn)
    dcontext = over_cols(dattn, out_weight).astype(jnp.bfloat16)
    dcontext_pages = dcontext.reshape(page_count, seq_len, group_heads, HD)
    dquery, dkeys, dvalues = lax.map(
        attend_back, (qkv_pages[0], qkv_pages[1], qkv_pages[2], valid, logsum, dcontext_pages)
    )
    dqkv = jnp.stack(
        [
            dquery.reshape(row_count, cols),
            dkeys.reshape(row_count, cols),
            dvalues.reshape(row_count, cols),
        ]
    )
    dqv_bias = jnp.stack(
        [jnp.sum(dqkv[0].astype(jnp.float32), axis=0), jnp.sum(dqkv[2].astype(jnp.float32), axis=0)]
    )
    dqkv_weight = jnp.einsum("rd,trc->tdc", tokens, dqkv, preferred_element_type=jnp.float32)
    dtok_part = jnp.einsum(
        "trc,tdc->rd", dqkv, qkv_weight, preferred_element_type=jnp.float32
    ).astype(jnp.bfloat16)
    input_grad = (
        dfirst_own
        + lax.psum_scatter(dtok_part, "mp", scatter_dimension=0, tiled=True).astype(jnp.float32)
    ).astype(jnp.bfloat16)
    qkv_share, out_share, ff1_share, ff2_share = (
        lax.psum_scatter(
            dqkv_weight.astype(jnp.bfloat16), "dp", scatter_dimension=1, tiled=True
        ).astype(jnp.float32),
        lax.psum_scatter(
            dout_weight.astype(jnp.bfloat16), "dp", scatter_dimension=1, tiled=True
        ).astype(jnp.float32),
        lax.psum_scatter(
            dff1_weight.astype(jnp.bfloat16), "dp", scatter_dimension=0, tiled=True
        ).astype(jnp.float32),
        lax.psum_scatter(
            dff2_weight.astype(jnp.bfloat16), "dp", scatter_dimension=1, tiled=True
        ).astype(jnp.float32),
    )
    qv_placed = lax.dynamic_update_slice_in_dim(
        jnp.zeros((2, cols * lax.axis_size("mp")), jnp.float32), dqv_bias, group * cols, 1
    )
    ff1_placed = lax.dynamic_update_slice_in_dim(
        jnp.zeros((ff_cols * lax.axis_size("mp"),), jnp.float32), dff1_bias, group * ff_cols, 0
    )
    small = lax.psum(
        (qv_placed, dout_bias, dgain_one, dshift_one, ff1_placed, dff2_bias, dgain_two, dshift_two),
        ("dp", "mp"),
    )
    return (
        out_rows,
        input_grad,
        qkv_share,
        small[0],
        out_share,
        small[1],
        small[2],
        small[3],
        ff1_share,
        small[4],
        ff2_share,
        small[5],
        small[6],
        small[7],
    )


BF = jnp.bfloat16
F32 = jnp.float32
ROOT_HALF = 2**-0.5
ROOT_TAU = 0.3989422804014327


def dg(left, right, left_dim, right_dim):
    return lax.dot_general(
        left, right, (((left_dim,), (right_dim,)), ((), ())), preferred_element_type=F32
    )


def whole(*shape):
    return pl.BlockSpec(shape, lambda *at: (0,) * len(shape), pipeline_mode=pl.Buffered(1))


def shaped(shape, dtype):
    return jax.ShapeDtypeStruct(shape, dtype)


def far_shaped(shape, dtype):
    return pltpu.HBM(shape, dtype)


TIMES = {
    "attn_fwd": 5,
    "pick": 2,
    "collect": 1,
    "attn_join": 5,
    "ffn_own": 3,
    "ffn_far": 5,
    "norm_two": 5,
    "grad_send": 3,
    "keep_ffn": 6,
    "ffn_back": 24,
    "second": 1000,
    "third": 1,
    "attn_back_other": 20,
    "fourth": 1,
    "keep_far": 5,
    "attn_back_own": 9,
    "second_attn": 1000,
    "keep_own": 2,
    "join_attn": 2,
    "last_attn": 1,
    "share_attn": 1,
}


def call(body, name, grid, ins, outs, args, scalars=(), scratch=(), aliases=None, flops=0, room=20, stay=()):
    args = [
        pltpu.with_memory_space_constraint(a, pltpu.HBM) if i in stay else a
        for i, a in enumerate(args)
    ]
    return pl.pallas_call(
        body,
        out_shape=[s for s, _ in outs],
        grid_spec=pltpu.PrefetchScalarGridSpec(
            num_scalar_prefetch=len(scalars),
            grid=grid,
            in_specs=ins,
            out_specs=[s for _, s in outs],
            scratch_shapes=list(scratch),
        ),
        input_output_aliases=aliases or {},
        cost_estimate=pl.CostEstimate(
            flops=TIMES[name] * 10**9, bytes_accessed=0, transcendentals=0
        ),
        name=name,
        compiler_params=pltpu.CompilerParams(vmem_limit_bytes=room * 2**20),
    )(*scalars, *args)


def permute_columns(source, target, me, rows):
    low = me & 1
    high = me >> 1
    size = min(rows, 128)
    lane = lax.broadcasted_iota(jnp.int32, (size, 128), 1)
    half = target.shape[1] // 2

    @pl.loop(0, rows // size)
    def _(i):
        at = pl.ds(pl.multiple_of(i * size, size), size)
        for u in range(4):
            blocks = []
            for z in range(2):
                rel = z * 4 + (u & 1) * 2 + (u >> 1)
                start = pl.multiple_of((rel ^ high) * 128, 128)
                blocks.append(source[at, pl.ds(start, 128)])
            turned = [pltpu.roll(block, 64, 1) for block in blocks]
            near = jnp.where(lane < 64, blocks[0], turned[1])
            far = jnp.where(lane < 64, turned[0], blocks[1])
            first = jnp.where(low == 0, near, far)
            second = jnp.where(low == 0, far, near)
            target[at, u * 128 : (u + 1) * 128] = first.astype(BF)
            target[at, half + u * 128 : half + (u + 1) * 128] = second.astype(BF)


def attn_fwd_body(s_ref, len_ref, x_ref, w_ref, b_ref, *outs, keep_rows, skip):
    q_ref, k_ref, v_ref = outs[-3:]
    ctx_ref, lse_ref = outs[skip : skip + 2]
    count = len_ref[s_ref[0]]
    x = x_ref[...]
    seq = x.shape[0]
    query = (dg(x, w_ref[0], 1, 0) + b_ref[0:1, :].astype(F32)).astype(BF)
    k_ref[...] = dg(x, w_ref[1], 1, 0).astype(BF)
    v_ref[...] = (dg(x, w_ref[2], 1, 0) + b_ref[1:2, :].astype(F32)).astype(BF)
    if keep_rows:
        outs[skip + 2][0] = query
        outs[skip + 2][1] = k_ref[...]
        outs[skip + 2][2] = v_ref[...]
    q_ref[...] = query * BF(HD**-0.5)
    first = lax.broadcasted_iota(jnp.int32, (seq, 2 * HD), 1) < HD
    valid = lax.broadcasted_iota(jnp.int32, (seq, seq), 0) < count

    for pair in range(query.shape[1] // (2 * HD)):
        cut = slice(pair * 2 * HD, (pair + 1) * 2 * HD)
        q_pair, k_pair = q_ref[:, cut], k_ref[:, cut]
        turned = v_ref[:, cut].T
        parts = []
        for h in range(2):
            own = jnp.where(first if h == 0 else ~first, q_pair, BF(0))
            scores = jnp.where(valid, dg(k_pair, own, 1, 1), NEGATIVE)
            top = jnp.max(scores, axis=0, keepdims=True)
            expo = jnp.exp(scores - top)
            total = jnp.sum(expo, axis=0, keepdims=True)
            part = dg(turned[h * HD : (h + 1) * HD], expo.astype(BF), 1, 0)
            parts.append(part * (1.0 / total))
            lse_ref[0, pair * 2 + h : pair * 2 + h + 1, :] = top + jnp.log(total)
        ctx_ref[:, cut] = jnp.concatenate(parts, axis=0).T.astype(BF)


def attn_fwd(page, lengths, tokens, weight, bias, keep_rows, tiles, before=()):
    depth = tokens.shape[1]
    seq = tokens.shape[0] // lengths.shape[0]
    cols = weight.shape[2]
    tile = 256
    heads = tile // HD
    start, stop = tiles
    outs = [
        (shaped((seq, cols), BF), pl.BlockSpec((seq, tile), lambda j, s, n: (0, start + j))),
        (
            shaped((cols // tile, heads, seq), F32),
            pl.BlockSpec((1, heads, seq), lambda j, s, n: (start + j, 0, 0)),
        ),
    ]
    if keep_rows:
        outs.append(
            (
                far_shaped((3, seq, cols), BF),
                pl.BlockSpec((3, seq, tile), lambda j, s, n: (0, 0, start + j)),
            )
        )
    return call(
        functools.partial(attn_fwd_body, keep_rows=keep_rows, skip=len(before)),
        "attn_fwd",
        (stop - start,),
        [
            pl.BlockSpec((seq, depth), lambda j, s, n: (s[0], 0)),
            pl.BlockSpec((3, depth, tile), lambda j, s, n: (0, 0, start + j)),
            pl.BlockSpec((2, tile), lambda j, s, n: (0, start + j)),
            *[pl.BlockSpec(memory_space=pl.ANY)] * len(before),
        ],
        outs,
        (tokens, weight, bias, *before),
        (page.reshape(1), lengths),
        [pltpu.VMEM((seq, tile), BF)] * 3,
        stay=(1,),
        aliases={5 + i: i for i in range(len(before))},
    )


def join_body(s_ref, x_ref, own_ref, oth_ref, w_ref, near_ref, core_ref, *refs):
    bias_ref, gain_ref, shift_ref = refs[:3]
    far_ref, normed_ref, scale_ref, low_ref, perm_ref, wide = refs[3:]
    me = s_ref[1]

    @pl.when(pl.program_id(0) == 0)
    def _():
        size = near_ref.shape[1]
        for i in range(2):
            for flip, stack in ((0, near_ref), (1, core_ref)):
                at = pl.multiple_of(((me & 3) ^ (2 * i) ^ flip) * size, 16)
                far_ref[pl.ds(at, size), :] = stack[i]

    attn = dg(own_ref[...], w_ref[...], 1, 0) + dg(oth_ref[...], far_ref[...], 1, 0)
    total = x_ref[...].astype(F32) + attn + bias_ref[...].astype(F32)
    center = total - jnp.mean(total, axis=-1, keepdims=True)
    scale = lax.rsqrt(jnp.mean(center * center, axis=-1, keepdims=True) + EPSILON)
    normed = center * scale
    normed_ref[...] = normed
    scale_ref[...] = scale
    hidden = normed * gain_ref[...].astype(F32) + shift_ref[...].astype(F32)
    low_ref[...] = hidden.astype(BF)
    wide[...] = hidden
    permute_columns(wide, perm_ref, me, wide.shape[0])


def join(scalars, tokens, own, other, weight, near, core, bias, gain, shift):
    seq, cols = own.shape
    depth = tokens.shape[1]
    steps = 2
    rows = seq // steps
    row = pl.BlockSpec((rows, depth), lambda i, s: (i, 0))
    half = pl.BlockSpec((rows, cols), lambda i, s: (i, 0))
    return call(
        join_body,
        "attn_join",
        (steps,),
        [
            pl.BlockSpec((rows, depth), lambda i, s: (s[0] * steps + i, 0)),
            half,
            half,
            whole(cols, depth),
            whole(*near.shape),
            whole(*near.shape),
            *[whole(1, depth)] * 3,
        ],
        [
            (far_shaped((cols, depth), BF), whole(cols, depth)),
            (far_shaped((seq, depth), F32), row),
            (shaped((seq, 1), F32), pl.BlockSpec((rows, 1), lambda i, s: (i, 0))),
            (shaped((seq, depth), BF), row),
            (far_shaped((seq, depth), BF), row),
        ],
        (
            tokens,
            own,
            other,
            weight,
            near,
            core,
            bias,
            gain,
            shift,
        ),
        (scalars,),
        [pltpu.VMEM((rows, depth), F32)],
        flops=4 * seq * cols * depth,
    )


def ffn_tile(h_ref, w_one, bias, w_two, act_ref, slope_ref):
    pre = dg(h_ref[...], w_one, 1, 0) + bias
    phi = 0.5 + 0.5 * lax.erf(pre * F32(ROOT_HALF))
    act = (pre * phi).astype(BF)
    act_ref[0] = act
    slope_ref[0] = (phi + pre * (jnp.exp(-0.5 * pre * pre) * F32(ROOT_TAU))).astype(BF)
    return dg(act, w_two, 1, 0)


TILE = 512


def start_sum(sum_ref, in_ref):
    @pl.when(pl.program_id(0) == 0)
    def _():
        sum_ref[...] = jnp.zeros_like(sum_ref) if in_ref is None else in_ref[...]


def ffn_own_body(h_ref, w1_ref, b_ref, w2_ref, *refs):
    act_ref, slope_ref, sum_ref = refs[-3:]
    start_sum(sum_ref, refs[0] if len(refs) > 3 else None)
    bias = b_ref[...].astype(F32)
    sum_ref[...] += ffn_tile(h_ref, w1_ref[...], bias, w2_ref[...], act_ref, slope_ref)


def ffn_own(hidden, w_one, bias, w_two, g, before):
    seq, depth = hidden.shape
    units = w_one.shape[1] // 2
    steps = units // TILE
    base = g * steps
    side = pl.BlockSpec((1, seq, TILE), lambda j: (g, 0, j))
    full = whole(seq, depth)
    hbm = pl.BlockSpec(memory_space=pl.ANY)
    return call(
        ffn_own_body,
        "ffn_own",
        (steps,),
        [
            full,
            pl.BlockSpec((depth, TILE), lambda j: (0, base + j)),
            pl.BlockSpec((1, TILE), lambda j: (0, base + j)),
            pl.BlockSpec((TILE, depth), lambda j: (base + j, 0)),
        ]
        + ([full, hbm, hbm] if before else []),
        [
            (shaped((4, seq, units), BF), side),
            (far_shaped((4, seq, units), BF), side),
            (shaped((seq, depth), F32), full),
        ],
        (hidden, w_one, bias, w_two) + before,
        aliases={4: 2, 5: 0, 6: 1} if before else None,
        stay=(1, 3),
    )


def pick_body(s_ref, one_ref, two_ref, more_ref, *refs):
    ffn_ref, out_ref = refs[-2:]
    size = one_ref.shape[0]
    ffn_ref[:size] = one_ref[...]
    ffn_ref[size : 2 * size] = two_ref[...]
    out_ref[...] = more_ref[...]
    if len(refs) > 2:
        low_ref, qv_ref = refs[:2]
        depth = ffn_ref.shape[1]
        lines = [low_ref[:, i * depth : (i + 1) * depth] for i in range(2)]
        lines.append(jnp.concatenate([qv_ref[i : i + 1] for i in range(2)], axis=1))
        lines.append(jnp.zeros((16 - len(lines), depth), BF))
        ffn_ref[2 * size :] = jnp.concatenate(lines, axis=0)


def pick(scalars, ff1_weight, ff2_weight, more, g, biases=()):
    depth, units = ff1_weight.shape[0], ff1_weight.shape[1] // 2
    size = depth // 8
    if more.ndim == 2:
        shape = (more.shape[0] // 4, more.shape[1])
        spec = pl.BlockSpec(shape, lambda i, s: (s[1] & 3, 0))
    else:
        shape = (more.shape[0], more.shape[1] // 8, more.shape[2])
        spec = pl.BlockSpec(shape, lambda i, s: (0, s[1] & 7, 0))
    rows = 2 * size + (16 if biases else 0)
    return call(
        pick_body,
        "pick",
        (1,),
        [
            pl.BlockSpec((size, units), lambda i, s: (s[1] & 7, g)),
            pl.BlockSpec((units // 8, depth), lambda i, s: (g * 8 + (s[1] & 7), 0)),
            spec,
            *[whole(*bias.shape) for bias in biases],
        ],
        [
            (shaped((rows, units), BF), whole(rows, units)),
            (shaped(shape, BF), whole(*shape)),
        ],
        (ff1_weight, ff2_weight, more, *biases),
        (scalars,),
        stay=(0, 1, 2),
    )


def collect_body(*refs):
    for i, piece in enumerate(refs[:-1]):
        refs[-1][i] = piece[...]


def collect(pieces):
    shape = pieces[0].shape
    return call(
        collect_body,
        "collect",
        (1,),
        [whole(*shape)] * len(pieces),
        [(shaped((len(pieces),) + shape, BF), whole(len(pieces), *shape))],
        tuple(pieces),
    )[0]


def ffn_far_body(
    s_ref, h_ref, b_ref, near_ref, core_ref, near2_ref, core2_ref, in_ref, *refs, rels, row
):
    act_ref, slope_ref, sum_ref, w1_ref, w2_ref = refs[-5:]
    j = pl.program_id(0)
    me = s_ref[1]

    def put(target, near, core):
        size = near.shape[1]
        for i, rel in enumerate(rels):
            for flip, stack in ((0, near), (1, core)):
                at = pl.multiple_of(((me & 7) ^ rel ^ flip) * size, 16)
                target[pl.ds(at, size), :] = stack[i]

    @pl.when(j == 0)
    def _():
        put(w2_ref, near2_ref, core2_ref)

    put(w1_ref, near_ref, core_ref)
    w_two = w2_ref[pl.ds(pl.multiple_of(j * TILE, TILE), TILE), :]
    start_sum(sum_ref, in_ref)
    bias = b_ref[row : row + 1, :].astype(F32)
    sum_ref[...] += ffn_tile(h_ref, w1_ref[...], bias, w_two, act_ref, slope_ref)


def ffn_far(scalars, hidden, bias, near, core, rels, g, before):
    seq, depth = hidden.shape
    units = before[1].shape[2]
    steps = units // TILE
    size = depth // 8
    side = pl.BlockSpec((1, seq, TILE), lambda j, s: (2 + g, 0, j))
    full = whole(seq, depth)
    hbm = pl.BlockSpec(memory_space=pl.ANY)
    one = pl.BlockSpec((4, size, TILE), lambda j, s: (0, 0, j))
    two = pl.BlockSpec(
        (4, size, depth), lambda j, s: (0, 1, 0), pipeline_mode=pl.Buffered(1)
    )
    args = (hidden, bias, near, core, near, core, *before)
    return call(
        functools.partial(ffn_far_body, rels=rels, row=g),
        "ffn_far",
        (steps,),
        [
            full,
            pl.BlockSpec((16, TILE), lambda j, s: (bias.shape[0] // 16 - 1, j)),
            one,
            one,
            two,
            two,
            full,
            *[hbm] * (len(before) - 1),
        ],
        [
            (shaped((4, seq, units), BF), side),
            (far_shaped((4, seq, units), BF), side),
            (shaped((seq, depth), F32), full),
            (
                far_shaped((depth, 2 * units), BF),
                pl.BlockSpec((depth, TILE), lambda j, s: (0, g * steps + j)),
            ),
            (
                far_shaped((2 * units, depth), BF),
                pl.BlockSpec((units, depth), lambda j, s: (g, 0), pipeline_mode=pl.Buffered(1)),
            ),
        ],
        args,
        (scalars,),
        aliases={7: 2, 8: 0, 9: 1} | ({10: 3, 11: 4} if g else {}),
        flops=4 * seq * depth * units,
    )


def norm_back(grad, normed, scale):
    return scale * (
        grad
        - jnp.mean(grad, axis=-1, keepdims=True)
        - normed * jnp.mean(grad * normed, axis=-1, keepdims=True)
    )


CHUNK = 64


def chunked(rows, sums_ref, chunk):
    zero = jnp.zeros((1, sums_ref.shape[1]), F32)

    def step(i, sums):
        news = chunk(pl.ds(pl.multiple_of(i * CHUNK, CHUNK), CHUNK))
        return tuple(
            old + jnp.sum(new, axis=0, keepdims=True) for old, new in zip(sums, news)
        )

    sums = lax.fori_loop(0, rows // CHUNK, step, (zero, zero, zero), unroll=True)
    first = pl.program_id(0) == 0
    for i in range(3):
        old = sums_ref[i : i + 1, :]
        sums_ref[i : i + 1, :] = jnp.where(first, 0.0, old) + sums[i]


def norm_two_body(
    s_ref, in_ref, normed_ref, cot_ref, *refs
):
    gain_one, shift_one, bias, gain, shift = [ref[...].astype(F32) for ref in refs[:5]]
    out_ref, ds_ref, df_ref, perm_ref, sums_ref = refs[5:]

    def chunk(at):
        total = normed_ref[at, :] * gain_one + shift_one + in_ref[at, :] + bias
        center = total - jnp.mean(total, axis=-1, keepdims=True)
        scale = lax.rsqrt(jnp.mean(center * center, axis=-1, keepdims=True) + EPSILON)
        normed = center * scale
        out_ref[at, :] = (normed * gain + shift).astype(BF)
        cot = cot_ref[at, :].astype(F32)
        ds = norm_back(cot * gain, normed, scale)
        ds_ref[at, :] = ds
        df_ref[at, :] = ds.astype(BF)
        return ds, cot * normed, cot

    rows = in_ref.shape[0]
    chunked(rows, sums_ref, chunk)
    permute_columns(ds_ref, perm_ref, s_ref[1], rows)


def norm_two(scalars, total, normed, cotangent, vectors):
    seq, depth = total.shape
    steps = 4
    row = pl.BlockSpec((seq // steps, depth), lambda i, s: (i, 0))
    return call(
        norm_two_body,
        "norm_two",
        (steps,),
        [
            row,
            row,
            pl.BlockSpec((seq // steps, depth), lambda i, s: (s[0] * steps + i, 0)),
            *[whole(1, depth)] * 5,
        ],
        [
            (far_shaped((seq, depth), BF), row),
            (shaped((seq, depth), F32), row),
            (shaped((seq, depth), BF), row),
            (shaped((seq, depth), BF), row),
            (shaped((8, depth), F32), pl.BlockSpec((8, depth), lambda i, s: (0, 0))),
        ],
        (total, normed, cotangent, *vectors),
        (scalars,),
        stay=(1, 2),
        flops=40 * seq * depth,
    )


def send_order(i):
    return (i % 2) * 2 + i // 2


def ffn_back_body(
    s_ref,
    df_ref,
    w2_ref,
    w2_far_ref,
    slope_ref,
    w1_ref,
    w1_far_ref,
    ds_ref,
    normed_ref,
    scale_ref,
    gain_ref,
    turned_ref,
    *refs,
    tiles,
):
    pieces = refs[:4]
    dpre_ref, db_ref, first_ref, low_ref, perm_ref, sums_ref = refs[4:10]
    send_a_ref, send_b_ref, near_ref, wide = refs[10:]
    j = pl.program_id(0)
    per = dpre_ref.shape[2] // TILE

    @pl.when(j == 1)
    def _():
        for i, piece in enumerate(pieces):
            near_ref[i] = piece[...]

    @pl.when(j == 0)
    def _():
        wide[...] = ds_ref[...]

    def tile(w_two, w_one):
        dact = dg(df_ref[...], w_two[...], 1, 1)
        dpre = (dact * slope_ref[0].astype(F32)).astype(BF)
        dpre_ref[j // per, :, pl.ds(pl.multiple_of((j % per) * TILE, TILE), TILE)] = dpre
        db_ref[...] = jnp.sum(dpre.astype(F32), axis=0, keepdims=True)
        wide[...] += dg(dpre, w_one[...], 1, 1)

    pl.when(j < tiles // 2)(functools.partial(tile, w2_ref, w1_ref))
    pl.when((j >= tiles // 2) & (j < tiles))(functools.partial(tile, w2_far_ref, w1_far_ref))

    @pl.when(j == tiles - 1)
    def _():
        gain = gain_ref[...].astype(F32)
        zero = jnp.zeros((1, gain.shape[1]), F32)

        def step(i, sums):
            at = pl.ds(pl.multiple_of(i * CHUNK, CHUNK), CHUNK)
            grad = wide[at, :]
            normed = normed_ref[at, :]
            first = norm_back(grad * gain, normed, scale_ref[at, :])
            first_ref[at, :] = first
            low_ref[at, :] = first.astype(BF)
            return tuple(
                old + jnp.sum(new, axis=0, keepdims=True)
                for old, new in zip(sums, (first, grad * normed, grad))
            )

        rows = wide.shape[0]
        sums = lax.fori_loop(0, rows // CHUNK, step, (zero, zero, zero), unroll=2)
        for i in range(3):
            sums_ref[i : i + 1, :] = sums[i]
        permute_columns(first_ref, perm_ref, s_ref[1], rows)

    @pl.when(j >= tiles)
    def _():
        part = dg(turned_ref[...], dpre_ref[send_order(j - tiles)], 0, 0).astype(BF)

        @pl.when(j < tiles + 2)
        def _():
            send_a_ref[0] = part

        @pl.when(j >= tiles + 2)
        def _():
            send_b_ref[0] = part


def ffn_back(
    scalars,
    dffn,
    w_two,
    w_two_far,
    slope,
    w_one,
    w_one_far,
    dsecond,
    normed,
    scale,
    gain,
    turned,
    pieces,
):
    seq, depth = dffn.shape
    units = slope.shape[2]
    steps = units // TILE
    half = 2 * steps
    tiles = 2 * half
    full = whole(seq, depth)

    def near(j):
        return jnp.minimum(j, half - 1)

    def far(j):
        return jnp.clip(j - half, 0, half - 1)

    def last(j):
        return jnp.minimum(j, tiles - 1)

    def send(first):
        return pl.BlockSpec(
            (1, depth // 2, units), lambda j, s: (jnp.clip(j - first, 0, 1), 0, 0)
        )

    return call(
        functools.partial(ffn_back_body, tiles=tiles),
        "ffn_back",
        (tiles + 4,),
        [
            full,
            pl.BlockSpec((TILE, depth), lambda j, s: (near(j), 0)),
            pl.BlockSpec((TILE, depth), lambda j, s: (far(j), 0)),
            pl.BlockSpec((1, seq, TILE), lambda j, s: (last(j) // steps, 0, last(j) % steps)),
            pl.BlockSpec((depth, TILE), lambda j, s: (0, near(j))),
            pl.BlockSpec((depth, TILE), lambda j, s: (0, far(j))),
            full,
            full,
            whole(seq, 1),
            whole(1, depth),
            pl.BlockSpec((seq, depth // 2), lambda j, s: (0, 1), pipeline_mode=pl.Buffered(1)),
            *[whole(*pieces[0].shape)] * 4,
        ],
        [
            (shaped((4, seq, units), BF), whole(4, seq, units)),
            (shaped((1, 4 * units), F32), pl.BlockSpec((1, TILE), lambda j, s: (0, last(j)))),
            (far_shaped((seq, depth), F32), full),
            (shaped((seq, depth), BF), full),
            (shaped((seq, depth), BF), full),
            (shaped((8, depth), F32), whole(8, depth)),
            (shaped((2, depth // 2, units), BF), send(tiles)),
            (shaped((2, depth // 2, units), BF), send(tiles + 2)),
            (shaped((4,) + pieces[0].shape, BF), whole(4, *pieces[0].shape)),
        ],
        (
            dffn,
            w_two,
            w_two_far,
            slope,
            w_one,
            w_one_far,
            dsecond,
            normed,
            scale,
            gain,
            turned,
            *pieces,
        ),
        (scalars,),
        [pltpu.VMEM((seq, depth), F32)],
        room=36,
        stay=(1, 2, 3, 4, 5, 7, 10),
    )


def attn_back_tile(j, count, refs, lse_ref, dc_ref, out_ref, dqkv_ref, db_ref):
    q_ref, k_ref, v_ref = refs
    seq, size = q_ref.shape
    first = lax.broadcasted_iota(jnp.int32, (seq, 2 * HD), 1) < HD
    valid = lax.broadcasted_iota(jnp.int32, (seq, seq), 0) < count

    @pl.loop(0, size // (2 * HD))
    def _(pair):
        cut = pl.ds(pl.multiple_of(pair * 2 * HD, 2 * HD), 2 * HD)
        q_pair, k_pair, v_pair, dc_pair = q_ref[:, cut], k_ref[:, cut], v_ref[:, cut], dc_ref[:, cut]
        dquery = dkeys = dvalues = 0.0
        for h in range(2):
            mask = first if h == 0 else ~first
            q_own = jnp.where(mask, q_pair, BF(0))
            k_own = jnp.where(mask, k_pair, BF(0))
            dc_own = jnp.where(mask, dc_pair, BF(0))
            scores = dg(k_pair, q_own, 1, 1) - lse_ref[0, pl.ds(pair * 2 + h, 1), :]
            probs = jnp.exp(jnp.where(valid, scores, NEGATIVE))
            dprobs = dg(v_pair, dc_own, 1, 1)
            delta = jnp.sum(probs * dprobs, axis=0, keepdims=True)
            dscores = (probs * (dprobs - delta)).astype(BF)
            dvalues = dvalues + dg(probs.astype(BF), dc_own, 1, 0)
            dkeys = dkeys + dg(dscores, q_own, 1, 0)
            dquery = dquery + dg(dscores, k_own, 0, 0)
        out_ref[0, :, cut] = (dquery * HD**-0.5).astype(BF)
        out_ref[1, :, cut] = dkeys.astype(BF)
        out_ref[2, :, cut] = dvalues.astype(BF)

    for t in range(3):
        dqkv_ref[t, :, pl.ds(pl.multiple_of(j * size, size), size)] = out_ref[t]
    db_ref[0:1, :] = jnp.sum(out_ref[0].astype(F32), axis=0, keepdims=True)
    db_ref[1:2, :] = jnp.sum(out_ref[2].astype(F32), axis=0, keepdims=True)


def attn_back_other_body(
    s_ref,
    len_ref,
    x_ref,
    da_ref,
    wo_ref,
    lse_ref,
    qb_ref,
    vb_ref,
    near_ref,
    core_ref,
    own_ref,
    oth_ref,
    da_turned_ref,
    dqkv_ref,
    db_ref,
    sum_ref,
    turned_ref,
    far_send_ref,
    out_send_ref,
    w_ref,
    wide,
    q_ref,
    k_ref,
    v_ref,
    dc_ref,
    out_ref,
    *,
    rels,
    tiles,
):
    j = pl.program_id(0)
    me = s_ref[1]
    half = turned_ref.shape[1] // 2

    @pl.when(j < tiles)
    def _():
        size = near_ref.shape[2]
        for i, rel in enumerate(rels):
            for flip, stack in ((0, near_ref), (1, core_ref)):
                at = pl.multiple_of(((me & 7) ^ rel ^ flip) * size, 16)
                w_ref[:, pl.ds(at, size), :] = stack[i]
        x = x_ref[...]
        query = (dg(x, w_ref[0], 1, 0) + qb_ref[2:3, :].astype(F32)).astype(BF)
        q_ref[...] = query * BF(HD**-0.5)
        k_ref[...] = dg(x, w_ref[1], 1, 0).astype(BF)
        v_ref[...] = (dg(x, w_ref[2], 1, 0) + vb_ref[2:3, :].astype(F32)).astype(BF)
        dc_ref[...] = dg(da_ref[...], wo_ref[...], 1, 1).astype(BF)
        count = len_ref[s_ref[0]]
        refs = (q_ref, k_ref, v_ref)
        attn_back_tile(j, count, refs, lse_ref, dc_ref, out_ref, dqkv_ref, db_ref)
        start_sum(sum_ref, None)
        for t in range(3):
            sum_ref[...] += dg(out_ref[t], w_ref[t], 1, 1)

    @pl.when(j == 0)
    def _():
        wide[...] = x_ref[...].astype(F32)
        permute_columns(wide, turned_ref, me, x_ref.shape[0])

    @pl.when((j >= tiles) & (j < tiles + 3))
    def _():
        right = dqkv_ref[jnp.clip(j - tiles, 0, 2)]
        far_send_ref[0] = dg(turned_ref[:, half:], right, 0, 0).astype(BF)

    for side, ref in enumerate((own_ref, oth_ref)):

        @pl.when(j == tiles + 3 + side)
        def _():
            out_send_ref[0] = dg(da_turned_ref[...], ref[...], 0, 0).astype(BF)


def attn_back_other(
    scalars, lengths, tokens, dattn, out_w, logsum, bias, near, core, rels, own, other, da_turned
):
    seq, depth = dattn.shape
    cols = out_w.shape[0]
    tile = 256
    heads = tile // HD
    tiles = cols // tile
    half = depth // 2
    ahead = bias.shape[0] // 16 - 1

    def at(j):
        return jnp.minimum(j, tiles - 1)

    stack = pl.BlockSpec((4, 3, depth // 8, tile), lambda j, s, n: (0, 0, 0, at(j)))
    return call(
        functools.partial(attn_back_other_body, rels=rels, tiles=tiles),
        "attn_back_other",
        (tiles + 5,),
        [
            pl.BlockSpec((seq, depth), lambda j, s, n: (s[0], 0)),
            whole(seq, depth),
            pl.BlockSpec((tile, depth), lambda j, s, n: (at(j), 0)),
            pl.BlockSpec((1, heads, seq), lambda j, s, n: (at(j), 0, 0)),
            pl.BlockSpec((16, tile), lambda j, s, n: (ahead, at(j))),
            pl.BlockSpec((16, tile), lambda j, s, n: (ahead, tiles + at(j))),
            stack,
            stack,
            whole(seq, cols),
            whole(seq, cols),
            pl.BlockSpec((seq, half), lambda j, s, n: (0, 1), pipeline_mode=pl.Buffered(1)),
        ],
        [
            (shaped((3, seq, cols), BF), whole(3, seq, cols)),
            (shaped((2, cols), F32), pl.BlockSpec((2, tile), lambda j, s, n: (0, at(j)))),
            (far_shaped((seq, depth), F32), whole(seq, depth)),
            (shaped((seq, depth), BF), whole(seq, depth)),
            (
                shaped((3, half, cols), BF),
                pl.BlockSpec((1, half, cols), lambda j, s, n: (jnp.clip(j - tiles, 0, 2), 0, 0)),
            ),
            (
                shaped((2, half, cols), BF),
                pl.BlockSpec(
                    (1, half, cols), lambda j, s, n: (jnp.clip(j - tiles - 3, 0, 1), 0, 0)
                ),
            ),
        ],
        (tokens, dattn, out_w, logsum, bias, bias, near, core, own, other, da_turned),
        (scalars, lengths),
        [pltpu.VMEM((3, depth, tile), BF), pltpu.VMEM((seq, depth), F32)]
        + [pltpu.VMEM((seq, tile), BF)] * 4
        + [pltpu.VMEM((3, seq, tile), BF)],
        room=30,
        stay=(0, 2),
    )


def attn_back_own_body(
    s_ref, len_ref, da_ref, wo_ref, lse_ref, qkv_ref, w_ref, *refs, last
):
    (wide, db_ref, q_ref, dc_ref, out_ref) = refs[-5:]
    j = pl.program_id(0)
    if last:
        in_ref, turned_ref, early_ref, early_db_ref, ffn_db_ref, far_db_ref = refs[:6]
        one_ref, two_ref, dqkv_ref, small_ref, grad_ref, send_ref = refs[6:12]
    else:
        in_ref, first_ref, dqkv_ref, sum_ref, db_out_ref = refs[:5]

    @pl.when(j == 0)
    def _():
        dc_ref[...] = dg(da_ref[...], wo_ref[...], 1, 1).astype(BF)
        q_ref[...] = qkv_ref[0] * BF(HD**-0.5)
        tile = (q_ref, qkv_ref.at[1], qkv_ref.at[2])
        attn_back_tile(0, len_ref[s_ref[0]], tile, lse_ref, dc_ref, out_ref, dqkv_ref, db_ref)
        wide[...] = in_ref[...] if last else in_ref[...] + first_ref[...]
        for t in range(3):
            wide[...] += dg(out_ref[t], w_ref[t], 1, 1)
        if not last:
            sum_ref[...] = wide[...]
            db_out_ref[...] = db_ref[...]
            return
        grad_ref[...] = wide[...].astype(BF)
        side = s_ref[0]
        cols = far_db_ref.shape[1]
        depth = small_ref.shape[1]
        own = jnp.concatenate([early_db_ref[...], db_ref[...]], axis=1)
        small_ref[0:2, pl.ds(pl.multiple_of(side * cols, 128), cols)] = own
        small_ref[0:2, pl.ds(pl.multiple_of((1 - side) * cols, 128), cols)] = far_db_ref[...]
        lines = [ffn_db_ref[:, i * depth : (i + 1) * depth] for i in range(4)]
        small_ref[2:6] = jnp.where(
            side == 0,
            jnp.concatenate(lines, axis=0),
            jnp.concatenate(lines[2:] + lines[:2], axis=0),
        )
        small_ref[6:9] = one_ref[0:3]
        small_ref[9:12] = two_ref[0:3]
        small_ref[12:16] = jnp.zeros((4, depth), F32)

    if last:

        @pl.when(j > 0)
        def _():
            at = jnp.maximum(j - 1, 0)
            halves = [
                dg(turned_ref[...], ref[at], 0, 0).astype(BF) for ref in (early_ref, dqkv_ref)
            ]
            send_ref[0] = jnp.concatenate(halves, axis=1)


def attn_back_own(scalars, lengths, dattn, out_w, logsum, qkv, weight, *more, last):
    seq, depth = dattn.shape
    cols = out_w.shape[0]
    tile = cols // 2
    heads = tile // HD
    half = depth // 2
    at = int(last)
    full = whole(seq, depth)
    outs = [(shaped((3, seq, tile), BF), whole(3, seq, tile))]
    if last:
        turned = pl.BlockSpec(
            (seq, half), lambda j, s, n: (0, 1), pipeline_mode=pl.Buffered(1)
        )
        ins = [full, turned] + [whole(*arg.shape) for arg in more[2:]]
        outs += [
            (shaped((16, depth), F32), whole(16, depth)),
            (far_shaped((seq, depth), BF), full),
            (
                shaped((3, half, cols), BF),
                pl.BlockSpec((1, half, cols), lambda j, s, n: (jnp.maximum(j - 1, 0), 0, 0)),
            ),
        ]
    else:
        ins = [full, full]
        outs += [(shaped((seq, depth), F32), full), (shaped((2, tile), F32), whole(2, tile))]
    return call(
        functools.partial(attn_back_own_body, last=last),
        "attn_back_own",
        (4 if last else 1,),
        [
            full,
            pl.BlockSpec((tile, depth), lambda j, s, n: (at, 0), pipeline_mode=pl.Buffered(1)),
            pl.BlockSpec(
                (1, heads, seq), lambda j, s, n: (at, 0, 0), pipeline_mode=pl.Buffered(1)
            ),
            pl.BlockSpec(
                (3, seq, tile), lambda j, s, n: (0, 0, at), pipeline_mode=pl.Buffered(1)
            ),
            pl.BlockSpec(
                (3, depth, tile), lambda j, s, n: (0, 0, at), pipeline_mode=pl.Buffered(1)
            ),
        ]
        + ins,
        outs,
        (dattn, out_w, logsum, qkv, weight) + more,
        (scalars, lengths),
        [
            pltpu.VMEM((seq, depth), F32),
            pltpu.VMEM((2, tile), F32),
            pltpu.VMEM((seq, tile), BF),
            pltpu.VMEM((seq, tile), BF),
            pltpu.VMEM((3, seq, tile), BF),
        ],
        room=24,
    )


def grad_send_body(a_ref, b_ref, out_ref):
    out_ref[0] = dg(a_ref[...], b_ref[0], 0, 0).astype(BF)


def grad_specs(turned, right, picks, part):
    seq, units = right.shape[1:]
    half = turned.shape[1] // 2
    start, stride = picks[0], (picks[1] - picks[0] if len(picks) > 1 else 1)
    return [
        pl.BlockSpec((seq, half), lambda i: (0, part), pipeline_mode=pl.Buffered(1)),
        pl.BlockSpec((1, seq, units), lambda i: (start + stride * i, 0, 0)),
    ], pl.BlockSpec((1, half, units), lambda i: (i, 0, 0))


def grad_send(turned, right, picks):
    seq, units = right.shape[1:]
    half = turned.shape[1] // 2
    count = len(picks)
    ins, out = grad_specs(turned, right, picks, 1)
    return call(
        grad_send_body,
        "grad_send",
        (count,),
        ins,
        [(shaped((count, half, units), BF), out)],
        (turned, right),
        flops=2 * count * seq * half * units,
    )[0]


def keep_ffn_body(a_ref, b_ref, ra_ref, rb_ref, keep_ref, send_ref, own_ref, far_ref):
    i = pl.program_id(0)
    part = dg(a_ref[...], b_ref[0], 0, 0)
    cut = keep_ref.shape[1]

    @pl.when(i < 2)
    def _():
        total = (part + ra_ref[0].astype(F32)).astype(BF)
        keep_ref[0] = total[:cut]
        send_ref[0] = total[cut:]

    @pl.when(i >= 2)
    def _():
        total = (part + rb_ref[0].astype(F32)).astype(BF)

        @pl.when(i == 2)
        def _():
            own_ref[...] = total

        @pl.when(i == 3)
        def _():
            far_ref[...] = total


def keep_ffn(turned, right, got_a, got_b):
    _, seq, units = right.shape
    half = turned.shape[1] // 2
    cut = pl.BlockSpec((1, half // 2, units), lambda i: (jnp.minimum(i, 1), 0, 0))
    return call(
        keep_ffn_body,
        "keep_ffn",
        (4,),
        [
            pl.BlockSpec((seq, half), lambda i: (0, 0), pipeline_mode=pl.Buffered(1)),
            pl.BlockSpec((1, seq, units), lambda i: (send_order(i), 0, 0)),
            pl.BlockSpec((1, half, units), lambda i: (jnp.minimum(i, 1), 0, 0)),
            pl.BlockSpec((1, half, units), lambda i: (jnp.maximum(i - 2, 0), 0, 0)),
        ],
        [
            (far_shaped((2, half // 2, units), BF), cut),
            (shaped((2, half // 2, units), BF), cut),
            (far_shaped((half, units), BF), whole(half, units)),
            (shaped((half, units), BF), whole(half, units)),
        ],
        (turned, right, got_a, got_b),
        room=24,
    )


def total(*refs):
    return sum(ref.astype(F32) for ref in refs).astype(BF)


def second_body(ka_ref, ga_ref, bo_ref, gb_ref, a_own_ref, a_far_ref, b_own_ref, b_send_ref):
    a_own_ref[...] = total(ka_ref[0], ga_ref[0])
    a_far_ref[...] = total(ka_ref[1], ga_ref[1])
    half = b_own_ref.shape[0]
    b_own_ref[...] = total(bo_ref[:half], gb_ref[:half])
    b_send_ref[...] = total(bo_ref[half:], gb_ref[half:])


def second(keep_a, got_a, b_own, got_b):
    _, rows, units = keep_a.shape
    part = (shaped((rows, units), BF), whole(rows, units))
    return call(
        second_body,
        "second",
        (1,),
        [whole(2, rows, units)] * 2 + [whole(2 * rows, units)] * 2,
        [part] * 4,
        (keep_a, got_a, b_own, got_b),
        stay=(0, 2),
    )


def third_body(a_ref, ga_ref, b_ref, gb_ref, keep_ref, send_ref):
    half, units = keep_ref.shape[0], a_ref.shape[1]
    for at, (left, right) in enumerate(((a_ref, ga_ref), (b_ref, gb_ref))):
        cut = slice(at * units, (at + 1) * units)
        keep_ref[:, cut] = total(left[:half], right[:half])
        send_ref[:, cut] = total(left[half:], right[half:])


def third(a_own, got_a, b_own, got_b):
    rows, units = a_own.shape
    part = (shaped((rows // 2, 2 * units), BF), whole(rows // 2, 2 * units))
    return call(
        third_body,
        "third",
        (1,),
        [whole(rows, units)] * 4,
        [part] * 2,
        (a_own, got_a, b_own, got_b),
    )


def fourth_body(a_ref, g_ref, keep_ref, send_ref):
    half = keep_ref.shape[-2]
    keep_ref[...] = total(a_ref[..., :half, :], g_ref[..., :half, :])
    send_ref[...] = total(a_ref[..., half:, :], g_ref[..., half:, :])


def fourth(values, got):
    shape = values.shape
    out = shape[:-2] + (shape[-2] // 2, shape[-1])
    return call(
        fourth_body,
        "fourth",
        (1,),
        [whole(*shape)] * 2,
        [(shaped(out, BF), whole(*out))] * 2,
        (values, got),
    )


def keep_far_body(
    da_ref, a_ref, own_ref, oth_ref, b_ref, ro_ref, rf_ref, keep_ref, send_ref, far_ref
):
    i = pl.program_id(0)
    cut = keep_ref.shape[1]

    def split(value):
        keep_ref[0] = value[:cut]
        send_ref[0] = value[cut:]

    for side, ref in enumerate((own_ref, oth_ref)):

        @pl.when(i == side)
        def _():
            split((dg(da_ref[...], ref[...], 0, 0) + ro_ref[0].astype(F32)).astype(BF))

    @pl.when(i >= 2)
    def _():
        value = (dg(a_ref[...], b_ref[0], 0, 0) + rf_ref[0].astype(F32)).astype(BF)

        @pl.when(i == 2)
        def _():
            split(value)

        @pl.when(i > 2)
        def _():
            far_ref[0] = value


def keep_far(da_turned, turned, own, other, dqkv, got_out, got_far):
    _, seq, cols = dqkv.shape
    half = turned.shape[1] // 2
    left = pl.BlockSpec((seq, half), lambda i: (0, 0), pipeline_mode=pl.Buffered(1))
    cut = pl.BlockSpec((1, half // 2, cols), lambda i: (jnp.minimum(i, 2), 0, 0))
    return call(
        keep_far_body,
        "keep_far",
        (5,),
        [
            left,
            left,
            whole(seq, cols),
            whole(seq, cols),
            pl.BlockSpec((1, seq, cols), lambda i: (jnp.maximum(i - 2, 0), 0, 0)),
            pl.BlockSpec((1, half, cols), lambda i: (jnp.minimum(i, 1), 0, 0)),
            pl.BlockSpec((1, half, cols), lambda i: (jnp.maximum(i - 2, 0), 0, 0)),
        ],
        [
            (shaped((3, half // 2, cols), BF), cut),
            (shaped((3, half // 2, cols), BF), cut),
            (
                shaped((2, half, cols), BF),
                pl.BlockSpec((1, half, cols), lambda i: (jnp.maximum(i - 3, 0), 0, 0)),
            ),
        ],
        (da_turned, turned, own, other, dqkv, got_out, got_far),
    )


def second_attn_body(k_ref, g_ref, out_ref, far_ref):
    out_ref[0] = total(k_ref[0], g_ref[0])
    far_ref[0] = total(k_ref[2], g_ref[2])
    far_ref[1] = total(k_ref[1], g_ref[1])


def second_attn(keep, got):
    _, rows, cols = keep.shape
    return call(
        second_attn_body,
        "second_attn",
        (1,),
        [whole(3, rows, cols)] * 2,
        [(shaped((n, rows, cols), BF), whole(n, rows, cols)) for n in (1, 2)],
        (keep, got),
    )


def keep_own_body(
    a_ref, b0_ref, b1_ref, r_ref, gb_ref, keep_ref, send_ref, z_keep_ref, z_send_ref
):
    i = pl.program_id(0)
    parts = [dg(a_ref[...], ref[0], 0, 0) for ref in (b0_ref, b1_ref)]
    value = jnp.concatenate(parts, axis=1) + r_ref[0].astype(F32)
    value = jnp.where(i == 0, value, value + gb_ref[0].astype(F32)).astype(BF)
    cut = keep_ref.shape[1]

    @pl.when(i < 2)
    def _():
        keep_ref[0] = value[:cut]
        send_ref[0] = value[cut:]

    @pl.when(i == 2)
    def _():
        half = cut // 2
        for x in range(2):
            z_keep_ref[x * half : (x + 1) * half] = value[x * cut : x * cut + half]
            z_send_ref[x * half : (x + 1) * half] = value[x * cut + half : (x + 1) * cut]


def keep_own(turned, early, late, got, got_b):
    _, seq, tile = early.shape
    cols = 2 * tile
    half = turned.shape[1] // 2
    part = (
        shaped((2, half // 2, cols), BF),
        pl.BlockSpec((1, half // 2, cols), lambda i: (jnp.minimum(i, 1), 0, 0)),
    )
    flat = (shaped((half // 2, cols), BF), whole(half // 2, cols))
    return call(
        keep_own_body,
        "keep_own",
        (3,),
        [
            pl.BlockSpec((seq, half), lambda i: (0, 0), pipeline_mode=pl.Buffered(1)),
            pl.BlockSpec((1, seq, tile), lambda i: (i, 0, 0)),
            pl.BlockSpec((1, seq, tile), lambda i: (i, 0, 0)),
            pl.BlockSpec((1, half, cols), lambda i: (i, 0, 0)),
            pl.BlockSpec((1, half, cols), lambda i: (jnp.maximum(i - 1, 0), 0, 0)),
        ],
        [part, part, flat, flat],
        (turned, early, late, got, got_b),
    )


def join_attn_body(
    k_ref, x_ref, o_ref, y_ref, v_ref, z_ref, keep_ref, send_ref, v_keep_ref, v_send_ref
):
    half = keep_ref.shape[1]
    for ref, cut in ((keep_ref, slice(0, half)), (send_ref, slice(half, 2 * half))):
        ref[0] = total(k_ref[0, cut], x_ref[0, cut], y_ref[0, cut])
        ref[1] = total(k_ref[1, cut], x_ref[1, cut])
        ref[2] = total(o_ref[0, cut], y_ref[1, cut])
    v_keep_ref[...] = total(v_ref[:half], z_ref[:half])
    v_send_ref[...] = total(v_ref[half:], z_ref[half:])


def join_attn(keep, got_x, out, got_y, value, got_z):
    _, rows, cols = keep.shape
    part = (shaped((3, rows // 2, cols), BF), whole(3, rows // 2, cols))
    flat = (shaped((rows // 2, cols), BF), whole(rows // 2, cols))
    return call(
        join_attn_body,
        "join_attn",
        (1,),
        [
            whole(2, rows, cols),
            whole(2, rows, cols),
            whole(1, rows, cols),
            whole(2, rows, cols),
            whole(rows, cols),
            whole(rows, cols),
        ],
        [part, part, flat, flat],
        (keep, got_x, out, got_y, value, got_z),
    )


def last_attn_body(k_ref, z_ref, v_ref, x_ref, keep_ref, send_ref):
    half = keep_ref.shape[1]
    for ref, cut in ((keep_ref, slice(0, half)), (send_ref, slice(half, 2 * half))):
        for i in range(3):
            ref[i] = total(k_ref[i, cut], z_ref[i, cut])
        ref[3] = total(v_ref[cut], x_ref[cut])


def last_attn(keep, got_z, value, got_x):
    _, rows, cols = keep.shape
    part = (shaped((4, rows // 2, cols), BF), whole(4, rows // 2, cols))
    return call(
        last_attn_body,
        "last_attn",
        (1,),
        [whole(3, rows, cols), whole(3, rows, cols), whole(rows, cols), whole(rows, cols)],
        [part, part],
        (keep, got_z, value, got_x),
    )


def share_attn_body(k_ref, g_ref, qkv_ref, out_ref):
    for at, i in ((0, 0), (1, 1), (2, 3)):
        qkv_ref[at] = k_ref[i].astype(F32) + g_ref[i].astype(F32)
    out_ref[...] = k_ref[2].astype(F32) + g_ref[2].astype(F32)


def share_attn(keep, got):
    _, rows, cols = keep.shape
    return call(
        share_attn_body,
        "share_attn",
        (1,),
        [whole(4, rows, cols)] * 2,
        [
            (far_shaped((3, rows, cols), F32), whole(3, rows, cols)),
            (far_shaped((rows, cols), F32), whole(rows, cols)),
        ],
        (keep, got),
    )


def swap(values, bit):
    count = lax.axis_size("dp")
    return lax.ppermute(values, "dp", [(i, i ^ (1 << bit)) for i in range(count)])


def swap_y(values):
    return lax.ppermute(values, "mp", [(0, 1), (1, 0)])


def add(left, right):
    return left.astype(F32) + right.astype(F32)


def low_add(left, right):
    return add(left, right).astype(BF)


def after(value, tick):
    flat, tree = jax.tree.flatten(value)
    arrays = [i for i, leaf in enumerate(flat) if not isinstance(leaf, int)]
    held = lax.optimization_barrier(([flat[i] for i in arrays], tick))[0]
    for i, leaf in zip(arrays, held):
        flat[i] = leaf
    return jax.tree.unflatten(tree, flat)


def paged(
    tokens,
    page_lengths,
    qkv_weight,
    qv_bias,
    out_weight,
    out_bias,
    ln1_gain,
    ln1_bias,
    ff1_weight,
    ff1_bias,
    ff2_weight,
    ff2_bias,
    ln2_gain,
    ln2_bias,
    cotangent,
):
    row_count, depth = tokens.shape
    seq = row_count // 2
    cols = qkv_weight.shape[2]
    units = ff1_weight.shape[1] // 2
    group = lax.axis_index("mp")
    me = lax.axis_index("dp")

    ready = (
        jnp.stack([group, me]).astype(jnp.int32),
        1 - group,
        group,
    )
    scalars, far_page, own_page = lax.optimization_barrier(ready)

    def outer(mine, bits):
        return [mine] + [swap(mine, bit) for bit in bits]

    def rels(bits):
        one, two = (1 << bit for bit in bits)
        return (0, one, two, one | two)

    ways = ((1, 2), (2, 1), (1, 2))

    block0, out_block = pick(scalars, ff1_weight, ff2_weight, out_weight, 0)
    out_mine, mine0 = swap_y(out_block), swap_y(block0)
    far_ctx, far_lse = attn_fwd(
        far_page, page_lengths, after(tokens, block0), qkv_weight, qv_bias, False, (0, 2)
    )
    oth_ctx, oth_lse = swap_y(far_ctx), swap_y(far_lse)
    own = attn_fwd(
        own_page, page_lengths, after(tokens, far_ctx), qkv_weight, qv_bias, True, (0, 1)
    )
    out_mine = after(out_mine, own[0])
    out_x = swap(out_mine, 1)
    own_ctx, own_lse, own_qkv = attn_fwd(
        own_page, page_lengths, after(tokens, out_mine), qkv_weight, qv_bias, True, (1, 2), own
    )
    mine0 = after(mine0, own_ctx)
    by_x, by_z = swap(mine0, 1), swap(mine0, 2)
    out_near = collect([out_mine, after(out_x, mine0)])
    out_core = swap(out_near, 0)
    bias_row = after(ff1_bias, own[0]).reshape(1, -1)
    block1, qkv_block = pick(
        after(scalars, out_near), ff1_weight, ff2_weight, qkv_weight, 1, (bias_row, qv_bias)
    )
    mine1 = swap_y(block1)
    rows = [v.reshape(1, -1) for v in after((out_bias, ln1_gain, ln1_bias), out_near)]
    out_bias, ln1_gain, ln1_bias = rows
    own_ctx, by_x, by_z = lax.optimization_barrier((own_ctx, by_x, by_z))
    out_far, normed_one, scale_one, hidden, hidden_turned = join(
        scalars,
        tokens,
        own_ctx,
        after(oth_ctx, (block1, oth_lse)),
        out_weight,
        out_near,
        out_core,
        out_bias,
        ln1_gain,
        ln1_bias,
    )
    stage0 = [mine0, by_x, by_z]
    last0 = swap(by_z, 1)
    act, slope, partial = ffn_own(hidden, ff1_weight, bias_row, ff2_weight, 0, ())
    mine1, last0 = after((mine1, last0), partial)
    far_biases = mine1
    stage1 = outer(mine1, ways[1])
    act, slope, partial = ffn_own(
        hidden, ff1_weight, bias_row, ff2_weight, 1, (after(partial, mine1), act, slope)
    )
    qkv_mine = swap_y(after(qkv_block, mine1))
    stage1 = after(stage1, partial)
    rows = [v.reshape(1, -1) for v in after((ff2_bias, ln2_gain, ln2_bias), partial)]
    ff2_bias, ln2_gain, ln2_bias = rows
    last1 = swap(stage1[2], ways[1][0])
    near0 = collect(after(stage0 + [last0], stage1[2]))
    core0 = swap(near0, 0)
    act, slope, partial, w1_far, w2_far = ffn_far(
        scalars,
        hidden,
        far_biases,
        near0,
        core0,
        rels(ways[0]),
        0,
        (after(partial, rows), act, slope),
    )
    last1, qkv_mine = after((last1, qkv_mine), partial)
    near1 = collect(stage1 + [last1])
    core1 = swap(near1, 0)
    qkv_stage = outer(after(qkv_mine, near1), ways[2])
    act, slope, partial, w1_far, w2_far = ffn_far(
        scalars,
        hidden,
        far_biases,
        near1,
        core1,
        rels(ways[1]),
        1,
        (partial, act, slope, w1_far, w2_far),
    )
    out_rows, dsecond, dffn, dffn_turned, sums_two = norm_two(
        scalars,
        partial,
        normed_one,
        cotangent,
        (ln1_gain, ln1_bias, ff2_bias, ln2_gain, ln2_bias),
    )

    qkv_stage = after(qkv_stage, dffn)
    last = swap(qkv_stage[2], ways[2][0])
    send_a = grad_send(after(dffn_turned, qkv_stage[0]), act, (0, 2))
    send_b = grad_send(after(dffn_turned, send_a), act, (1, 3))
    got_a, got_b = swap(send_a, 0), swap(send_b, 0)
    keep_a, send_a, b_own, b_far = keep_ffn(after(dffn_turned, send_b), act, got_a, got_b)
    ff2_x, ff2_y = swap(send_a, 1), swap_y(b_far)
    last = after(last, keep_a)
    dpre, db, dfirst, dattn, dattn_turned, sums_one, send_a, send_b, qkv_near = ffn_back(
        scalars,
        after(dffn, last),
        ff2_weight,
        w2_far,
        slope,
        ff1_weight,
        w1_far,
        dsecond,
        normed_one,
        scale_one,
        ln1_gain,
        hidden_turned,
        qkv_stage + [last],
    )
    got_a, got_b = swap(send_a, 0), swap(send_b, 0)
    qkv_core = swap(qkv_near, 0)
    ff2_own, ff2_far, ff2_keep, ff2_send = second(after(keep_a, dattn), ff2_x, b_own, ff2_y)
    ff2_y, ff2_x = swap_y(ff2_far), swap(ff2_send, 1)
    keep_a, send_a, b_own, b_far = keep_ffn(after(hidden_turned, ff2_own), dpre, got_a, got_b)
    ff1_x, ff1_y = swap(send_a, 1), swap_y(b_far)
    dqkv_far, dqv_far, dtok, tok_turned, far_send, out_send = attn_back_other(
        scalars,
        page_lengths,
        tokens,
        after(dattn, keep_a),
        out_far,
        oth_lse,
        far_biases,
        qkv_near,
        qkv_core,
        rels(ways[2]),
        own_ctx,
        oth_ctx,
        dattn_turned,
    )
    out_got, far_got = swap(out_send, 0), swap(far_send, 0)
    ff2_keep, ff2_send = third(after(ff2_own, dtok), ff2_y, ff2_keep, ff2_x)
    ff2_z = swap(ff2_send, 2)
    ff1_own, ff1_far, ff1_keep, ff1_send = second(after(keep_a, ff2_keep), ff1_x, b_own, ff1_y)
    ff1_y, ff1_x = swap_y(ff1_far), swap(ff1_send, 1)
    far_keep, far_send, b_far = keep_far(
        after(dattn_turned, ff1_own), tok_turned, own_ctx, oth_ctx, dqkv_far, out_got, far_got
    )
    far_x, far_y = swap(far_send, 1), swap_y(b_far)
    early, dtok, early_db = attn_back_own(
        scalars,
        page_lengths,
        after(dattn, far_keep),
        out_weight,
        own_lse,
        own_qkv,
        qkv_weight,
        dtok,
        dfirst,
        last=False,
    )
    ff1_keep, ff1_send = third(after(ff1_own, dtok), ff1_y, ff1_keep, ff1_x)
    ff1_z = swap(ff1_send, 2)
    ff2_keep, ff2_send = fourth(after(ff2_keep, ff1_keep), ff2_z)
    ff2_z = swap(ff2_send, 3)
    late, small, input_grad, own_send = attn_back_own(
        scalars,
        page_lengths,
        after(dattn, ff2_keep),
        out_weight,
        own_lse,
        own_qkv,
        qkv_weight,
        dtok,
        tok_turned,
        early,
        early_db,
        db,
        dqv_far,
        sums_one,
        sums_two,
        last=True,
    )
    own_got = swap(own_send, 0)
    other = swap(small, 0)
    ff1_keep, ff1_send = fourth(after(ff1_keep, own_send), ff1_z)
    ff1_z = swap(ff1_send, 3)
    small = small + after(other, ff1_keep)
    far_keep, far_x, far_y = after((far_keep, far_x, far_y), ff1_keep)
    far_keep, ff2_z, small = lax.optimization_barrier((far_keep, ff2_z, small))
    other = swap_y(small)
    out_keep, far_send = second_attn(far_keep, far_x)
    got_y = swap_y(far_send)
    keep, send, z_keep, z_send = keep_own(
        after(tok_turned, out_keep), early, late, own_got, far_y
    )
    got_x, got_z = swap(send, 1), swap(z_send, 2)
    small = small + after(other, keep)
    small = small + swap(small, 1)
    keep, ff1_z = lax.optimization_barrier((keep, ff1_z))
    keep, send, v_keep, v_send = join_attn(
        after(keep, small), got_x, out_keep, got_y, z_keep, got_z
    )
    got_z, got_x = swap(send, 2), swap(v_send, 1)
    ff2_share = add(*after((ff2_keep, ff2_z), keep))
    other = swap(after(small, keep), 2)
    keep, send = last_attn(after(keep, ff2_share), got_z, v_keep, got_x)
    got = swap(send, 3)
    small = small + after(other, keep)
    other = swap(small, 3)
    ff1_share = add(*after((ff1_keep, ff1_z), keep))
    small = (small + after(other, ff1_share)).reshape(-1)
    ends = []
    at = 0
    for length in (4 * cols, 4 * units, depth, depth, depth, depth, depth, depth):
        ends.append(small[at : at + length])
        at += length
    ends[0] = ends[0].reshape(2, -1)
    keep, ends, ff1_share = lax.optimization_barrier((keep, ends, ff1_share))
    qkv_share, out_share = share_attn(keep, got)
    return (
        out_rows,
        input_grad,
        qkv_share,
        ends[0],
        out_share.T,
        ends[2],
        ends[3],
        ends[4],
        ff1_share,
        ends[1],
        ff2_share.T,
        ends[5],
        ends[6],
        ends[7],
    )


def suits(mesh):
    return mesh.shape["mp"] == 2 and mesh.shape["dp"] == 16


def solution(mesh):
    in_specs = (
        P("dp", None),
        P("dp"),
        P(None, None, "mp"),
        P(None, "mp"),
        P("mp", None),
        P(),
        P(),
        P(),
        P(None, "mp"),
        P("mp"),
        P("mp", None),
        P(),
        P(),
        P(),
        P("dp", None),
    )
    out_specs = (
        P(("dp", "mp"), None),
        P(("dp", "mp"), None),
        P(None, "dp", "mp"),
        P(),
        P("mp", "dp"),
        P(),
        P(),
        P(),
        P("dp", "mp"),
        P(),
        P("mp", "dp"),
        P(),
        P(),
        P(),
    )
    body = paged if suits(mesh) else local
    return jax.shard_map(body, mesh=mesh, in_specs=in_specs, out_specs=out_specs, check_vma=False)
```

```python
import functools

import jax
import jax.numpy as jnp
from jax import lax
from jax.experimental import pallas as pl
from jax.experimental.pallas import tpu as pltpu
from jax.sharding import PartitionSpec as P

HD = 64


EPSILON = 1e-05
NEGATIVE = -1e30


def normalize(values):
    center = values - jnp.mean(values, axis=-1, keepdims=True)
    spread = jnp.mean(center * center, axis=-1, keepdims=True)
    return center * lax.rsqrt(spread + EPSILON)


def gelu_exact(values):
    return jax.nn.gelu(values, approximate=False)


def over_rows(left, right):
    return lax.dot_general(
        left, right, (((0,), (0,)), ((), ())), preferred_element_type=jnp.float32
    )


def over_cols(left, right):
    return lax.dot_general(
        left, right, (((1,), (1,)), ((), ())), preferred_element_type=jnp.float32
    )


def page_scores(query, keyset, valid):
    raw = jnp.einsum("qhe,khe->hqk", query, keyset, preferred_element_type=jnp.float32) * HD ** (
        -0.5
    )
    return jnp.where(valid[None, None, :], raw, NEGATIVE)


def attend(block):
    query, keyset, valueset, valid = block
    scores = page_scores(query, keyset, valid)
    top = jnp.max(scores, axis=-1, keepdims=True)
    expo = jnp.exp(scores - top)
    total = jnp.sum(expo, axis=-1, keepdims=True)
    probs = expo / total
    context = jnp.einsum(
        "hqk,khe->qhe", probs.astype(jnp.bfloat16), valueset, preferred_element_type=jnp.float32
    )
    context = context.astype(jnp.bfloat16)
    return (context.reshape(context.shape[0], -1), top[..., 0] + jnp.log(total[..., 0]))


def attend_back(block):
    query, keyset, valueset, valid, logsum, dcontext = block
    scale = HD ** (-0.5)
    scores = page_scores(query, keyset, valid)
    probs = jnp.exp(scores - logsum[..., None])
    dprobs = jnp.einsum("qhe,khe->hqk", dcontext, valueset, preferred_element_type=jnp.float32)
    delta = jnp.sum(probs * dprobs, axis=-1, keepdims=True)
    dscores = (probs * (dprobs - delta)).astype(jnp.bfloat16)
    dquery = (
        jnp.einsum("hqk,khe->qhe", dscores, keyset, preferred_element_type=jnp.float32) * scale
    ).astype(jnp.bfloat16)
    dkeys = (
        jnp.einsum("hqk,qhe->khe", dscores, query, preferred_element_type=jnp.float32) * scale
    ).astype(jnp.bfloat16)
    dvalues = jnp.einsum(
        "hqk,qhe->khe", probs.astype(jnp.bfloat16), dcontext, preferred_element_type=jnp.float32
    ).astype(jnp.bfloat16)
    seq_len = query.shape[0]
    return (dquery.reshape(seq_len, -1), dkeys.reshape(seq_len, -1), dvalues.reshape(seq_len, -1))


def local(
    tokens,
    page_lengths,
    qkv_weight,
    qv_bias,
    out_weight,
    out_bias,
    ln1_gain,
    ln1_bias,
    ff1_weight,
    ff1_bias,
    ff2_weight,
    ff2_bias,
    ln2_gain,
    ln2_bias,
    cotangent,
):
    row_count = tokens.shape[0]
    page_count = page_lengths.shape[0]
    seq_len = row_count // page_count
    cols = qkv_weight.shape[2]
    ff_cols = ff1_weight.shape[1]
    group_heads = cols // HD
    share = row_count // lax.axis_size("mp")
    group = lax.axis_index("mp")
    share_start = group * share
    gain_one = ln1_gain.astype(jnp.float32)
    shift_one = ln1_bias.astype(jnp.float32)
    gain_two = ln2_gain.astype(jnp.float32)
    shift_two = ln2_bias.astype(jnp.float32)

    def own_rows(values):
        return lax.dynamic_slice_in_dim(values, share_start, share, 0)

    projected = jnp.einsum("rd,tdc->trc", tokens, qkv_weight, preferred_element_type=jnp.float32)
    bias_rows = jnp.stack([qv_bias[0], jnp.zeros_like(qv_bias[0]), qv_bias[1]]).astype(jnp.float32)
    qkv_rows = (projected + bias_rows[:, None, :]).astype(jnp.bfloat16)
    qkv_pages = qkv_rows.reshape(3, page_count, seq_len, group_heads, HD)
    valid = jnp.arange(seq_len)[None, :] < page_lengths[:, None]
    context, logsum = lax.map(attend, (qkv_pages[0], qkv_pages[1], qkv_pages[2], valid))
    context = context.reshape(row_count, cols)
    attn_part = jnp.dot(context, out_weight, preferred_element_type=jnp.float32).astype(
        jnp.bfloat16
    )
    attn = lax.psum(attn_part, "mp").astype(jnp.float32)
    first_sum = tokens.astype(jnp.float32) + attn + out_bias.astype(jnp.float32)
    normed_one, norm_one_back = jax.vjp(normalize, first_sum)
    hidden = normed_one * gain_one + shift_one
    hidden_low = hidden.astype(jnp.bfloat16)
    normed_one_own = own_rows(normed_one)
    pre = jnp.dot(hidden_low, ff1_weight, preferred_element_type=jnp.float32) + ff1_bias.astype(
        jnp.float32
    )
    activated, gelu_back = jax.vjp(gelu_exact, pre)
    act_low = activated.astype(jnp.bfloat16)
    ffn_part = jnp.dot(act_low, ff2_weight, preferred_element_type=jnp.float32).astype(jnp.bfloat16)
    cot_own = own_rows(cotangent).astype(jnp.float32)
    ffn = lax.psum(ffn_part, "mp").astype(jnp.float32)
    second_sum = hidden + ffn + ff2_bias.astype(jnp.float32)
    normed_two, norm_two_back = jax.vjp(normalize, second_sum)
    normed_two_own = own_rows(normed_two)
    out_rows = (normed_two_own * gain_two + shift_two).astype(jnp.bfloat16)
    dsecond = norm_two_back(cotangent.astype(jnp.float32) * gain_two)[0]
    dffn = dsecond.astype(jnp.bfloat16)
    dsecond_own = own_rows(dsecond)
    dgain_two = jnp.sum(cot_own * normed_two_own, axis=0)
    dshift_two = jnp.sum(cot_own, axis=0)
    dff2_bias = jnp.sum(dsecond_own, axis=0)
    dff2_weight = over_rows(act_low, dffn)
    dact = over_cols(dffn, ff2_weight)
    dpre = gelu_back(dact)[0].astype(jnp.bfloat16)
    dff1_bias = jnp.sum(dpre.astype(jnp.float32), axis=0)
    dff1_weight = over_rows(hidden_low, dpre)
    dhid_part = over_cols(dpre, ff1_weight).astype(jnp.bfloat16)
    dhidden = dsecond + lax.psum(dhid_part, "mp").astype(jnp.float32)
    dfirst = norm_one_back(dhidden * gain_one)[0]
    dattn = dfirst.astype(jnp.bfloat16)
    dhidden_own = own_rows(dhidden)
    dfirst_own = own_rows(dfirst)
    dgain_one = jnp.sum(dhidden_own * normed_one_own, axis=0)
    dshift_one = jnp.sum(dhidden_own, axis=0)
    dout_bias = jnp.sum(dfirst_own, axis=0)
    dout_weight = over_rows(context, dattn)
    dcontext = over_cols(dattn, out_weight).astype(jnp.bfloat16)
    dcontext_pages = dcontext.reshape(page_count, seq_len, group_heads, HD)
    dquery, dkeys, dvalues = lax.map(
        attend_back, (qkv_pages[0], qkv_pages[1], qkv_pages[2], valid, logsum, dcontext_pages)
    )
    dqkv = jnp.stack(
        [
            dquery.reshape(row_count, cols),
            dkeys.reshape(row_count, cols),
            dvalues.reshape(row_count, cols),
        ]
    )
    dqv_bias = jnp.stack(
        [jnp.sum(dqkv[0].astype(jnp.float32), axis=0), jnp.sum(dqkv[2].astype(jnp.float32), axis=0)]
    )
    dqkv_weight = jnp.einsum("rd,trc->tdc", tokens, dqkv, preferred_element_type=jnp.float32)
    dtok_part = jnp.einsum(
        "trc,tdc->rd", dqkv, qkv_weight, preferred_element_type=jnp.float32
    ).astype(jnp.bfloat16)
    input_grad = (
        dfirst_own
        + lax.psum_scatter(dtok_part, "mp", scatter_dimension=0, tiled=True).astype(jnp.float32)
    ).astype(jnp.bfloat16)
    qkv_share, out_share, ff1_share, ff2_share = (
        lax.psum_scatter(
            dqkv_weight.astype(jnp.bfloat16), "dp", scatter_dimension=1, tiled=True
        ).astype(jnp.float32),
        lax.psum_scatter(
            dout_weight.astype(jnp.bfloat16), "dp", scatter_dimension=1, tiled=True
        ).astype(jnp.float32),
        lax.psum_scatter(
            dff1_weight.astype(jnp.bfloat16), "dp", scatter_dimension=0, tiled=True
        ).astype(jnp.float32),
        lax.psum_scatter(
            dff2_weight.astype(jnp.bfloat16), "dp", scatter_dimension=1, tiled=True
        ).astype(jnp.float32),
    )
    qv_placed = lax.dynamic_update_slice_in_dim(
        jnp.zeros((2, cols * lax.axis_size("mp")), jnp.float32), dqv_bias, group * cols, 1
    )
    ff1_placed = lax.dynamic_update_slice_in_dim(
        jnp.zeros((ff_cols * lax.axis_size("mp"),), jnp.float32), dff1_bias, group * ff_cols, 0
    )
    small = lax.psum(
        (qv_placed, dout_bias, dgain_one, dshift_one, ff1_placed, dff2_bias, dgain_two, dshift_two),
        ("dp", "mp"),
    )
    return (
        out_rows,
        input_grad,
        qkv_share,
        small[0],
        out_share,
        small[1],
        small[2],
        small[3],
        ff1_share,
        small[4],
        ff2_share,
        small[5],
        small[6],
        small[7],
    )


BF = jnp.bfloat16
F32 = jnp.float32
ROOT_HALF = 2**-0.5
ROOT_TAU = 0.3989422804014327


def dg(left, right, left_dim, right_dim):
    return lax.dot_general(
        left, right, (((left_dim,), (right_dim,)), ((), ())), preferred_element_type=F32
    )


def whole(*shape):
    return pl.BlockSpec(shape, lambda *at: (0,) * len(shape), pipeline_mode=pl.Buffered(1))


def shaped(shape, dtype):
    return jax.ShapeDtypeStruct(shape, dtype)


def far_shaped(shape, dtype):
    return pltpu.HBM(shape, dtype)


TIMES = {
    "attn_fwd": 5,
    "pick": 2,
    "collect": 1,
    "attn_join": 5,
    "ffn_own": 3,
    "ffn_far": 5,
    "norm_two": 5,
    "grad_send": 3,
    "keep_ffn": 3,
    "ffn_back": 24,
    "second": 1000,
    "third": 1,
    "attn_back_other": 20,
    "fourth": 1,
    "keep_far": 5,
    "attn_back_own": 9,
    "second_attn": 1000,
    "keep_own": 2,
    "join_attn": 2,
    "last_attn": 1,
    "share_attn": 1,
}


def call(body, name, grid, ins, outs, args, scalars=(), scratch=(), aliases=None, flops=0, room=20, stay=()):
    args = [
        pltpu.with_memory_space_constraint(a, pltpu.HBM) if i in stay else a
        for i, a in enumerate(args)
    ]
    return pl.pallas_call(
        body,
        out_shape=[s for s, _ in outs],
        grid_spec=pltpu.PrefetchScalarGridSpec(
            num_scalar_prefetch=len(scalars),
            grid=grid,
            in_specs=ins,
            out_specs=[s for _, s in outs],
            scratch_shapes=list(scratch),
        ),
        input_output_aliases=aliases or {},
        cost_estimate=pl.CostEstimate(
            flops=TIMES[name] * 10**9, bytes_accessed=0, transcendentals=0
        ),
        name=name,
        compiler_params=pltpu.CompilerParams(vmem_limit_bytes=room * 2**20),
    )(*scalars, *args)


def permute_columns(source, target, me, rows):
    low = me & 1
    high = me >> 1
    size = min(rows, 128)
    lane = lax.broadcasted_iota(jnp.int32, (size, 128), 1)
    half = target.shape[1] // 2

    @pl.loop(0, rows // size)
    def _(i):
        at = pl.ds(pl.multiple_of(i * size, size), size)
        for u in range(4):
            blocks = []
            for z in range(2):
                rel = z * 4 + (u & 1) * 2 + (u >> 1)
                start = pl.multiple_of((rel ^ high) * 128, 128)
                blocks.append(source[at, pl.ds(start, 128)])
            turned = [pltpu.roll(block, 64, 1) for block in blocks]
            near = jnp.where(lane < 64, blocks[0], turned[1])
            far = jnp.where(lane < 64, turned[0], blocks[1])
            first = jnp.where(low == 0, near, far)
            second = jnp.where(low == 0, far, near)
            target[at, u * 128 : (u + 1) * 128] = first.astype(BF)
            target[at, half + u * 128 : half + (u + 1) * 128] = second.astype(BF)


def attn_fwd_body(s_ref, len_ref, x_ref, w_ref, b_ref, *outs, keep_rows, skip):
    q_ref, k_ref, v_ref = outs[-3:]
    ctx_ref, lse_ref = outs[skip : skip + 2]
    count = len_ref[s_ref[0]]
    x = x_ref[...]
    seq = x.shape[0]
    query = (dg(x, w_ref[0], 1, 0) + b_ref[0:1, :].astype(F32)).astype(BF)
    k_ref[...] = dg(x, w_ref[1], 1, 0).astype(BF)
    v_ref[...] = (dg(x, w_ref[2], 1, 0) + b_ref[1:2, :].astype(F32)).astype(BF)
    if keep_rows:
        outs[skip + 2][0] = query
        outs[skip + 2][1] = k_ref[...]
        outs[skip + 2][2] = v_ref[...]
    q_ref[...] = query * BF(HD**-0.5)
    first = lax.broadcasted_iota(jnp.int32, (seq, 2 * HD), 1) < HD
    valid = lax.broadcasted_iota(jnp.int32, (seq, seq), 0) < count

    for pair in range(query.shape[1] // (2 * HD)):
        cut = slice(pair * 2 * HD, (pair + 1) * 2 * HD)
        q_pair, k_pair = q_ref[:, cut], k_ref[:, cut]
        turned = v_ref[:, cut].T
        parts = []
        for h in range(2):
            own = jnp.where(first if h == 0 else ~first, q_pair, BF(0))
            scores = jnp.where(valid, dg(k_pair, own, 1, 1), NEGATIVE)
            top = jnp.max(scores, axis=0, keepdims=True)
            expo = jnp.exp(scores - top)
            total = jnp.sum(expo, axis=0, keepdims=True)
            part = dg(turned[h * HD : (h + 1) * HD], expo.astype(BF), 1, 0)
            parts.append(part * (1.0 / total))
            lse_ref[0, pair * 2 + h : pair * 2 + h + 1, :] = top + jnp.log(total)
        ctx_ref[:, cut] = jnp.concatenate(parts, axis=0).T.astype(BF)


def attn_fwd(page, lengths, tokens, weight, bias, keep_rows, tiles, before=()):
    depth = tokens.shape[1]
    seq = tokens.shape[0] // lengths.shape[0]
    cols = weight.shape[2]
    tile = 256
    heads = tile // HD
    start, stop = tiles
    outs = [
        (shaped((seq, cols), BF), pl.BlockSpec((seq, tile), lambda j, s, n: (0, start + j))),
        (
            shaped((cols // tile, heads, seq), F32),
            pl.BlockSpec((1, heads, seq), lambda j, s, n: (start + j, 0, 0)),
        ),
    ]
    if keep_rows:
        outs.append(
            (
                far_shaped((3, seq, cols), BF),
                pl.BlockSpec((3, seq, tile), lambda j, s, n: (0, 0, start + j)),
            )
        )
    return call(
        functools.partial(attn_fwd_body, keep_rows=keep_rows, skip=len(before)),
        "attn_fwd",
        (stop - start,),
        [
            pl.BlockSpec((seq, depth), lambda j, s, n: (s[0], 0)),
            pl.BlockSpec((3, depth, tile), lambda j, s, n: (0, 0, start + j)),
            pl.BlockSpec((2, tile), lambda j, s, n: (0, start + j)),
            *[pl.BlockSpec(memory_space=pl.ANY)] * len(before),
        ],
        outs,
        (tokens, weight, bias, *before),
        (page.reshape(1), lengths),
        [pltpu.VMEM((seq, tile), BF)] * 3,
        stay=(1,),
        aliases={5 + i: i for i in range(len(before))},
    )


def join_body(s_ref, x_ref, own_ref, oth_ref, w_ref, near_ref, core_ref, *refs):
    bias_ref, gain_ref, shift_ref = refs[:3]
    far_ref, normed_ref, scale_ref, low_ref, perm_ref, wide = refs[3:]
    me = s_ref[1]

    @pl.when(pl.program_id(0) == 0)
    def _():
        size = near_ref.shape[1]
        for i in range(2):
            for flip, stack in ((0, near_ref), (1, core_ref)):
                at = pl.multiple_of(((me & 3) ^ (2 * i) ^ flip) * size, 16)
                far_ref[pl.ds(at, size), :] = stack[i]

    attn = dg(own_ref[...], w_ref[...], 1, 0) + dg(oth_ref[...], far_ref[...], 1, 0)
    total = x_ref[...].astype(F32) + attn + bias_ref[...].astype(F32)
    center = total - jnp.mean(total, axis=-1, keepdims=True)
    scale = lax.rsqrt(jnp.mean(center * center, axis=-1, keepdims=True) + EPSILON)
    normed = center * scale
    normed_ref[...] = normed
    scale_ref[...] = scale
    hidden = normed * gain_ref[...].astype(F32) + shift_ref[...].astype(F32)
    low_ref[...] = hidden.astype(BF)
    wide[...] = hidden
    permute_columns(wide, perm_ref, me, wide.shape[0])


def join(scalars, tokens, own, other, weight, near, core, bias, gain, shift):
    seq, cols = own.shape
    depth = tokens.shape[1]
    steps = 2
    rows = seq // steps
    row = pl.BlockSpec((rows, depth), lambda i, s: (i, 0))
    half = pl.BlockSpec((rows, cols), lambda i, s: (i, 0))
    return call(
        join_body,
        "attn_join",
        (steps,),
        [
            pl.BlockSpec((rows, depth), lambda i, s: (s[0] * steps + i, 0)),
            half,
            half,
            whole(cols, depth),
            whole(*near.shape),
            whole(*near.shape),
            *[whole(1, depth)] * 3,
        ],
        [
            (far_shaped((cols, depth), BF), whole(cols, depth)),
            (far_shaped((seq, depth), F32), row),
            (shaped((seq, 1), F32), pl.BlockSpec((rows, 1), lambda i, s: (i, 0))),
            (shaped((seq, depth), BF), row),
            (far_shaped((seq, depth), BF), row),
        ],
        (
            tokens,
            own,
            other,
            weight,
            near,
            core,
            bias,
            gain,
            shift,
        ),
        (scalars,),
        [pltpu.VMEM((rows, depth), F32)],
        flops=4 * seq * cols * depth,
    )


def ffn_tile(h_ref, w_one, bias, w_two, act_ref, slope_ref):
    pre = dg(h_ref[...], w_one, 1, 0) + bias
    phi = 0.5 + 0.5 * lax.erf(pre * F32(ROOT_HALF))
    act = (pre * phi).astype(BF)
    act_ref[0] = act
    slope_ref[0] = (phi + pre * (jnp.exp(-0.5 * pre * pre) * F32(ROOT_TAU))).astype(BF)
    return dg(act, w_two, 1, 0)


TILE = 512


def start_sum(sum_ref, in_ref):
    @pl.when(pl.program_id(0) == 0)
    def _():
        sum_ref[...] = jnp.zeros_like(sum_ref) if in_ref is None else in_ref[...]


def ffn_own_body(h_ref, w1_ref, b_ref, w2_ref, *refs):
    act_ref, slope_ref, sum_ref = refs[-3:]
    start_sum(sum_ref, refs[0] if len(refs) > 3 else None)
    bias = b_ref[...].astype(F32)
    sum_ref[...] += ffn_tile(h_ref, w1_ref[...], bias, w2_ref[...], act_ref, slope_ref)


def ffn_own(hidden, w_one, bias, w_two, g, before):
    seq, depth = hidden.shape
    units = w_one.shape[1] // 2
    steps = units // TILE
    base = g * steps
    side = pl.BlockSpec((1, seq, TILE), lambda j: (g, 0, j))
    full = whole(seq, depth)
    hbm = pl.BlockSpec(memory_space=pl.ANY)
    return call(
        ffn_own_body,
        "ffn_own",
        (steps,),
        [
            full,
            pl.BlockSpec((depth, TILE), lambda j: (0, base + j)),
            pl.BlockSpec((1, TILE), lambda j: (0, base + j)),
            pl.BlockSpec((TILE, depth), lambda j: (base + j, 0)),
        ]
        + ([full, hbm, hbm] if before else []),
        [
            (shaped((4, seq, units), BF), side),
            (far_shaped((4, seq, units), BF), side),
            (shaped((seq, depth), F32), full),
        ],
        (hidden, w_one, bias, w_two) + before,
        aliases={4: 2, 5: 0, 6: 1} if before else None,
        stay=(1, 3),
    )


def pick_body(s_ref, one_ref, two_ref, more_ref, *refs):
    ffn_ref, out_ref = refs[-2:]
    size = one_ref.shape[0]
    ffn_ref[:size] = one_ref[...]
    ffn_ref[size : 2 * size] = two_ref[...]
    out_ref[...] = more_ref[...]
    if len(refs) > 2:
        low_ref, qv_ref = refs[:2]
        depth = ffn_ref.shape[1]
        lines = [low_ref[:, i * depth : (i + 1) * depth] for i in range(2)]
        lines.append(jnp.concatenate([qv_ref[i : i + 1] for i in range(2)], axis=1))
        lines.append(jnp.zeros((16 - len(lines), depth), BF))
        ffn_ref[2 * size :] = jnp.concatenate(lines, axis=0)


def pick(scalars, ff1_weight, ff2_weight, more, g, biases=()):
    depth, units = ff1_weight.shape[0], ff1_weight.shape[1] // 2
    size = depth // 8
    if more.ndim == 2:
        shape = (more.shape[0] // 4, more.shape[1])
        spec = pl.BlockSpec(shape, lambda i, s: (s[1] & 3, 0))
    else:
        shape = (more.shape[0], more.shape[1] // 8, more.shape[2])
        spec = pl.BlockSpec(shape, lambda i, s: (0, s[1] & 7, 0))
    rows = 2 * size + (16 if biases else 0)
    return call(
        pick_body,
        "pick",
        (1,),
        [
            pl.BlockSpec((size, units), lambda i, s: (s[1] & 7, g)),
            pl.BlockSpec((units // 8, depth), lambda i, s: (g * 8 + (s[1] & 7), 0)),
            spec,
            *[whole(*bias.shape) for bias in biases],
        ],
        [
            (shaped((rows, units), BF), whole(rows, units)),
            (shaped(shape, BF), whole(*shape)),
        ],
        (ff1_weight, ff2_weight, more, *biases),
        (scalars,),
        stay=(0, 1, 2),
    )


def collect_body(*refs):
    for i, piece in enumerate(refs[:-1]):
        refs[-1][i] = piece[...]


def collect(pieces):
    shape = pieces[0].shape
    return call(
        collect_body,
        "collect",
        (1,),
        [whole(*shape)] * len(pieces),
        [(shaped((len(pieces),) + shape, BF), whole(len(pieces), *shape))],
        tuple(pieces),
    )[0]


def ffn_far_body(
    s_ref, h_ref, b_ref, near_ref, core_ref, near2_ref, core2_ref, in_ref, *refs, rels, row
):
    act_ref, slope_ref, sum_ref, w1_ref, w2_ref = refs[-5:]
    j = pl.program_id(0)
    me = s_ref[1]

    def put(target, near, core):
        size = near.shape[1]
        for i, rel in enumerate(rels):
            for flip, stack in ((0, near), (1, core)):
                at = pl.multiple_of(((me & 7) ^ rel ^ flip) * size, 16)
                target[pl.ds(at, size), :] = stack[i]

    @pl.when(j == 0)
    def _():
        put(w2_ref, near2_ref, core2_ref)

    put(w1_ref, near_ref, core_ref)
    w_two = w2_ref[pl.ds(pl.multiple_of(j * TILE, TILE), TILE), :]
    start_sum(sum_ref, in_ref)
    bias = b_ref[row : row + 1, :].astype(F32)
    sum_ref[...] += ffn_tile(h_ref, w1_ref[...], bias, w_two, act_ref, slope_ref)


def ffn_far(scalars, hidden, bias, near, core, rels, g, before):
    seq, depth = hidden.shape
    units = before[1].shape[2]
    steps = units // TILE
    size = depth // 8
    side = pl.BlockSpec((1, seq, TILE), lambda j, s: (2 + g, 0, j))
    full = whole(seq, depth)
    hbm = pl.BlockSpec(memory_space=pl.ANY)
    one = pl.BlockSpec((4, size, TILE), lambda j, s: (0, 0, j))
    two = pl.BlockSpec(
        (4, size, depth), lambda j, s: (0, 1, 0), pipeline_mode=pl.Buffered(1)
    )
    args = (hidden, bias, near, core, near, core, *before)
    return call(
        functools.partial(ffn_far_body, rels=rels, row=g),
        "ffn_far",
        (steps,),
        [
            full,
            pl.BlockSpec((16, TILE), lambda j, s: (bias.shape[0] // 16 - 1, j)),
            one,
            one,
            two,
            two,
            full,
            *[hbm] * (len(before) - 1),
        ],
        [
            (shaped((4, seq, units), BF), side),
            (far_shaped((4, seq, units), BF), side),
            (shaped((seq, depth), F32), full),
            (
                far_shaped((depth, 2 * units), BF),
                pl.BlockSpec((depth, TILE), lambda j, s: (0, g * steps + j)),
            ),
            (
                far_shaped((2 * units, depth), BF),
                pl.BlockSpec((units, depth), lambda j, s: (g, 0), pipeline_mode=pl.Buffered(1)),
            ),
        ],
        args,
        (scalars,),
        aliases={7: 2, 8: 0, 9: 1} | ({10: 3, 11: 4} if g else {}),
        flops=4 * seq * depth * units,
    )


def norm_back(grad, normed, scale):
    return scale * (
        grad
        - jnp.mean(grad, axis=-1, keepdims=True)
        - normed * jnp.mean(grad * normed, axis=-1, keepdims=True)
    )


CHUNK = 64


def chunked(rows, sums_ref, chunk):
    zero = jnp.zeros((1, sums_ref.shape[1]), F32)

    def step(i, sums):
        news = chunk(pl.ds(pl.multiple_of(i * CHUNK, CHUNK), CHUNK))
        return tuple(
            old + jnp.sum(new, axis=0, keepdims=True) for old, new in zip(sums, news)
        )

    sums = lax.fori_loop(0, rows // CHUNK, step, (zero, zero, zero), unroll=True)
    first = pl.program_id(0) == 0
    for i in range(3):
        old = sums_ref[i : i + 1, :]
        sums_ref[i : i + 1, :] = jnp.where(first, 0.0, old) + sums[i]


def norm_two_body(
    s_ref, in_ref, normed_ref, cot_ref, *refs
):
    gain_one, shift_one, bias, gain, shift = [ref[...].astype(F32) for ref in refs[:5]]
    out_ref, ds_ref, df_ref, perm_ref, sums_ref = refs[5:]

    def chunk(at):
        total = normed_ref[at, :] * gain_one + shift_one + in_ref[at, :] + bias
        center = total - jnp.mean(total, axis=-1, keepdims=True)
        scale = lax.rsqrt(jnp.mean(center * center, axis=-1, keepdims=True) + EPSILON)
        normed = center * scale
        out_ref[at, :] = (normed * gain + shift).astype(BF)
        cot = cot_ref[at, :].astype(F32)
        ds = norm_back(cot * gain, normed, scale)
        ds_ref[at, :] = ds
        df_ref[at, :] = ds.astype(BF)
        return ds, cot * normed, cot

    rows = in_ref.shape[0]
    chunked(rows, sums_ref, chunk)
    permute_columns(ds_ref, perm_ref, s_ref[1], rows)


def norm_two(scalars, total, normed, cotangent, vectors):
    seq, depth = total.shape
    steps = 4
    row = pl.BlockSpec((seq // steps, depth), lambda i, s: (i, 0))
    return call(
        norm_two_body,
        "norm_two",
        (steps,),
        [
            row,
            row,
            pl.BlockSpec((seq // steps, depth), lambda i, s: (s[0] * steps + i, 0)),
            *[whole(1, depth)] * 5,
        ],
        [
            (far_shaped((seq, depth), BF), row),
            (shaped((seq, depth), F32), row),
            (shaped((seq, depth), BF), row),
            (shaped((seq, depth), BF), row),
            (shaped((8, depth), F32), pl.BlockSpec((8, depth), lambda i, s: (0, 0))),
        ],
        (total, normed, cotangent, *vectors),
        (scalars,),
        stay=(1, 2),
        flops=40 * seq * depth,
    )


def send_order(i):
    return (i % 2) * 2 + i // 2


def ffn_back_body(
    s_ref,
    df_ref,
    w2_ref,
    w2_far_ref,
    slope_ref,
    w1_ref,
    w1_far_ref,
    ds_ref,
    normed_ref,
    scale_ref,
    gain_ref,
    turned_ref,
    *refs,
    tiles,
):
    pieces = refs[:4]
    dpre_ref, db_ref, first_ref, low_ref, perm_ref, sums_ref = refs[4:10]
    send_a_ref, send_b_ref, near_ref, wide = refs[10:]
    j = pl.program_id(0)
    per = dpre_ref.shape[2] // TILE

    @pl.when(j == 1)
    def _():
        for i, piece in enumerate(pieces):
            near_ref[i] = piece[...]

    @pl.when(j == 0)
    def _():
        wide[...] = ds_ref[...]

    def tile(w_two, w_one):
        dact = dg(df_ref[...], w_two[...], 1, 1)
        dpre = (dact * slope_ref[0].astype(F32)).astype(BF)
        dpre_ref[j // per, :, pl.ds(pl.multiple_of((j % per) * TILE, TILE), TILE)] = dpre
        db_ref[...] = jnp.sum(dpre.astype(F32), axis=0, keepdims=True)
        wide[...] += dg(dpre, w_one[...], 1, 1)

    pl.when(j < tiles // 2)(functools.partial(tile, w2_ref, w1_ref))
    pl.when((j >= tiles // 2) & (j < tiles))(functools.partial(tile, w2_far_ref, w1_far_ref))

    @pl.when(j == tiles - 1)
    def _():
        gain = gain_ref[...].astype(F32)
        zero = jnp.zeros((1, gain.shape[1]), F32)

        def step(i, sums):
            at = pl.ds(pl.multiple_of(i * CHUNK, CHUNK), CHUNK)
            grad = wide[at, :]
            normed = normed_ref[at, :]
            first = norm_back(grad * gain, normed, scale_ref[at, :])
            first_ref[at, :] = first
            low_ref[at, :] = first.astype(BF)
            return tuple(
                old + jnp.sum(new, axis=0, keepdims=True)
                for old, new in zip(sums, (first, grad * normed, grad))
            )

        rows = wide.shape[0]
        sums = lax.fori_loop(0, rows // CHUNK, step, (zero, zero, zero), unroll=2)
        for i in range(3):
            sums_ref[i : i + 1, :] = sums[i]
        permute_columns(first_ref, perm_ref, s_ref[1], rows)

    @pl.when(j >= tiles)
    def _():
        part = dg(turned_ref[...], dpre_ref[send_order(j - tiles)], 0, 0).astype(BF)

        @pl.when(j < tiles + 2)
        def _():
            send_a_ref[0] = part

        @pl.when(j >= tiles + 2)
        def _():
            send_b_ref[0] = part


def ffn_back(
    scalars,
    dffn,
    w_two,
    w_two_far,
    slope,
    w_one,
    w_one_far,
    dsecond,
    normed,
    scale,
    gain,
    turned,
    pieces,
):
    seq, depth = dffn.shape
    units = slope.shape[2]
    steps = units // TILE
    half = 2 * steps
    tiles = 2 * half
    full = whole(seq, depth)

    def near(j):
        return jnp.minimum(j, half - 1)

    def far(j):
        return jnp.clip(j - half, 0, half - 1)

    def last(j):
        return jnp.minimum(j, tiles - 1)

    def send(first):
        return pl.BlockSpec(
            (1, depth // 2, units), lambda j, s: (jnp.clip(j - first, 0, 1), 0, 0)
        )

    return call(
        functools.partial(ffn_back_body, tiles=tiles),
        "ffn_back",
        (tiles + 4,),
        [
            full,
            pl.BlockSpec((TILE, depth), lambda j, s: (near(j), 0)),
            pl.BlockSpec((TILE, depth), lambda j, s: (far(j), 0)),
            pl.BlockSpec((1, seq, TILE), lambda j, s: (last(j) // steps, 0, last(j) % steps)),
            pl.BlockSpec((depth, TILE), lambda j, s: (0, near(j))),
            pl.BlockSpec((depth, TILE), lambda j, s: (0, far(j))),
            full,
            full,
            whole(seq, 1),
            whole(1, depth),
            pl.BlockSpec((seq, depth // 2), lambda j, s: (0, 1), pipeline_mode=pl.Buffered(1)),
            *[whole(*pieces[0].shape)] * 4,
        ],
        [
            (shaped((4, seq, units), BF), whole(4, seq, units)),
            (shaped((1, 4 * units), F32), pl.BlockSpec((1, TILE), lambda j, s: (0, last(j)))),
            (far_shaped((seq, depth), F32), full),
            (shaped((seq, depth), BF), full),
            (shaped((seq, depth), BF), full),
            (shaped((8, depth), F32), whole(8, depth)),
            (shaped((2, depth // 2, units), BF), send(tiles)),
            (shaped((2, depth // 2, units), BF), send(tiles + 2)),
            (shaped((4,) + pieces[0].shape, BF), whole(4, *pieces[0].shape)),
        ],
        (
            dffn,
            w_two,
            w_two_far,
            slope,
            w_one,
            w_one_far,
            dsecond,
            normed,
            scale,
            gain,
            turned,
            *pieces,
        ),
        (scalars,),
        [pltpu.VMEM((seq, depth), F32)],
        room=36,
        stay=(1, 2, 3, 4, 5, 7, 10),
    )


def attn_back_tile(j, count, refs, lse_ref, dc_ref, out_ref, dqkv_ref, db_ref):
    q_ref, k_ref, v_ref = refs
    seq, size = q_ref.shape
    first = lax.broadcasted_iota(jnp.int32, (seq, 2 * HD), 1) < HD
    valid = lax.broadcasted_iota(jnp.int32, (seq, seq), 0) < count

    @pl.loop(0, size // (2 * HD))
    def _(pair):
        cut = pl.ds(pl.multiple_of(pair * 2 * HD, 2 * HD), 2 * HD)
        q_pair, k_pair, v_pair, dc_pair = q_ref[:, cut], k_ref[:, cut], v_ref[:, cut], dc_ref[:, cut]
        dquery = dkeys = dvalues = 0.0
        for h in range(2):
            mask = first if h == 0 else ~first
            q_own = jnp.where(mask, q_pair, BF(0))
            k_own = jnp.where(mask, k_pair, BF(0))
            dc_own = jnp.where(mask, dc_pair, BF(0))
            scores = dg(k_pair, q_own, 1, 1) - lse_ref[0, pl.ds(pair * 2 + h, 1), :]
            probs = jnp.exp(jnp.where(valid, scores, NEGATIVE))
            dprobs = dg(v_pair, dc_own, 1, 1)
            delta = jnp.sum(probs * dprobs, axis=0, keepdims=True)
            dscores = (probs * (dprobs - delta)).astype(BF)
            dvalues = dvalues + dg(probs.astype(BF), dc_own, 1, 0)
            dkeys = dkeys + dg(dscores, q_own, 1, 0)
            dquery = dquery + dg(dscores, k_own, 0, 0)
        out_ref[0, :, cut] = (dquery * HD**-0.5).astype(BF)
        out_ref[1, :, cut] = dkeys.astype(BF)
        out_ref[2, :, cut] = dvalues.astype(BF)

    for t in range(3):
        dqkv_ref[t, :, pl.ds(pl.multiple_of(j * size, size), size)] = out_ref[t]
    db_ref[0:1, :] = jnp.sum(out_ref[0].astype(F32), axis=0, keepdims=True)
    db_ref[1:2, :] = jnp.sum(out_ref[2].astype(F32), axis=0, keepdims=True)


def attn_back_other_body(
    s_ref,
    len_ref,
    x_ref,
    da_ref,
    wo_ref,
    lse_ref,
    qb_ref,
    vb_ref,
    near_ref,
    core_ref,
    own_ref,
    oth_ref,
    da_turned_ref,
    dqkv_ref,
    db_ref,
    sum_ref,
    turned_ref,
    far_send_ref,
    out_send_ref,
    w_ref,
    wide,
    q_ref,
    k_ref,
    v_ref,
    dc_ref,
    out_ref,
    *,
    rels,
    tiles,
):
    j = pl.program_id(0)
    me = s_ref[1]
    half = turned_ref.shape[1] // 2

    @pl.when(j < tiles)
    def _():
        size = near_ref.shape[2]
        for i, rel in enumerate(rels):
            for flip, stack in ((0, near_ref), (1, core_ref)):
                at = pl.multiple_of(((me & 7) ^ rel ^ flip) * size, 16)
                w_ref[:, pl.ds(at, size), :] = stack[i]
        x = x_ref[...]
        query = (dg(x, w_ref[0], 1, 0) + qb_ref[2:3, :].astype(F32)).astype(BF)
        q_ref[...] = query * BF(HD**-0.5)
        k_ref[...] = dg(x, w_ref[1], 1, 0).astype(BF)
        v_ref[...] = (dg(x, w_ref[2], 1, 0) + vb_ref[2:3, :].astype(F32)).astype(BF)
        dc_ref[...] = dg(da_ref[...], wo_ref[...], 1, 1).astype(BF)
        count = len_ref[s_ref[0]]
        refs = (q_ref, k_ref, v_ref)
        attn_back_tile(j, count, refs, lse_ref, dc_ref, out_ref, dqkv_ref, db_ref)
        start_sum(sum_ref, None)
        for t in range(3):
            sum_ref[...] += dg(out_ref[t], w_ref[t], 1, 1)

    @pl.when(j == 0)
    def _():
        wide[...] = x_ref[...].astype(F32)
        permute_columns(wide, turned_ref, me, x_ref.shape[0])

    @pl.when((j >= tiles) & (j < tiles + 3))
    def _():
        right = dqkv_ref[jnp.clip(j - tiles, 0, 2)]
        far_send_ref[0] = dg(turned_ref[:, half:], right, 0, 0).astype(BF)

    for side, ref in enumerate((own_ref, oth_ref)):

        @pl.when(j == tiles + 3 + side)
        def _():
            out_send_ref[0] = dg(da_turned_ref[...], ref[...], 0, 0).astype(BF)


def attn_back_other(
    scalars, lengths, tokens, dattn, out_w, logsum, bias, near, core, rels, own, other, da_turned
):
    seq, depth = dattn.shape
    cols = out_w.shape[0]
    tile = 256
    heads = tile // HD
    tiles = cols // tile
    half = depth // 2
    ahead = bias.shape[0] // 16 - 1

    def at(j):
        return jnp.minimum(j, tiles - 1)

    stack = pl.BlockSpec((4, 3, depth // 8, tile), lambda j, s, n: (0, 0, 0, at(j)))
    return call(
        functools.partial(attn_back_other_body, rels=rels, tiles=tiles),
        "attn_back_other",
        (tiles + 5,),
        [
            pl.BlockSpec((seq, depth), lambda j, s, n: (s[0], 0)),
            whole(seq, depth),
            pl.BlockSpec((tile, depth), lambda j, s, n: (at(j), 0)),
            pl.BlockSpec((1, heads, seq), lambda j, s, n: (at(j), 0, 0)),
            pl.BlockSpec((16, tile), lambda j, s, n: (ahead, at(j))),
            pl.BlockSpec((16, tile), lambda j, s, n: (ahead, tiles + at(j))),
            stack,
            stack,
            whole(seq, cols),
            whole(seq, cols),
            pl.BlockSpec((seq, half), lambda j, s, n: (0, 1), pipeline_mode=pl.Buffered(1)),
        ],
        [
            (shaped((3, seq, cols), BF), whole(3, seq, cols)),
            (shaped((2, cols), F32), pl.BlockSpec((2, tile), lambda j, s, n: (0, at(j)))),
            (far_shaped((seq, depth), F32), whole(seq, depth)),
            (shaped((seq, depth), BF), whole(seq, depth)),
            (
                shaped((3, half, cols), BF),
                pl.BlockSpec((1, half, cols), lambda j, s, n: (jnp.clip(j - tiles, 0, 2), 0, 0)),
            ),
            (
                shaped((2, half, cols), BF),
                pl.BlockSpec(
                    (1, half, cols), lambda j, s, n: (jnp.clip(j - tiles - 3, 0, 1), 0, 0)
                ),
            ),
        ],
        (tokens, dattn, out_w, logsum, bias, bias, near, core, own, other, da_turned),
        (scalars, lengths),
        [pltpu.VMEM((3, depth, tile), BF), pltpu.VMEM((seq, depth), F32)]
        + [pltpu.VMEM((seq, tile), BF)] * 4
        + [pltpu.VMEM((3, seq, tile), BF)],
        room=30,
        stay=(0, 2),
    )


def attn_back_own_body(
    s_ref, len_ref, da_ref, wo_ref, lse_ref, qkv_ref, w_ref, *refs, last
):
    (wide, db_ref, q_ref, dc_ref, out_ref) = refs[-5:]
    j = pl.program_id(0)
    if last:
        in_ref, turned_ref, early_ref, early_db_ref, ffn_db_ref, far_db_ref = refs[:6]
        one_ref, two_ref, dqkv_ref, small_ref, grad_ref, send_ref = refs[6:12]
    else:
        in_ref, first_ref, dqkv_ref, sum_ref, db_out_ref = refs[:5]

    @pl.when(j == 0)
    def _():
        dc_ref[...] = dg(da_ref[...], wo_ref[...], 1, 1).astype(BF)
        q_ref[...] = qkv_ref[0] * BF(HD**-0.5)
        tile = (q_ref, qkv_ref.at[1], qkv_ref.at[2])
        attn_back_tile(0, len_ref[s_ref[0]], tile, lse_ref, dc_ref, out_ref, dqkv_ref, db_ref)
        wide[...] = in_ref[...] if last else in_ref[...] + first_ref[...]
        for t in range(3):
            wide[...] += dg(out_ref[t], w_ref[t], 1, 1)
        if not last:
            sum_ref[...] = wide[...]
            db_out_ref[...] = db_ref[...]
            return
        grad_ref[...] = wide[...].astype(BF)
        side = s_ref[0]
        cols = far_db_ref.shape[1]
        depth = small_ref.shape[1]
        own = jnp.concatenate([early_db_ref[...], db_ref[...]], axis=1)
        small_ref[0:2, pl.ds(pl.multiple_of(side * cols, 128), cols)] = own
        small_ref[0:2, pl.ds(pl.multiple_of((1 - side) * cols, 128), cols)] = far_db_ref[...]
        lines = [ffn_db_ref[:, i * depth : (i + 1) * depth] for i in range(4)]
        small_ref[2:6] = jnp.where(
            side == 0,
            jnp.concatenate(lines, axis=0),
            jnp.concatenate(lines[2:] + lines[:2], axis=0),
        )
        small_ref[6:9] = one_ref[0:3]
        small_ref[9:12] = two_ref[0:3]
        small_ref[12:16] = jnp.zeros((4, depth), F32)

    if last:

        @pl.when(j > 0)
        def _():
            at = jnp.maximum(j - 1, 0)
            halves = [
                dg(turned_ref[...], ref[at], 0, 0).astype(BF) for ref in (early_ref, dqkv_ref)
            ]
            send_ref[0] = jnp.concatenate(halves, axis=1)


def attn_back_own(scalars, lengths, dattn, out_w, logsum, qkv, weight, *more, last):
    seq, depth = dattn.shape
    cols = out_w.shape[0]
    tile = cols // 2
    heads = tile // HD
    half = depth // 2
    at = int(last)
    full = whole(seq, depth)
    outs = [(shaped((3, seq, tile), BF), whole(3, seq, tile))]
    if last:
        turned = pl.BlockSpec(
            (seq, half), lambda j, s, n: (0, 1), pipeline_mode=pl.Buffered(1)
        )
        ins = [full, turned] + [whole(*arg.shape) for arg in more[2:]]
        outs += [
            (shaped((16, depth), F32), whole(16, depth)),
            (far_shaped((seq, depth), BF), full),
            (
                shaped((3, half, cols), BF),
                pl.BlockSpec((1, half, cols), lambda j, s, n: (jnp.maximum(j - 1, 0), 0, 0)),
            ),
        ]
    else:
        ins = [full, full]
        outs += [(shaped((seq, depth), F32), full), (shaped((2, tile), F32), whole(2, tile))]
    return call(
        functools.partial(attn_back_own_body, last=last),
        "attn_back_own",
        (4 if last else 1,),
        [
            full,
            pl.BlockSpec((tile, depth), lambda j, s, n: (at, 0), pipeline_mode=pl.Buffered(1)),
            pl.BlockSpec(
                (1, heads, seq), lambda j, s, n: (at, 0, 0), pipeline_mode=pl.Buffered(1)
            ),
            pl.BlockSpec(
                (3, seq, tile), lambda j, s, n: (0, 0, at), pipeline_mode=pl.Buffered(1)
            ),
            pl.BlockSpec(
                (3, depth, tile), lambda j, s, n: (0, 0, at), pipeline_mode=pl.Buffered(1)
            ),
        ]
        + ins,
        outs,
        (dattn, out_w, logsum, qkv, weight) + more,
        (scalars, lengths),
        [
            pltpu.VMEM((seq, depth), F32),
            pltpu.VMEM((2, tile), F32),
            pltpu.VMEM((seq, tile), BF),
            pltpu.VMEM((seq, tile), BF),
            pltpu.VMEM((3, seq, tile), BF),
        ],
        room=24,
    )


def grad_send_body(a_ref, b_ref, out_ref):
    out_ref[0] = dg(a_ref[...], b_ref[0], 0, 0).astype(BF)


def grad_specs(turned, right, picks, part):
    seq, units = right.shape[1:]
    half = turned.shape[1] // 2
    start, stride = picks[0], (picks[1] - picks[0] if len(picks) > 1 else 1)
    return [
        pl.BlockSpec((seq, half), lambda i: (0, part), pipeline_mode=pl.Buffered(1)),
        pl.BlockSpec((1, seq, units), lambda i: (start + stride * i, 0, 0)),
    ], pl.BlockSpec((1, half, units), lambda i: (i, 0, 0))


def grad_send(turned, right, picks):
    seq, units = right.shape[1:]
    half = turned.shape[1] // 2
    count = len(picks)
    ins, out = grad_specs(turned, right, picks, 1)
    return call(
        grad_send_body,
        "grad_send",
        (count,),
        ins,
        [(shaped((count, half, units), BF), out)],
        (turned, right),
        flops=2 * count * seq * half * units,
    )[0]


def keep_ffn_body(a_ref, b_ref, r_ref, keep_ref, send_ref, *, cut):
    value = (dg(a_ref[...], b_ref[0], 0, 0) + r_ref[0].astype(F32)).astype(BF)
    if cut:
        rows = keep_ref.shape[1]
        keep_ref[0] = value[:rows]
        send_ref[0] = value[rows:]
    else:

        @pl.when(pl.program_id(0) == 0)
        def _():
            send_ref[...] = value

        @pl.when(pl.program_id(0) == 1)
        def _():
            keep_ref[...] = value


def keep_ffn(turned, right, got, group):
    _, seq, units = right.shape
    half = turned.shape[1] // 2
    cut = group == 0

    def side(i):
        return i if cut else 1 - i

    if cut:
        spec = pl.BlockSpec((1, half // 2, units), lambda i: (i, 0, 0))
        outs = [
            (far_shaped((2, half // 2, units), BF), spec),
            (shaped((2, half // 2, units), BF), spec),
        ]
    else:
        outs = [
            (far_shaped((half, units), BF), whole(half, units)),
            (shaped((half, units), BF), whole(half, units)),
        ]
    return call(
        functools.partial(keep_ffn_body, cut=cut),
        "keep_ffn",
        (2,),
        [
            pl.BlockSpec((seq, half), lambda i: (0, 0), pipeline_mode=pl.Buffered(1)),
            pl.BlockSpec((1, seq, units), lambda i: (group + 2 * side(i), 0, 0)),
            pl.BlockSpec((1, half, units), lambda i: (side(i), 0, 0)),
        ],
        outs,
        (turned, right, got),
    )


def total(*refs):
    return sum(ref.astype(F32) for ref in refs).astype(BF)


def second_body(ka_ref, ga_ref, bo_ref, gb_ref, a_own_ref, a_far_ref, b_own_ref, b_send_ref):
    a_own_ref[...] = total(ka_ref[0], ga_ref[0])
    a_far_ref[...] = total(ka_ref[1], ga_ref[1])
    half = b_own_ref.shape[0]
    b_own_ref[...] = total(bo_ref[:half], gb_ref[:half])
    b_send_ref[...] = total(bo_ref[half:], gb_ref[half:])


def second(keep_a, got_a, b_own, got_b):
    _, rows, units = keep_a.shape
    part = (shaped((rows, units), BF), whole(rows, units))
    return call(
        second_body,
        "second",
        (1,),
        [whole(2, rows, units)] * 2 + [whole(2 * rows, units)] * 2,
        [part] * 4,
        (keep_a, got_a, b_own, got_b),
        stay=(0, 2),
    )


def third_body(a_ref, ga_ref, b_ref, gb_ref, keep_ref, send_ref):
    half, units = keep_ref.shape[0], a_ref.shape[1]
    for at, (left, right) in enumerate(((a_ref, ga_ref), (b_ref, gb_ref))):
        cut = slice(at * units, (at + 1) * units)
        keep_ref[:, cut] = total(left[:half], right[:half])
        send_ref[:, cut] = total(left[half:], right[half:])


def third(a_own, got_a, b_own, got_b):
    rows, units = a_own.shape
    part = (shaped((rows // 2, 2 * units), BF), whole(rows // 2, 2 * units))
    return call(
        third_body,
        "third",
        (1,),
        [whole(rows, units)] * 4,
        [part] * 2,
        (a_own, got_a, b_own, got_b),
    )


def fourth_body(a_ref, g_ref, keep_ref, send_ref):
    half = keep_ref.shape[-2]
    keep_ref[...] = total(a_ref[..., :half, :], g_ref[..., :half, :])
    send_ref[...] = total(a_ref[..., half:, :], g_ref[..., half:, :])


def fourth(values, got):
    shape = values.shape
    out = shape[:-2] + (shape[-2] // 2, shape[-1])
    return call(
        fourth_body,
        "fourth",
        (1,),
        [whole(*shape)] * 2,
        [(shaped(out, BF), whole(*out))] * 2,
        (values, got),
    )


def keep_far_body(
    da_ref, a_ref, own_ref, oth_ref, b_ref, ro_ref, rf_ref, keep_ref, send_ref, far_ref
):
    i = pl.program_id(0)
    cut = keep_ref.shape[1]

    def split(value):
        keep_ref[0] = value[:cut]
        send_ref[0] = value[cut:]

    for side, ref in enumerate((own_ref, oth_ref)):

        @pl.when(i == side)
        def _():
            split((dg(da_ref[...], ref[...], 0, 0) + ro_ref[0].astype(F32)).astype(BF))

    @pl.when(i >= 2)
    def _():
        value = (dg(a_ref[...], b_ref[0], 0, 0) + rf_ref[0].astype(F32)).astype(BF)

        @pl.when(i == 2)
        def _():
            split(value)

        @pl.when(i > 2)
        def _():
            far_ref[0] = value


def keep_far(da_turned, turned, own, other, dqkv, got_out, got_far):
    _, seq, cols = dqkv.shape
    half = turned.shape[1] // 2
    left = pl.BlockSpec((seq, half), lambda i: (0, 0), pipeline_mode=pl.Buffered(1))
    cut = pl.BlockSpec((1, half // 2, cols), lambda i: (jnp.minimum(i, 2), 0, 0))
    return call(
        keep_far_body,
        "keep_far",
        (5,),
        [
            left,
            left,
            whole(seq, cols),
            whole(seq, cols),
            pl.BlockSpec((1, seq, cols), lambda i: (jnp.maximum(i - 2, 0), 0, 0)),
            pl.BlockSpec((1, half, cols), lambda i: (jnp.minimum(i, 1), 0, 0)),
            pl.BlockSpec((1, half, cols), lambda i: (jnp.maximum(i - 2, 0), 0, 0)),
        ],
        [
            (shaped((3, half // 2, cols), BF), cut),
            (shaped((3, half // 2, cols), BF), cut),
            (
                shaped((2, half, cols), BF),
                pl.BlockSpec((1, half, cols), lambda i: (jnp.maximum(i - 3, 0), 0, 0)),
            ),
        ],
        (da_turned, turned, own, other, dqkv, got_out, got_far),
    )


def second_attn_body(k_ref, g_ref, out_ref, far_ref):
    out_ref[0] = total(k_ref[0], g_ref[0])
    far_ref[0] = total(k_ref[2], g_ref[2])
    far_ref[1] = total(k_ref[1], g_ref[1])


def second_attn(keep, got):
    _, rows, cols = keep.shape
    return call(
        second_attn_body,
        "second_attn",
        (1,),
        [whole(3, rows, cols)] * 2,
        [(shaped((n, rows, cols), BF), whole(n, rows, cols)) for n in (1, 2)],
        (keep, got),
    )


def keep_own_body(
    a_ref, b0_ref, b1_ref, r_ref, gb_ref, keep_ref, send_ref, z_keep_ref, z_send_ref
):
    i = pl.program_id(0)
    parts = [dg(a_ref[...], ref[0], 0, 0) for ref in (b0_ref, b1_ref)]
    value = jnp.concatenate(parts, axis=1) + r_ref[0].astype(F32)
    value = jnp.where(i == 0, value, value + gb_ref[0].astype(F32)).astype(BF)
    cut = keep_ref.shape[1]

    @pl.when(i < 2)
    def _():
        keep_ref[0] = value[:cut]
        send_ref[0] = value[cut:]

    @pl.when(i == 2)
    def _():
        half = cut // 2
        for x in range(2):
            z_keep_ref[x * half : (x + 1) * half] = value[x * cut : x * cut + half]
            z_send_ref[x * half : (x + 1) * half] = value[x * cut + half : (x + 1) * cut]


def keep_own(turned, early, late, got, got_b):
    _, seq, tile = early.shape
    cols = 2 * tile
    half = turned.shape[1] // 2
    part = (
        shaped((2, half // 2, cols), BF),
        pl.BlockSpec((1, half // 2, cols), lambda i: (jnp.minimum(i, 1), 0, 0)),
    )
    flat = (shaped((half // 2, cols), BF), whole(half // 2, cols))
    return call(
        keep_own_body,
        "keep_own",
        (3,),
        [
            pl.BlockSpec((seq, half), lambda i: (0, 0), pipeline_mode=pl.Buffered(1)),
            pl.BlockSpec((1, seq, tile), lambda i: (i, 0, 0)),
            pl.BlockSpec((1, seq, tile), lambda i: (i, 0, 0)),
            pl.BlockSpec((1, half, cols), lambda i: (i, 0, 0)),
            pl.BlockSpec((1, half, cols), lambda i: (jnp.maximum(i - 1, 0), 0, 0)),
        ],
        [part, part, flat, flat],
        (turned, early, late, got, got_b),
    )


def join_attn_body(
    k_ref, x_ref, o_ref, y_ref, v_ref, z_ref, keep_ref, send_ref, v_keep_ref, v_send_ref
):
    half = keep_ref.shape[1]
    for ref, cut in ((keep_ref, slice(0, half)), (send_ref, slice(half, 2 * half))):
        ref[0] = total(k_ref[0, cut], x_ref[0, cut], y_ref[0, cut])
        ref[1] = total(k_ref[1, cut], x_ref[1, cut])
        ref[2] = total(o_ref[0, cut], y_ref[1, cut])
    v_keep_ref[...] = total(v_ref[:half], z_ref[:half])
    v_send_ref[...] = total(v_ref[half:], z_ref[half:])


def join_attn(keep, got_x, out, got_y, value, got_z):
    _, rows, cols = keep.shape
    part = (shaped((3, rows // 2, cols), BF), whole(3, rows // 2, cols))
    flat = (shaped((rows // 2, cols), BF), whole(rows // 2, cols))
    return call(
        join_attn_body,
        "join_attn",
        (1,),
        [
            whole(2, rows, cols),
            whole(2, rows, cols),
            whole(1, rows, cols),
            whole(2, rows, cols),
            whole(rows, cols),
            whole(rows, cols),
        ],
        [part, part, flat, flat],
        (keep, got_x, out, got_y, value, got_z),
    )


def last_attn_body(k_ref, z_ref, v_ref, x_ref, keep_ref, send_ref):
    half = keep_ref.shape[1]
    for ref, cut in ((keep_ref, slice(0, half)), (send_ref, slice(half, 2 * half))):
        for i in range(3):
            ref[i] = total(k_ref[i, cut], z_ref[i, cut])
        ref[3] = total(v_ref[cut], x_ref[cut])


def last_attn(keep, got_z, value, got_x):
    _, rows, cols = keep.shape
    part = (shaped((4, rows // 2, cols), BF), whole(4, rows // 2, cols))
    return call(
        last_attn_body,
        "last_attn",
        (1,),
        [whole(3, rows, cols), whole(3, rows, cols), whole(rows, cols), whole(rows, cols)],
        [part, part],
        (keep, got_z, value, got_x),
    )


def share_attn_body(k_ref, g_ref, qkv_ref, out_ref):
    for at, i in ((0, 0), (1, 1), (2, 3)):
        qkv_ref[at] = k_ref[i].astype(F32) + g_ref[i].astype(F32)
    out_ref[...] = k_ref[2].astype(F32) + g_ref[2].astype(F32)


def share_attn(keep, got):
    _, rows, cols = keep.shape
    return call(
        share_attn_body,
        "share_attn",
        (1,),
        [whole(4, rows, cols)] * 2,
        [
            (far_shaped((3, rows, cols), F32), whole(3, rows, cols)),
            (far_shaped((rows, cols), F32), whole(rows, cols)),
        ],
        (keep, got),
    )


def swap(values, bit):
    count = lax.axis_size("dp")
    return lax.ppermute(values, "dp", [(i, i ^ (1 << bit)) for i in range(count)])


def swap_y(values):
    return lax.ppermute(values, "mp", [(0, 1), (1, 0)])


def add(left, right):
    return left.astype(F32) + right.astype(F32)


def low_add(left, right):
    return add(left, right).astype(BF)


def after(value, tick):
    flat, tree = jax.tree.flatten(value)
    arrays = [i for i, leaf in enumerate(flat) if not isinstance(leaf, int)]
    held = lax.optimization_barrier(([flat[i] for i in arrays], tick))[0]
    for i, leaf in zip(arrays, held):
        flat[i] = leaf
    return jax.tree.unflatten(tree, flat)


def paged(
    tokens,
    page_lengths,
    qkv_weight,
    qv_bias,
    out_weight,
    out_bias,
    ln1_gain,
    ln1_bias,
    ff1_weight,
    ff1_bias,
    ff2_weight,
    ff2_bias,
    ln2_gain,
    ln2_bias,
    cotangent,
):
    row_count, depth = tokens.shape
    seq = row_count // 2
    cols = qkv_weight.shape[2]
    units = ff1_weight.shape[1] // 2
    group = lax.axis_index("mp")
    me = lax.axis_index("dp")

    ready = (
        jnp.stack([group, me]).astype(jnp.int32),
        1 - group,
        group,
    )
    scalars, far_page, own_page = lax.optimization_barrier(ready)

    def outer(mine, bits):
        return [mine] + [swap(mine, bit) for bit in bits]

    def rels(bits):
        one, two = (1 << bit for bit in bits)
        return (0, one, two, one | two)

    ways = ((1, 2), (2, 1), (1, 2))

    block0, out_block = pick(scalars, ff1_weight, ff2_weight, out_weight, 0)
    out_mine, mine0 = swap_y(out_block), swap_y(block0)
    far_ctx, far_lse = attn_fwd(
        far_page, page_lengths, after(tokens, block0), qkv_weight, qv_bias, False, (0, 2)
    )
    oth_ctx, oth_lse = swap_y(far_ctx), swap_y(far_lse)
    own = attn_fwd(
        own_page, page_lengths, after(tokens, far_ctx), qkv_weight, qv_bias, True, (0, 1)
    )
    out_mine = after(out_mine, own[0])
    out_x = swap(out_mine, 1)
    own_ctx, own_lse, own_qkv = attn_fwd(
        own_page, page_lengths, after(tokens, out_mine), qkv_weight, qv_bias, True, (1, 2), own
    )
    mine0 = after(mine0, own_ctx)
    by_x, by_z = swap(mine0, 1), swap(mine0, 2)
    out_near = collect([out_mine, after(out_x, mine0)])
    out_core = swap(out_near, 0)
    bias_row = after(ff1_bias, own[0]).reshape(1, -1)
    block1, qkv_block = pick(
        after(scalars, out_near), ff1_weight, ff2_weight, qkv_weight, 1, (bias_row, qv_bias)
    )
    mine1 = swap_y(block1)
    rows = [v.reshape(1, -1) for v in after((out_bias, ln1_gain, ln1_bias), out_near)]
    out_bias, ln1_gain, ln1_bias = rows
    own_ctx, by_x, by_z = lax.optimization_barrier((own_ctx, by_x, by_z))
    out_far, normed_one, scale_one, hidden, hidden_turned = join(
        scalars,
        tokens,
        own_ctx,
        after(oth_ctx, (block1, oth_lse)),
        out_weight,
        out_near,
        out_core,
        out_bias,
        ln1_gain,
        ln1_bias,
    )
    stage0 = [mine0, by_x, by_z]
    last0 = swap(by_z, 1)
    act, slope, partial = ffn_own(hidden, ff1_weight, bias_row, ff2_weight, 0, ())
    mine1, last0 = after((mine1, last0), partial)
    far_biases = mine1
    stage1 = outer(mine1, ways[1])
    act, slope, partial = ffn_own(
        hidden, ff1_weight, bias_row, ff2_weight, 1, (after(partial, mine1), act, slope)
    )
    qkv_mine = swap_y(after(qkv_block, mine1))
    stage1 = after(stage1, partial)
    rows = [v.reshape(1, -1) for v in after((ff2_bias, ln2_gain, ln2_bias), partial)]
    ff2_bias, ln2_gain, ln2_bias = rows
    last1 = swap(stage1[2], ways[1][0])
    near0 = collect(after(stage0 + [last0], stage1[2]))
    core0 = swap(near0, 0)
    act, slope, partial, w1_far, w2_far = ffn_far(
        scalars,
        hidden,
        far_biases,
        near0,
        core0,
        rels(ways[0]),
        0,
        (after(partial, rows), act, slope),
    )
    last1, qkv_mine = after((last1, qkv_mine), partial)
    near1 = collect(stage1 + [last1])
    core1 = swap(near1, 0)
    qkv_stage = outer(after(qkv_mine, near1), ways[2])
    act, slope, partial, w1_far, w2_far = ffn_far(
        scalars,
        hidden,
        far_biases,
        near1,
        core1,
        rels(ways[1]),
        1,
        (partial, act, slope, w1_far, w2_far),
    )
    out_rows, dsecond, dffn, dffn_turned, sums_two = norm_two(
        scalars,
        partial,
        normed_one,
        cotangent,
        (ln1_gain, ln1_bias, ff2_bias, ln2_gain, ln2_bias),
    )

    qkv_stage = after(qkv_stage, dffn)
    last = swap(qkv_stage[2], ways[2][0])
    send_b = grad_send(after(dffn_turned, qkv_stage[0]), act, (1, 3))
    send_a = grad_send(after(dffn_turned, send_b), act, (0, 2))
    got_a, got_b = swap(send_a, 0), swap(send_b, 0)
    b_own, b_far = keep_ffn(after(dffn_turned, send_a), act, got_b, 1)
    keep_a, send_a = keep_ffn(after(dffn_turned, b_own), act, got_a, 0)
    ff2_x, ff2_y = swap(send_a, 1), swap_y(b_far)
    last = after(last, keep_a)
    dpre, db, dfirst, dattn, dattn_turned, sums_one, send_a, send_b, qkv_near = ffn_back(
        scalars,
        after(dffn, last),
        ff2_weight,
        w2_far,
        slope,
        ff1_weight,
        w1_far,
        dsecond,
        normed_one,
        scale_one,
        ln1_gain,
        hidden_turned,
        qkv_stage + [last],
    )
    got_a, got_b = swap(send_a, 0), swap(send_b, 0)
    qkv_core = swap(qkv_near, 0)
    ff2_own, ff2_far, ff2_keep, ff2_send = second(after(keep_a, dattn), ff2_x, b_own, ff2_y)
    ff2_y, ff2_x = swap_y(ff2_far), swap(ff2_send, 1)
    b_own, b_far = keep_ffn(after(hidden_turned, ff2_own), dpre, got_b, 1)
    keep_a, send_a = keep_ffn(after(hidden_turned, b_own), dpre, got_a, 0)
    ff1_x, ff1_y = swap(send_a, 1), swap_y(b_far)
    dqkv_far, dqv_far, dtok, tok_turned, far_send, out_send = attn_back_other(
        scalars,
        page_lengths,
        tokens,
        after(dattn, keep_a),
        out_far,
        oth_lse,
        far_biases,
        qkv_near,
        qkv_core,
        rels(ways[2]),
        own_ctx,
        oth_ctx,
        dattn_turned,
    )
    out_got, far_got = swap(out_send, 0), swap(far_send, 0)
    ff2_keep, ff2_send = third(after(ff2_own, dtok), ff2_y, ff2_keep, ff2_x)
    ff2_z = swap(ff2_send, 2)
    ff1_own, ff1_far, ff1_keep, ff1_send = second(after(keep_a, ff2_keep), ff1_x, b_own, ff1_y)
    ff1_y, ff1_x = swap_y(ff1_far), swap(ff1_send, 1)
    far_keep, far_send, b_far = keep_far(
        after(dattn_turned, ff1_own), tok_turned, own_ctx, oth_ctx, dqkv_far, out_got, far_got
    )
    far_x, far_y = swap(far_send, 1), swap_y(b_far)
    early, dtok, early_db = attn_back_own(
        scalars,
        page_lengths,
        after(dattn, far_keep),
        out_weight,
        own_lse,
        own_qkv,
        qkv_weight,
        dtok,
        dfirst,
        last=False,
    )
    ff1_keep, ff1_send = third(after(ff1_own, dtok), ff1_y, ff1_keep, ff1_x)
    ff1_z = swap(ff1_send, 2)
    ff2_keep, ff2_send = fourth(after(ff2_keep, ff1_keep), ff2_z)
    ff2_z = swap(ff2_send, 3)
    late, small, input_grad, own_send = attn_back_own(
        scalars,
        page_lengths,
        after(dattn, ff2_keep),
        out_weight,
        own_lse,
        own_qkv,
        qkv_weight,
        dtok,
        tok_turned,
        early,
        early_db,
        db,
        dqv_far,
        sums_one,
        sums_two,
        last=True,
    )
    own_got = swap(own_send, 0)
    other = swap(small, 0)
    ff1_keep, ff1_send = fourth(after(ff1_keep, own_send), ff1_z)
    ff1_z = swap(ff1_send, 3)
    small = small + after(other, ff1_keep)
    far_keep, far_x, far_y = after((far_keep, far_x, far_y), ff1_keep)
    far_keep, ff2_z, small = lax.optimization_barrier((far_keep, ff2_z, small))
    other = swap_y(small)
    out_keep, far_send = second_attn(far_keep, far_x)
    got_y = swap_y(far_send)
    keep, send, z_keep, z_send = keep_own(
        after(tok_turned, out_keep), early, late, own_got, far_y
    )
    got_x, got_z = swap(send, 1), swap(z_send, 2)
    small = small + after(other, keep)
    small = small + swap(small, 1)
    keep, ff1_z = lax.optimization_barrier((keep, ff1_z))
    keep, send, v_keep, v_send = join_attn(
        after(keep, small), got_x, out_keep, got_y, z_keep, got_z
    )
    got_z, got_x = swap(send, 2), swap(v_send, 1)
    ff2_share = add(*after((ff2_keep, ff2_z), keep))
    other = swap(after(small, keep), 2)
    keep, send = last_attn(after(keep, ff2_share), got_z, v_keep, got_x)
    got = swap(send, 3)
    small = small + after(other, keep)
    other = swap(small, 3)
    ff1_share = add(*after((ff1_keep, ff1_z), keep))
    small = (small + after(other, ff1_share)).reshape(-1)
    ends = []
    at = 0
    for length in (4 * cols, 4 * units, depth, depth, depth, depth, depth, depth):
        ends.append(small[at : at + length])
        at += length
    ends[0] = ends[0].reshape(2, -1)
    keep, ends, ff1_share = lax.optimization_barrier((keep, ends, ff1_share))
    qkv_share, out_share = share_attn(keep, got)
    return (
        out_rows,
        input_grad,
        qkv_share,
        ends[0],
        out_share.T,
        ends[2],
        ends[3],
        ends[4],
        ff1_share,
        ends[1],
        ff2_share.T,
        ends[5],
        ends[6],
        ends[7],
    )


def suits(mesh):
    return mesh.shape["mp"] == 2 and mesh.shape["dp"] == 16


def solution(mesh):
    in_specs = (
        P("dp", None),
        P("dp"),
        P(None, None, "mp"),
        P(None, "mp"),
        P("mp", None),
        P(),
        P(),
        P(),
        P(None, "mp"),
        P("mp"),
        P("mp", None),
        P(),
        P(),
        P(),
        P("dp", None),
    )
    out_specs = (
        P(("dp", "mp"), None),
        P(("dp", "mp"), None),
        P(None, "dp", "mp"),
        P(),
        P("mp", "dp"),
        P(),
        P(),
        P(),
        P("dp", "mp"),
        P(),
        P("mp", "dp"),
        P(),
        P(),
        P(),
    )
    body = paged if suits(mesh) else local
    return jax.shard_map(body, mesh=mesh, in_specs=in_specs, out_specs=out_specs, check_vma=False)
```
